256 devices in a mesh: vx: 16 (over y, x), vy: 8 (over z), subj: 2 (over core).
Axes of the slice: x: 4, y: 4, z: 8, core: 2. Of those that a mesh axis runs over, the one named last changes fastest.
Arguments:
- volumes: bfloat16 [8, 64, 32, 64, 128], P('subj', None, 'vx', 'vy'), may hold values from -24 to 24
- flip_bits: int32 [32, 64, 128], P('vx', 'vy'), may hold values from 0 to 1
- hadamard_block: int32 [4096], replicated, may hold values from 0 to 127
- stratum_offset: int32 [4096], replicated, may hold values from 0 to 15
- subject_order: int32 [8], replicated, may hold values from 0 to 7, each once
Outputs:
- sketch: float32 [4096, 512], P(('vx', 'vy'), 'subj')
- gram: float32 [512, 512], P('subj')
The draws below stay inside these ranges and needn't reach their ends.
Inputs may be any that keep to these rules, and one draw needn't show every extreme that they name: `subject_order`: each of 0 to 7 appears once.
All inputs are finite; a program needn't handle non-finite values.
Results may differ from the reference program's by a relative error of at most 0.0003.
Values may be sent and summed in bfloat16 or wider, within the bound.
A program may use at most 64 MiB of HBM per device.

```python
import math
import jax
import jax.numpy as jnp
from jax import lax

CX = 2
CY = 8
NZ = 128
TR = 64
KD = 32
X = 32
Y = 64
BLOCKS = 128
STRATUM = 16
K = 4096
SUBJECTS = 8
N_VX = 16
N_VY = 8


def place_ends(entries, key, least, high):
    dims = entries.shape
    place = [jax.random.randint(jax.random.fold_in(key, axis), (), 0, dims[axis]) for axis in range(len(dims))]
    entries = entries.at[tuple(place)].set(least)
    longest = dims.index(max(dims))
    place[longest] = (place[longest] + 1) % dims[longest]
    return entries.at[tuple(place)].set(high)


def steps_of(stream_key, extent, split, smallest, top_value):
    gain, own = 1.0, jax.random.fold_in(stream_key, 6)
    for axis_at, blocks in split:
        draws = jnp.exp(jax.random.uniform(jax.random.fold_in(own, axis_at), (blocks,), jnp.float32, smallest / len(split), top_value / len(split)))
        gain = gain * jnp.repeat(draws, extent[axis_at] // blocks).reshape([-1 if axis == axis_at else 1 for axis in range(len(extent))])
    return gain


def gaussian(stream_key, shape, deviation, reach, pieces=(), kind=jnp.bfloat16):
    factor_of = steps_of(stream_key, shape, pieces, -0.22, 0.18) if pieces else 1.0
    values = jax.random.normal(stream_key, shape, jnp.float32) * deviation * factor_of
    return jnp.minimum(jnp.maximum(values, -reach), reach).astype(kind)


def setup_inputs(seed: int = 0) -> dict:
    splits = jax.random.split(jax.random.key(seed), 6)
    return {
        "volumes": gaussian(splits[0], (SUBJECTS, TR, X, Y, NZ), 4.0, 24.0, ((0, 2), (2, 16), (3, 8))),
        "flip_bits": place_ends(jax.random.randint(splits[1], (X, Y, NZ), 0, 2), jax.random.fold_in(splits[1], 1), 0, 1).astype(jnp.int32),
        "hadamard_block": place_ends(jax.random.randint(splits[2], (K,), 0, BLOCKS), jax.random.fold_in(splits[2], 1), 0, BLOCKS - 1).astype(jnp.int32),
        "stratum_offset": place_ends(jax.random.randint(splits[3], (K,), 0, STRATUM), jax.random.fold_in(splits[3], 1), 0, STRATUM - 1).astype(jnp.int32),
        "subject_order": jax.random.permutation(splits[4], SUBJECTS).astype(jnp.int32),
    }


w_side = 0.2741
w_mid = 0.4518

def hadamard_sign(first, second, nbits):
    parity = jnp.zeros_like(first + second, dtype=jnp.int32)
    for level in range(nbits):
        parity = parity + first // (1 << level) % 2 * (second // (1 << level) % 2)
    return (1 - 2 * (parity % 2)).astype(jnp.float32)

def hadamard_table(order):
    index = jnp.arange(order, dtype=jnp.int32)
    return hadamard_sign(index[:, None], index[None, :], order.bit_length() - 1)

def smooth_axis(padded, axis):
    length = padded.shape[axis]
    lower = lax.slice_in_dim(padded, 0, length - 2, axis=axis)
    centre = lax.slice_in_dim(padded, 1, length - 1, axis=axis)
    upper = lax.slice_in_dim(padded, 2, length, axis=axis)
    return w_side * (lower + upper) + w_mid * centre

def reference(volumes, flip_bits, hadamard_block, stratum_offset, subject_order):
    highest_level = lax.Precision.HIGHEST
    blocks = N_VX * N_VY
    local_rows = CX * CY * NZ
    stratum = local_rows // blocks
    total_rows = KD * blocks
    scale = 1.0 / math.sqrt(local_rows * blocks)
    signs = (2 * flip_bits - 1).astype(jnp.float32)
    first_table = hadamard_table(CX * CY)
    second_table = hadamard_table(NZ)
    rows = jnp.arange(total_rows, dtype=jnp.int32)
    picked_rows = (rows // KD * stratum + stratum_offset).astype(jnp.int32)
    block_signs = hadamard_sign(hadamard_block[:, None], jnp.arange(blocks, dtype=jnp.int32)[None, :], blocks.bit_length() - 1)

    def one_subject(volume):
        field = volume.astype(jnp.float32)
        padded = jnp.pad(field, ((0, 0), (1, 1), (1, 1), (1, 1)))
        smoothed = smooth_axis(smooth_axis(smooth_axis(padded, 1), 2), 3)
        flipped_signs = smoothed * signs[None]
        shaped = flipped_signs.reshape(TR, N_VX, CX, N_VY, CY, NZ).transpose(0, 1, 3, 2, 4, 5).reshape(TR, blocks, CX * CY, NZ)
        half_span = jnp.einsum('pa,tdab->tdpb', first_table, shaped, precision=highest_level)
        mixed_rows = jnp.einsum('tdpb,qb->tdpq', half_span, second_table, precision=highest_level).reshape(TR, blocks, local_rows)
        chosen = jnp.take(mixed_rows, picked_rows, axis=2)
        return jnp.einsum('tdr,rd->rt', chosen, block_signs, precision=highest_level) * scale
    sketches = lax.map(one_subject, volumes)
    sketch = sketches.transpose(1, 0, 2).reshape(total_rows, SUBJECTS * TR)
    columns = jnp.arange(SUBJECTS * TR, dtype=jnp.int32)
    subject_of = columns // TR
    position = lax.optimization_barrier(jnp.sum(jnp.where(subject_of[:, None] == jnp.arange(SUBJECTS, dtype=jnp.int32)[None, :], subject_order[None, :], 0), axis=1))
    target = position * TR + columns % TR
    mover = (target[:, None] == columns[None, :]).astype(jnp.float32)
    ordered = jnp.dot(sketch, mover, precision=highest_level)
    gram = jnp.dot(ordered.T, ordered, precision=highest_level) / total_rows
    return (sketch, gram)
```

```python
import functools
import math

import jax
import jax.numpy as jnp
from jax import lax
from jax.experimental import pallas as pl
from jax.experimental.pallas import tpu as pltpu
from jax.sharding import PartitionSpec as P

MESH = pl.DeviceIdType.MESH
F32, BF16, I32 = jnp.float32, jnp.bfloat16, jnp.int32

w_side = 0.2741
w_mid = 0.4518

RX, RY, RZ = 4, 4, 8
PLANE = RX * RY
KD = 32
COLS = 256
HALF = 128
EX, EY = 4, 10
PLANES = EX * EY
STRATUM = 16


def split2(v):
    hi = v.astype(BF16)
    return hi, (v - hi.astype(F32)).astype(BF16)


def halo_kernel(flip_ref, ext_ref, buf, send_sem, recv_sem):
    vx, vy, sj = lax.axis_index("vx"), lax.axis_index("vy"), lax.axis_index("subj")
    offs = [(dx, dy) for dx in (-1, 0, 1) for dy in (-1, 0, 1) if (dx, dy) != (0, 0)]

    def dev(dx, dy):
        return (lax.rem(vx + dx + 16, 16), lax.rem(vy + dy + 8, 8), sj)

    barrier = pltpu.get_barrier_semaphore()
    for dx, dy in offs:
        pl.semaphore_signal(barrier, inc=1, device_id=dev(dx, dy), device_id_type=MESH)
    pl.semaphore_wait(barrier, len(offs))
    copies = []
    for i, (dx, dy) in enumerate(offs):
        copies.append(
            pltpu.make_async_remote_copy(
                src_ref=flip_ref,
                dst_ref=buf.at[i],
                send_sem=send_sem.at[i],
                recv_sem=recv_sem.at[i],
                device_id=dev(dx, dy),
                device_id_type=MESH,
            )
        )
    for c in copies:
        c.start()
    lo_x = jnp.where(vx > 0, 1, 0)
    hi_x = jnp.where(vx < 15, 1, 0)
    lo_y = jnp.where(vy > 0, 1, 0)
    hi_y = jnp.where(vy < 7, 1, 0)
    okx = {-1: lo_x, 0: 1, 1: hi_x}
    oky = {-1: lo_y, 0: 1, 1: hi_y}
    for x in range(2):
        for y in range(8):
            ext_ref[x + 1, y + 1] = (2 * flip_ref[x, pl.ds(y, 1), :] - 1).astype(F32)
    for c in copies:
        c.wait()
    for i, (dx, dy) in enumerate(offs):
        sx, sy = -dx, -dy
        ok = (okx[sx] * oky[sy]).astype(F32)
        xs = {-1: [(0, 1)], 0: [(1, 0), (2, 1)], 1: [(3, 0)]}[sx]
        ys = {-1: [(0, 7)], 0: [(k + 1, k) for k in range(8)], 1: [(9, 0)]}[sy]
        for ex, bx in xs:
            for ey, by in ys:
                ext_ref[ex, ey] = (2 * buf[i, bx, pl.ds(by, 1), :] - 1).astype(F32) * ok


def sign_halo(flip_bits):
    return pl.pallas_call(
        halo_kernel,
        out_shape=jax.ShapeDtypeStruct((EX, EY, 1, 128), F32),
        in_specs=[pl.BlockSpec(memory_space=pltpu.VMEM)],
        out_specs=pl.BlockSpec(memory_space=pltpu.VMEM),
        scratch_shapes=[
            pltpu.VMEM((8, 2, 8, 128), I32),
            pltpu.SemaphoreType.DMA((8,)),
            pltpu.SemaphoreType.DMA((8,)),
        ],
        compiler_params=pltpu.CompilerParams(collective_id=0, has_side_effects=True),
        name="sign_halo",
    )(flip_bits)


def local_kernel(vol_ref, ext_ref, rc_ref, so_ref, c_ref, zs, xs, tt_hi, tt_lo):
    vx, vy = lax.axis_index("vx"), lax.axis_index("vy")
    row = lax.broadcasted_iota(I32, (128, 128), 0)
    col = lax.broadcasted_iota(I32, (128, 128), 1)
    dist = jnp.abs(row - col)
    band = jnp.where(dist == 0, w_mid, jnp.where(dist == 1, w_side, 0.0)).astype(F32)
    wcat = jnp.concatenate(split2(band), axis=1)

    def smooth_z(i, _):
        v = vol_ref[pl.ds(i * 32, 32)].astype(F32).reshape(256, 128).astype(BF16)
        r = jnp.dot(v, wcat, preferred_element_type=F32)
        zs[pl.ds(i * 256, 256), :] = r[:, :128] + r[:, 128:]
        return 0

    lax.fori_loop(0, 16, smooth_z, 0)

    zero = jnp.zeros((COLS, 128), F32)
    for ex in range(EX):
        for y in (0, 1, 10, 11):
            xs[ex, y] = zero

    for y in range(8):
        a = zs[pl.ds(y, COLS, stride=16), :]
        b = zs[pl.ds(8 + y, COLS, stride=16), :]
        xs[0, y + 2] = w_side * a
        xs[1, y + 2] = w_mid * a + w_side * b
        xs[2, y + 2] = w_side * a + w_mid * b
        xs[3, y + 2] = w_side * b

    bits = row & col
    for s in (4, 2, 1):
        bits = bits ^ (bits >> s)
    hz = (1 - 2 * (bits & 1)).astype(F32).astype(BF16)
    hcat = jnp.concatenate([hz, hz], axis=1)

    def planes(yi, _):
        for ex in range(EX):
            f = w_side * (xs[ex, yi] + xs[ex, yi + 2]) + w_mid * xs[ex, yi + 1]
            f = f * ext_ref[ex, yi]
            fcat = jnp.concatenate(split2(f), axis=1)
            t = lax.dot_general(hcat, fcat, (((1,), (1,)), ((), ())), preferred_element_type=F32)
            thi, tlo = split2(t)
            at = pl.ds(pl.multiple_of((ex * EY + yi) * STRATUM, STRATUM), STRATUM)
            for g in range(RZ):
                tt_hi[g, at, :] = thi[g * STRATUM : (g + 1) * STRATUM, :]
                tt_lo[g, at, :] = tlo[g * STRATUM : (g + 1) * STRATUM, :]
        return 0

    lax.fori_loop(0, EY, planes, 0)

    lane = lax.broadcasted_iota(I32, (1, 128), 1)
    gx = vx * 2 + lane // EY - 1 + 32
    gy = vy * 8 + lane % EY - 1 + 64
    voxel = (((gx >> 1) & 15) * 8 + ((gy >> 3) & 7)) * 16 + (gx & 1) * 8 + (gy & 7)
    off_lane = lane & 15
    ej = lax.broadcasted_iota(I32, (128, PLANES * STRATUM), 0)
    ek = lax.broadcasted_iota(I32, (128, PLANES * STRATUM), 1)
    spread = jnp.where((ek >> 4) == ej, 1.0, 0.0).astype(BF16)
    scale = 1.0 / 512.0

    for g in range(RZ):
        bits = rc_ref[:, g : g + 1] & voxel
        for s in (8, 4, 2, 1):
            bits = bits ^ (bits >> s)
        sgn = (1 - 2 * (bits & 1)).astype(F32).astype(BF16)
        wide = jnp.dot(sgn, spread, preferred_element_type=F32)
        pick = so_ref[:, g : g + 1] == off_lane
        parts = [
            jnp.where(pick, wide[:, k * 128 : (k + 1) * 128], 0.0).astype(BF16)
            for k in range(PLANES * STRATUM // 128)
        ]
        s_mat = jnp.concatenate(parts, axis=1)
        c = jnp.dot(s_mat, tt_hi[g], preferred_element_type=F32)
        c = c + jnp.dot(s_mat, tt_lo[g], preferred_element_type=F32)
        c_ref[g] = (c * scale).reshape(RY, RX, KD, COLS)


def contributions(vol, ext, rc, so):
    return pl.pallas_call(
        local_kernel,
        out_shape=jax.ShapeDtypeStruct((RZ, RY, RX, KD, COLS), F32),
        in_specs=[pl.BlockSpec(memory_space=pltpu.VMEM)] * 4,
        out_specs=pl.BlockSpec(memory_space=pltpu.VMEM),
        scratch_shapes=[
            pltpu.VMEM((COLS * 16, 128), F32),
            pltpu.VMEM((EX, EY + 2, COLS, 128), F32),
            pltpu.VMEM((RZ, PLANES * STRATUM, COLS), BF16),
            pltpu.VMEM((RZ, PLANES * STRATUM, COLS), BF16),
        ],
        compiler_params=pltpu.CompilerParams(vmem_limit_bytes=60 * 1024 * 1024),
        name="contributions",
    )(vol, ext, rc, so)


def comm_kernel(
    order_ref, c_ref, sk_ref, gram_ref,
    c, ra1, ra2, rb1, rb2, rz, other, gs, r1, p1, r2, p3, out,
    ld_sem, a_send, a_recv, z_send, z_recv, g_send, g_recv,
):
    vx, vy, sj = lax.axis_index("vx"), lax.axis_index("vy"), lax.axis_index("subj")
    x, y = lax.rem(vx, RX), lax.div(vx, RX)

    def xy(dx, dy):
        return (lax.rem(y + dy + RY, RY) * RX + lax.rem(x + dx + RX, RX), vy, sj)

    def plane_dev(o):
        return (lax.rem(vx + o, PLANE), vy, sj)

    def z_dev(o):
        return (vx, lax.rem(vy + o, RZ), sj)

    partner = (vx, vy, 1 - sj)
    barrier = pltpu.get_barrier_semaphore()
    peers = [plane_dev(o) for o in range(1, PLANE)] + [z_dev(o) for o in range(1, RZ)] + [partner]
    for d in peers:
        pl.semaphore_signal(barrier, inc=1, device_id=d, device_id_type=MESH)

    load = pltpu.make_async_copy(c_ref, c, ld_sem)
    load.start()

    lanes = lax.broadcasted_iota(I32, (64, 512), 1)
    rows = lax.broadcasted_iota(I32, (64, 512), 0)
    mover = jnp.concatenate(
        [jnp.where(lanes == order_ref[s] * 64 + rows, 1.0, 0.0).astype(BF16) for s in range(8)], axis=0
    )
    load.wait()
    pl.semaphore_wait(barrier, len(peers))

    def remote(src, dst, ssem, rsem, dev):
        return pltpu.make_async_remote_copy(
            src_ref=src, dst_ref=dst, send_sem=ssem, recv_sem=rsem, device_id=dev, device_id_type=MESH
        )

    started = []

    def go(copy):
        copy.start()
        started.append(copy)
        return copy

    lanes_of = [pl.ds(0, HALF), pl.ds(HALF, HALF)]
    x1, x2, x3 = lax.rem(x + 1, RX), lax.rem(x + 2, RX), lax.rem(x + 3, RX)
    y1, y2, y3 = lax.rem(y + 1, RY), lax.rem(y + 2, RY), lax.rem(y + 3, RY)
    A1, A2, B1, B2 = {}, {}, {}, {}

    def sems(g, h, k):
        return a_send.at[g, h, k], a_recv.at[g, h, k]

    def start_a1(g):
        for h in range(2):
            L = lanes_of[h]
            for k in range(2):
                cross = pl.ds(2 * k, 2)
                if h == 0:
                    src, dev = c.at[g, cross, x2, :, L], xy(1 - 2 * k, 0)
                else:
                    src, dev = c.at[g, y2, cross, :, L], xy(0, 1 - 2 * k)
                A1[g, h, k] = go(remote(src, ra1.at[g, h, k], *sems(g, h, k), dev))

    def do_a2(g):
        for h in range(2):
            L = lanes_of[h]
            for k in range(2):
                A1[g, h, k].wait_recv()
                cross = pl.ds(2 * k, 2)
                if h == 0:
                    nxt = (x1, x3)[k]
                    c[g, cross, nxt, :, L] = c[g, cross, nxt, :, L] + ra1[g, h, k]
                    src, dev = c.at[g, :, nxt, :, L], xy(1 - 2 * k, 0)
                else:
                    nxt = (y1, y3)[k]
                    c[g, nxt, cross, :, L] = c[g, nxt, cross, :, L] + ra1[g, h, k]
                    src, dev = c.at[g, nxt, :, :, L], xy(0, 1 - 2 * k)
                A2[g, h, k] = go(remote(src, ra2.at[g, h, k], *sems(g, h, 2 + k), dev))

    def do_b1(g):
        for h in range(2):
            L = lanes_of[h]
            A2[g, h, 0].wait_recv()
            A2[g, h, 1].wait_recv()
            if h == 0:
                c[g, :, x, :, L] = c[g, :, x, :, L] + ra2[g, h, 0] + ra2[g, h, 1]
            else:
                c[g, y, :, :, L] = c[g, y, :, :, L] + ra2[g, h, 0] + ra2[g, h, 1]
            for k in range(2):
                part = pl.ds(16 * k, 16)
                if h == 0:
                    src, dev = c.at[g, y2, x, part, L], xy(0, 1 - 2 * k)
                else:
                    src, dev = c.at[g, y, x2, part, L], xy(1 - 2 * k, 0)
                B1[g, h, k] = go(remote(src, rb1.at[g, h, k], *sems(g, h, 4 + k), dev))

    def do_b2(g):
        for h in range(2):
            L = lanes_of[h]
            for k in range(2):
                B1[g, h, k].wait_recv()
                part = pl.ds(16 * k, 16)
                if h == 0:
                    nxt = (y1, y3)[k]
                    c[g, nxt, x, part, L] = c[g, nxt, x, part, L] + rb1[g, h, k]
                    src, dev = c.at[g, nxt, x, :, L], xy(0, 1 - 2 * k)
                else:
                    nxt = (x1, x3)[k]
                    c[g, y, nxt, part, L] = c[g, y, nxt, part, L] + rb1[g, h, k]
                    src, dev = c.at[g, y, nxt, :, L], xy(1 - 2 * k, 0)
                B2[g, h, k] = go(remote(src, rb2.at[g, h, k], *sems(g, h, 6 + k), dev))

    def do_b3(g):
        for h in range(2):
            L = lanes_of[h]
            B2[g, h, 0].wait_recv()
            B2[g, h, 1].wait_recv()
            c[g, y, x, :, L] = c[g, y, x, :, L] + rb2[g, h, 0] + rb2[g, h, 1]

    for g in range(RZ):
        start_a1(g)
    for g in range(2):
        do_a2(g)
    for g in range(RZ + 4):
        if g + 2 < RZ:
            do_a2(g + 2)
        if g < RZ:
            do_b1(g)
        if 0 <= g - 2 < RZ:
            do_b2(g - 2)
        if 0 <= g - 4 < RZ:
            do_b3(g - 4)

    zc = []
    for o in range(1, RZ):
        g = lax.rem(vy + o, RZ)
        zc.append(go(remote(c.at[g, y, x], rz.at[o - 1], z_send.at[o - 1], z_recv.at[o - 1], z_dev(o))))
    total = c[vy, y, x]
    for o in range(1, RZ):
        zc[o - 1].wait_recv()
        total = total + rz[o - 1]
    sk_ref[...] = total

    swap = go(remote(sk_ref, other, z_send.at[7], z_recv.at[7], partner))
    swap.wait_recv()
    theirs = other[...]
    first = jnp.where(sj == 0, 1.0, 0.0)
    left = total * first + theirs * (1.0 - first)
    right = theirs * first + total * (1.0 - first)
    parts = jnp.concatenate(split2(jnp.concatenate([left, right], axis=1)), axis=0)
    moved = jnp.dot(parts, mover, preferred_element_type=F32)
    mine = moved[:, :COLS] * first + moved[:, COLS:] * (1.0 - first)
    lhs = jnp.concatenate([mine[:KD], mine[:KD], mine[KD:]], axis=0).astype(BF16)
    rhs = jnp.concatenate([moved[:KD], moved[KD:], moved[:KD]], axis=0).astype(BF16)
    part = lax.dot_general(lhs, rhs, (((0,), (0,)), ((), ())), preferred_element_type=F32)
    for i in range(32):
        for j in range(4):
            gs[4 * i + j] = part[8 * i : 8 * i + 8, 128 * j : 128 * j + 128]

    cp = []
    for o in range(1, PLANE):
        d = lax.rem(vx + o, PLANE)
        cp.append(go(remote(gs.at[pl.ds(d * 8, 8)], r1.at[o - 1], g_send.at[0, o], g_recv.at[0, o], plane_dev(o))))
    acc = gs[pl.ds(vx * 8, 8)]
    for o in range(1, PLANE):
        cp[o - 1].wait_recv()
        acc = acc + r1[o - 1]
    p1[...] = acc
    cp = []
    for o in range(1, RZ):
        d = lax.rem(vy + o, RZ)
        cp.append(go(remote(p1.at[d], r2.at[o - 1], g_send.at[1, o], g_recv.at[1, o], z_dev(o))))
    acc = p1[vy]
    for o in range(1, RZ):
        cp[o - 1].wait_recv()
        acc = acc + r2[o - 1]
    p3[vy] = acc * (1.0 / 4096.0)
    cp = []
    for o in range(1, RZ):
        cp.append(go(remote(p3.at[vy], p3.at[vy], g_send.at[2, o], g_recv.at[2, o], z_dev(o))))
    for o in range(1, RZ):
        cp[o - 1].wait_recv()
    cp = []
    for o in range(1, PLANE):
        cp.append(go(remote(p3, out.at[pl.ds(vx * 8, 8)], g_send.at[3, o], g_recv.at[3, o], plane_dev(o))))
    out[pl.ds(vx * 8, 8)] = p3[...]
    for o in range(1, PLANE):
        cp[o - 1].wait_recv()
    for i in range(32):
        for j in range(4):
            gram_ref[8 * i : 8 * i + 8, 128 * j : 128 * j + 128] = out[4 * i + j]
    for copy in started:
        copy.wait_send()


def reduce_and_gram(order, c):
    V = pltpu.VMEM
    dma = pltpu.SemaphoreType.DMA
    return pl.pallas_call(
        comm_kernel,
        out_shape=(
            jax.ShapeDtypeStruct((KD, COLS), F32),
            jax.ShapeDtypeStruct((COLS, 2 * COLS), F32),
        ),
        in_specs=[pl.BlockSpec(memory_space=pltpu.SMEM), pl.BlockSpec(memory_space=pl.ANY)],
        out_specs=(pl.BlockSpec(memory_space=V), pl.BlockSpec(memory_space=V)),
        scratch_shapes=[
            V((RZ, RY, RX, KD, COLS), F32),
            V((RZ, 2, 2, 2, KD, HALF), F32),
            V((RZ, 2, 2, 4, KD, HALF), F32),
            V((RZ, 2, 2, KD // 2, HALF), F32),
            V((RZ, 2, 2, KD, HALF), F32),
            V((RZ - 1, KD, COLS), F32),
            V((KD, COLS), F32),
            V((128, 8, 128), F32),
            V((PLANE - 1, 8, 8, 128), F32),
            V((8, 8, 128), F32),
            V((RZ - 1, 8, 128), F32),
            V((8, 8, 128), F32),
            V((128, 8, 128), F32),
            dma,
            dma((RZ, 2, 8)),
            dma((RZ, 2, 8)),
            dma((8,)),
            dma((8,)),
            dma((4, 16)),
            dma((4, 16)),
        ],
        compiler_params=pltpu.CompilerParams(
            collective_id=1, has_side_effects=True, vmem_limit_bytes=40 * 1024 * 1024
        ),
        name="reduce_and_gram",
    )(order, c)


def on_device(volumes, flip_bits, hadamard_block, stratum_offset, subject_order):
    vol = volumes.reshape(COLS * 2, 8, 128)
    ext = sign_halo(flip_bits)
    block = hadamard_block.reshape(PLANE, RZ, KD)
    rc = (block * 16 + jnp.arange(PLANE, dtype=I32)[:, None, None]).transpose(0, 2, 1).reshape(PLANE * KD, RZ)
    so = stratum_offset.reshape(PLANE, RZ, KD).transpose(0, 2, 1).reshape(PLANE * KD, RZ)
    c = contributions(vol, ext, rc, so)
    return reduce_and_gram(subject_order, c)


def solution(mesh):
    placed = (P("subj", None, "vx", "vy", None), P("vx", "vy", None), P(), P(), P())
    return jax.shard_map(
        on_device,
        mesh=mesh,
        in_specs=placed,
        out_specs=(P(("vx", "vy"), "subj"), P("subj", None)),
        check_vma=False,
    )
```

```python
import jax
import jax.numpy as jnp
from jax import lax
from jax.experimental import pallas as pl
from jax.experimental.pallas import tpu as pltpu
from jax.sharding import PartitionSpec as P

MESH = pl.DeviceIdType.MESH
F32, BF16, I32 = jnp.float32, jnp.bfloat16, jnp.int32

w_side = 0.2741
w_mid = 0.4518

RX, RY, RZ = 4, 4, 8
PLANE = RX * RY
KD = 32
COLS = 256
HALF = 128
EX, EY = 4, 10
PLANES = EX * EY
STRATUM = 16


def split2(v):
    hi = v.astype(BF16)
    return hi, (v - hi.astype(F32)).astype(BF16)

HALO = [(dx, dy) for dx in (-1, 0, 1) for dy in (-1, 0, 1) if (dx, dy) != (0, 0)]
ORDER = (4, 3, 5, 2, 6, 1, 7, 0)
CHUNKS = 4
LAG_A2, LAG_B1, LAG_B2, LAG_B3 = 3, 5, 7, 9
BANDS = PLANES * STRATUM // 128


def parity_sign(bits, shifts):
    for s in shifts:
        bits = bits ^ (bits >> s)
    return jnp.where((bits & 1) == 0, 1.0, -1.0)


def kernel(
    order_ref, vol_hbm, flip_ref, block_ref, offset_ref, sk_ref, gram_ref,
    vol, halo, ext, codes, mover, zs, xs, tt_hi, tt_lo,
    c, ra1, ra2, rb1, rb2, rz, other, gs, r1, p1, r2, p3, out,
    ld_sem, h_send, h_recv, a_send, a_recv, z_send, z_recv, g_send, g_recv,
):
    vx, vy, sj = lax.axis_index("vx"), lax.axis_index("vy"), lax.axis_index("subj")
    x, y = lax.rem(vx, RX), lax.div(vx, RX)

    def xy(dx, dy):
        return (lax.rem(y + dy + RY, RY) * RX + lax.rem(x + dx + RX, RX), vy, sj)

    def plane_dev(o):
        return (lax.rem(vx + o, PLANE), vy, sj)

    def z_dev(o):
        return (vx, lax.rem(vy + o, RZ), sj)

    def near(dx, dy):
        return (lax.rem(vx + dx + PLANE, PLANE), lax.rem(vy + dy + RZ, RZ), sj)

    partner = (vx, vy, 1 - sj)

    loads = []
    per = COLS * 2 // CHUNKS
    for i in range(CHUNKS):
        part = pl.ds(i * per, per)
        loads.append(pltpu.make_async_copy(vol_hbm.at[part], vol.at[part], ld_sem.at[i]))
        loads[-1].start()

    barrier = pltpu.get_barrier_semaphore()
    peers = [plane_dev(o) for o in range(1, PLANE)] + [z_dev(o) for o in range(1, RZ)] + [partner]
    peers += [near(dx, dy) for dx, dy in HALO if dx * dy != 0]
    for d in peers:
        pl.semaphore_signal(barrier, inc=1, device_id=d, device_id_type=MESH)

    for bx in range(2):
        for by in range(8):
            ext[bx + 1, by + 1] = (2 * flip_ref[bx, pl.ds(by, 1), :] - 1).astype(F32)

    row = lax.broadcasted_iota(I32, (128, 128), 0)
    col = lax.broadcasted_iota(I32, (128, 128), 1)
    dist = jnp.abs(row - col)
    band = jnp.where(dist == 0, w_mid, jnp.where(dist == 1, w_side, 0.0)).astype(F32)
    wcat = jnp.concatenate(split2(band), axis=1)
    hz = parity_sign(row & col, (4, 2, 1)).astype(BF16)
    hcat = jnp.concatenate([hz, hz], axis=1)

    def smooth_z(i, _):
        v = vol[pl.ds(i * 32, 32)].astype(F32).reshape(256, 128).astype(BF16)
        r = jnp.dot(v, wcat, preferred_element_type=F32)
        zs[pl.ds(i * 256, 256), :] = r[:, :128] + r[:, 128:]
        return 0

    for i in range(CHUNKS):
        loads[i].wait()
        lax.fori_loop(i * per // 32, (i + 1) * per // 32, smooth_z, 0)

    def remote(src, dst, ssem, rsem, dev):
        return pltpu.make_async_remote_copy(
            src_ref=src, dst_ref=dst, send_sem=ssem, recv_sem=rsem, device_id=dev, device_id_type=MESH
        )

    started = []

    def go(copy):
        copy.start()
        started.append(copy)
        return copy

    pl.semaphore_wait(barrier, len(peers))
    signs = [
        go(remote(flip_ref, halo.at[i], h_send.at[i], h_recv.at[i], near(dx, dy)))
        for i, (dx, dy) in enumerate(HALO)
    ]

    zero = jnp.zeros((COLS, 128), F32)
    for ex in range(EX):
        for yi in (0, 1, 10, 11):
            xs[ex, yi] = zero
    for yi in range(8):
        a = zs[pl.ds(yi, COLS, stride=16), :]
        b = zs[pl.ds(8 + yi, COLS, stride=16), :]
        xs[0, yi + 2] = w_side * a
        xs[1, yi + 2] = w_mid * a + w_side * b
        xs[2, yi + 2] = w_side * a + w_mid * b
        xs[3, yi + 2] = w_side * b

    def plane(ex, yi):
        f = w_side * (xs[ex, yi] + xs[ex, yi + 2]) + w_mid * xs[ex, yi + 1]
        f = f * ext[ex, yi]
        fcat = jnp.concatenate(split2(f), axis=1)
        t = lax.dot_general(hcat, fcat, (((1,), (1,)), ((), ())), preferred_element_type=F32)
        thi, tlo = split2(t)
        at = pl.ds(pl.multiple_of((ex * EY + yi) * STRATUM, STRATUM), STRATUM)
        for g in range(RZ):
            tt_hi[g, at, :] = thi[g * STRATUM : (g + 1) * STRATUM, :]
            tt_lo[g, at, :] = tlo[g * STRATUM : (g + 1) * STRATUM, :]

    def own_planes(i, _):
        plane(1, i + 1)
        plane(2, i + 1)
        return 0

    lax.fori_loop(0, 8, own_planes, 0)

    code_t = (block_ref[...] * 16 + offset_ref[...]).astype(F32).T.astype(I32)
    for g in range(RZ):
        for p in range(PLANE):
            i = 2 * p + g // 4
            codes[g, p * KD : (p + 1) * KD, :] = jnp.broadcast_to(
                code_t[(g % 4) * KD : (g % 4 + 1) * KD, i : i + 1], (KD, 128)
            )

    lanes = lax.broadcasted_iota(I32, (64, 512), 1)
    rows = lax.broadcasted_iota(I32, (64, 512), 0)
    for s in range(8):
        mover[64 * s : 64 * s + 64, :] = jnp.where(lanes == order_ref[s] * 64 + rows, 1.0, 0.0).astype(BF16)

    okx = {-1: jnp.where(vx > 0, 1, 0), 0: 1, 1: jnp.where(vx < PLANE - 1, 1, 0)}
    oky = {-1: jnp.where(vy > 0, 1, 0), 0: 1, 1: jnp.where(vy < RZ - 1, 1, 0)}
    for copy in signs:
        copy.wait_recv()
    for i, (dx, dy) in enumerate(HALO):
        ok = (okx[-dx] * oky[-dy]).astype(F32)
        xpos = {-1: [(0, 1)], 0: [(1, 0), (2, 1)], 1: [(3, 0)]}[-dx]
        ypos = {-1: [(0, 7)], 0: [(k + 1, k) for k in range(8)], 1: [(9, 0)]}[-dy]
        for ex, bx in xpos:
            for ey, by in ypos:
                ext[ex, ey] = (2 * halo[i, bx, pl.ds(by, 1), :] - 1).astype(F32) * ok

    def x_planes(i, _):
        plane(0, i)
        plane(3, i)
        return 0

    def y_planes(i, _):
        plane(1, i * 9)
        plane(2, i * 9)
        return 0

    lax.fori_loop(0, EY, x_planes, 0)
    lax.fori_loop(0, 2, y_planes, 0)

    lane = lax.broadcasted_iota(I32, (1, 128), 1)
    gx = vx * 2 + lane // EY - 1 + 32
    gy = vy * 8 + lane % EY - 1 + 64
    voxel = (((gx >> 1) & 15) * 8 + ((gy >> 3) & 7)) * 16 + (gx & 1) * 8 + (gy & 7)
    off_lane = lane & 15
    ej = lax.broadcasted_iota(I32, (128, PLANES * STRATUM), 0)
    ek = lax.broadcasted_iota(I32, (128, PLANES * STRATUM), 1)
    spread = jnp.where((ek >> 4) == ej, 1.0, 0.0).astype(BF16)
    place = lax.broadcasted_iota(I32, (PLANE * KD, 128), 0) // KD

    def group(o):
        return lax.rem(vy + o, RZ)

    def contribute(o):
        g = group(o)
        code = codes[g]
        sgn = parity_sign(((code & -16) + place) & voxel, (8, 4, 2, 1)).astype(BF16)
        wide = jnp.dot(sgn, spread, preferred_element_type=F32)
        pick = (code & 15) == off_lane
        s_mat = jnp.concatenate(
            [jnp.where(pick, wide[:, k * 128 : (k + 1) * 128], 0.0).astype(BF16) for k in range(BANDS)], axis=1
        )
        r = jnp.dot(s_mat, tt_hi[g], preferred_element_type=F32)
        r = r + jnp.dot(s_mat, tt_lo[g], preferred_element_type=F32)
        c[g] = (r * (1.0 / 512.0)).reshape(RY, RX, KD, COLS)

    lanes_of = [pl.ds(0, HALF), pl.ds(HALF, HALF)]
    x1, x2, x3 = lax.rem(x + 1, RX), lax.rem(x + 2, RX), lax.rem(x + 3, RX)
    y1, y2, y3 = lax.rem(y + 1, RY), lax.rem(y + 2, RY), lax.rem(y + 3, RY)
    A1, A2, B1, B2, ZC = {}, {}, {}, {}, {}

    def sems(o, h, k):
        return a_send.at[o, h, k], a_recv.at[o, h, k]

    def start_a1(o):
        g = group(o)
        for h in range(2):
            L = lanes_of[h]
            for k in range(2):
                cross = pl.ds(2 * k, 2)
                if h == 0:
                    src, dev = c.at[g, cross, x2, :, L], xy(1 - 2 * k, 0)
                else:
                    src, dev = c.at[g, y2, cross, :, L], xy(0, 1 - 2 * k)
                A1[o, h, k] = go(remote(src, ra1.at[o, h, k], *sems(o, h, k), dev))

    def do_a2(o):
        g = group(o)
        for h in range(2):
            L = lanes_of[h]
            for k in range(2):
                A1[o, h, k].wait_recv()
                cross = pl.ds(2 * k, 2)
                if h == 0:
                    nxt = (x1, x3)[k]
                    c[g, cross, nxt, :, L] = c[g, cross, nxt, :, L] + ra1[o, h, k]
                    src, dev = c.at[g, :, nxt, :, L], xy(1 - 2 * k, 0)
                else:
                    nxt = (y1, y3)[k]
                    c[g, nxt, cross, :, L] = c[g, nxt, cross, :, L] + ra1[o, h, k]
                    src, dev = c.at[g, nxt, :, :, L], xy(0, 1 - 2 * k)
                A2[o, h, k] = go(remote(src, ra2.at[o, h, k], *sems(o, h, 2 + k), dev))

    def do_b1(o):
        g = group(o)
        for h in range(2):
            L = lanes_of[h]
            A2[o, h, 0].wait_recv()
            A2[o, h, 1].wait_recv()
            if h == 0:
                c[g, :, x, :, L] = c[g, :, x, :, L] + ra2[o, h, 0] + ra2[o, h, 1]
            else:
                c[g, y, :, :, L] = c[g, y, :, :, L] + ra2[o, h, 0] + ra2[o, h, 1]
            for k in range(2):
                part = pl.ds(16 * k, 16)
                if h == 0:
                    src, dev = c.at[g, y2, x, part, L], xy(0, 1 - 2 * k)
                else:
                    src, dev = c.at[g, y, x2, part, L], xy(1 - 2 * k, 0)
                B1[o, h, k] = go(remote(src, rb1.at[o, h, k], *sems(o, h, 4 + k), dev))

    def do_b2(o):
        g = group(o)
        for h in range(2):
            L = lanes_of[h]
            for k in range(2):
                B1[o, h, k].wait_recv()
                part = pl.ds(16 * k, 16)
                if h == 0:
                    nxt = (y1, y3)[k]
                    c[g, nxt, x, part, L] = c[g, nxt, x, part, L] + rb1[o, h, k]
                    src, dev = c.at[g, nxt, x, :, L], xy(0, 1 - 2 * k)
                else:
                    nxt = (x1, x3)[k]
                    c[g, y, nxt, part, L] = c[g, y, nxt, part, L] + rb1[o, h, k]
                    src, dev = c.at[g, y, nxt, :, L], xy(1 - 2 * k, 0)
                B2[o, h, k] = go(remote(src, rb2.at[o, h, k], *sems(o, h, 6 + k), dev))

    def do_b3(o):
        g = group(o)
        for h in range(2):
            L = lanes_of[h]
            B2[o, h, 0].wait_recv()
            B2[o, h, 1].wait_recv()
            c[g, y, x, :, L] = c[g, y, x, :, L] + rb2[o, h, 0] + rb2[o, h, 1]
        if o:
            ZC[o] = go(remote(c.at[g, y, x], rz.at[o - 1], z_send.at[o - 1], z_recv.at[o - 1], z_dev(o)))

    stages = ((0, contribute), (0, start_a1), (LAG_A2, do_a2), (LAG_B1, do_b1), (LAG_B2, do_b2), (LAG_B3, do_b3))
    for step in range(RZ + LAG_B3):
        for lag, stage in stages:
            if 0 <= step - lag < RZ:
                stage(ORDER[step - lag])

    total = c[vy, y, x]
    for o in ORDER[:-1]:
        ZC[o].wait_recv()
        total = total + rz[o - 1]
    sk_ref[...] = total

    swap = go(remote(sk_ref, other, z_send.at[7], z_recv.at[7], partner))
    swap.wait_recv()
    theirs = other[...]
    first = jnp.where(sj == 0, 1.0, 0.0)
    left = total * first + theirs * (1.0 - first)
    right = theirs * first + total * (1.0 - first)
    parts = jnp.concatenate(split2(jnp.concatenate([left, right], axis=1)), axis=0)
    moved = jnp.dot(parts, mover[...], preferred_element_type=F32)
    mine = moved[:, :COLS] * first + moved[:, COLS:] * (1.0 - first)
    lhs = jnp.concatenate([mine[:KD], mine[:KD], mine[KD:]], axis=0).astype(BF16)
    rhs = jnp.concatenate([moved[:KD], moved[KD:], moved[:KD]], axis=0).astype(BF16)
    part = lax.dot_general(lhs, rhs, (((0,), (0,)), ((), ())), preferred_element_type=F32)
    for i in range(32):
        for j in range(4):
            gs[4 * i + j] = part[8 * i : 8 * i + 8, 128 * j : 128 * j + 128]

    cp = []
    for o in range(1, PLANE):
        d = lax.rem(vx + o, PLANE)
        cp.append(go(remote(gs.at[pl.ds(d * 8, 8)], r1.at[o - 1], g_send.at[0, o], g_recv.at[0, o], plane_dev(o))))
    acc = gs[pl.ds(vx * 8, 8)]
    for o in range(1, PLANE):
        cp[o - 1].wait_recv()
        acc = acc + r1[o - 1]
    p1[...] = acc
    cp = []
    for o in range(1, RZ):
        d = lax.rem(vy + o, RZ)
        cp.append(go(remote(p1.at[d], r2.at[o - 1], g_send.at[1, o], g_recv.at[1, o], z_dev(o))))
    acc = p1[vy]
    for o in range(1, RZ):
        cp[o - 1].wait_recv()
        acc = acc + r2[o - 1]
    p3[vy] = acc * (1.0 / 4096.0)
    cp = []
    for o in range(1, RZ):
        cp.append(go(remote(p3.at[vy], p3.at[vy], g_send.at[2, o], g_recv.at[2, o], z_dev(o))))
    for o in range(1, RZ):
        cp[o - 1].wait_recv()
    cp = []
    for o in range(1, PLANE):
        cp.append(go(remote(p3, out.at[pl.ds(vx * 8, 8)], g_send.at[3, o], g_recv.at[3, o], plane_dev(o))))
    out[pl.ds(vx * 8, 8)] = p3[...]
    for o in range(1, PLANE):
        cp[o - 1].wait_recv()
    for i in range(32):
        for j in range(4):
            gram_ref[8 * i : 8 * i + 8, 128 * j : 128 * j + 128] = out[4 * i + j]
    for copy in started:
        copy.wait_send()


def sketch_and_gram(order, vol, flip, block, offset):
    V = pltpu.VMEM
    dma = pltpu.SemaphoreType.DMA
    return pl.pallas_call(
        kernel,
        out_shape=(
            jax.ShapeDtypeStruct((KD, COLS), F32),
            jax.ShapeDtypeStruct((COLS, 2 * COLS), F32),
        ),
        in_specs=[
            pl.BlockSpec(memory_space=pltpu.SMEM),
            pl.BlockSpec(memory_space=pl.ANY),
            pl.BlockSpec(memory_space=V),
            pl.BlockSpec(memory_space=V),
            pl.BlockSpec(memory_space=V),
        ],
        out_specs=(pl.BlockSpec(memory_space=V), pl.BlockSpec(memory_space=V)),
        scratch_shapes=[
            V((COLS * 2, 8, 128), BF16),
            V((8, 2, 8, 128), I32),
            V((EX, EY, 1, 128), F32),
            V((RZ, PLANE * KD, 128), I32),
            V((512, 512), BF16),
            V((COLS * 16, 128), F32),
            V((EX, EY + 2, COLS, 128), F32),
            V((RZ, PLANES * STRATUM, COLS), BF16),
            V((RZ, PLANES * STRATUM, COLS), BF16),
            V((RZ, RY, RX, KD, COLS), F32),
            V((RZ, 2, 2, 2, KD, HALF), F32),
            V((RZ, 2, 2, 4, KD, HALF), F32),
            V((RZ, 2, 2, KD // 2, HALF), F32),
            V((RZ, 2, 2, KD, HALF), F32),
            V((RZ - 1, KD, COLS), F32),
            V((KD, COLS), F32),
            V((128, 8, 128), F32),
            V((PLANE - 1, 8, 8, 128), F32),
            V((8, 8, 128), F32),
            V((RZ - 1, 8, 128), F32),
            V((8, 8, 128), F32),
            V((128, 8, 128), F32),
            dma((CHUNKS,)),
            dma((8,)),
            dma((8,)),
            dma((RZ, 2, 8)),
            dma((RZ, 2, 8)),
            dma((8,)),
            dma((8,)),
            dma((4, 16)),
            dma((4, 16)),
        ],
        compiler_params=pltpu.CompilerParams(
            collective_id=0, has_side_effects=True, vmem_limit_bytes=60 * 1024 * 1024
        ),
        name="sketch_and_gram",
    )(order, vol, flip, block, offset)


def on_device(volumes, flip_bits, hadamard_block, stratum_offset, subject_order):
    return sketch_and_gram(
        subject_order,
        volumes.reshape(COLS * 2, 8, 128),
        flip_bits,
        hadamard_block.reshape(32, 128),
        stratum_offset.reshape(32, 128),
    )


def solution(mesh):
    placed = (P("subj", None, "vx", "vy", None), P("vx", "vy", None), P(), P(), P())
    return jax.shard_map(
        on_device,
        mesh=mesh,
        in_specs=placed,
        out_specs=(P(("vx", "vy"), "subj"), P("subj", None)),
        check_vma=False,
    )
```

```python
import jax
import jax.numpy as jnp
from jax import lax
from jax.experimental import pallas as pl
from jax.experimental.pallas import tpu as pltpu
from jax.sharding import PartitionSpec as P

MESH = pl.DeviceIdType.MESH
F32, BF16, I32 = jnp.float32, jnp.bfloat16, jnp.int32

w_side = 0.2741
w_mid = 0.4518

RX, RY, RZ = 4, 4, 8
PLANE = RX * RY
KD = 32
COLS = 256
HALF = 128
EX, EY = 4, 10
PLANES = EX * EY
STRATUM = 16


def split2(v):
    hi = v.astype(BF16)
    return hi, (v - hi.astype(F32)).astype(BF16)

HALO = [(dx, dy) for dx in (-1, 0, 1) for dy in (-1, 0, 1) if (dx, dy) != (0, 0)]
ORDER = (4, 3, 5, 2, 6, 1, 7, 0)
CHUNKS = 4
LAG_A2, LAG_B1, LAG_B2, LAG_B3 = 3, 7, 9, 11
ZR = 8
XR = KD - ZR
BANDS = PLANES * STRATUM // 128


def parity_sign(bits, shifts):
    for s in shifts:
        bits = bits ^ (bits >> s)
    return jnp.where((bits & 1) == 0, 1.0, -1.0)


def kernel(
    order_ref, vol_hbm, flip_ref, block_ref, offset_ref, sk_ref, gram_ref,
    vol, halo, ext, codes, mover, zs, xs, tt_hi, tt_lo,
    c, ra1, ra2, rb1, rb2, rz, rv, rw, other, gs, r1, p1, r2, p3, out,
    ld_sem, h_send, h_recv, a_send, a_recv, z_send, z_recv, v_send, v_recv, g_send, g_recv,
):
    vx, vy, sj = lax.axis_index("vx"), lax.axis_index("vy"), lax.axis_index("subj")
    x, y = lax.rem(vx, RX), lax.div(vx, RX)

    def xy(dx, dy):
        return (lax.rem(y + dy + RY, RY) * RX + lax.rem(x + dx + RX, RX), vy, sj)

    def plane_dev(o):
        return (lax.rem(vx + o, PLANE), vy, sj)

    def z_dev(o):
        return (vx, lax.rem(vy + o, RZ), sj)

    def near(dx, dy):
        return (lax.rem(vx + dx + PLANE, PLANE), lax.rem(vy + dy + RZ, RZ), sj)

    partner = (vx, vy, 1 - sj)

    loads = []
    per = COLS * 2 // CHUNKS
    for i in range(CHUNKS):
        part = pl.ds(i * per, per)
        loads.append(pltpu.make_async_copy(vol_hbm.at[part], vol.at[part], ld_sem.at[i]))
        loads[-1].start()

    barrier = pltpu.get_barrier_semaphore()
    peers = [plane_dev(o) for o in range(1, PLANE)] + [z_dev(o) for o in range(1, RZ)] + [partner]
    peers += [near(dx, dy) for dx, dy in HALO if dx * dy != 0]
    for d in peers:
        pl.semaphore_signal(barrier, inc=1, device_id=d, device_id_type=MESH)

    for bx in range(2):
        for by in range(8):
            ext[bx + 1, by + 1] = (2 * flip_ref[bx, pl.ds(by, 1), :] - 1).astype(F32)

    row = lax.broadcasted_iota(I32, (128, 128), 0)
    col = lax.broadcasted_iota(I32, (128, 128), 1)
    dist = jnp.abs(row - col)
    band = jnp.where(dist == 0, w_mid, jnp.where(dist == 1, w_side, 0.0)).astype(F32)
    wcat = jnp.concatenate(split2(band), axis=1)
    hz = parity_sign(row & col, (4, 2, 1)).astype(BF16)
    hcat = jnp.concatenate([hz, hz], axis=1)

    def smooth_z(i, _):
        v = vol[pl.ds(i * 32, 32)].astype(F32).reshape(256, 128).astype(BF16)
        r = jnp.dot(v, wcat, preferred_element_type=F32)
        zs[pl.ds(i * 256, 256), :] = r[:, :128] + r[:, 128:]
        return 0

    for i in range(CHUNKS):
        loads[i].wait()
        lax.fori_loop(i * per // 32, (i + 1) * per // 32, smooth_z, 0)

    def remote(src, dst, ssem, rsem, dev):
        return pltpu.make_async_remote_copy(
            src_ref=src, dst_ref=dst, send_sem=ssem, recv_sem=rsem, device_id=dev, device_id_type=MESH
        )

    started = []

    def go(copy):
        copy.start()
        started.append(copy)
        return copy

    pl.semaphore_wait(barrier, len(peers))
    signs = [
        go(remote(flip_ref, halo.at[i], h_send.at[i], h_recv.at[i], near(dx, dy)))
        for i, (dx, dy) in enumerate(HALO)
    ]

    zero = jnp.zeros((COLS, 128), F32)
    for ex in range(EX):
        for yi in (0, 1, 10, 11):
            xs[ex, yi] = zero
    for yi in range(8):
        a = zs[pl.ds(yi, COLS, stride=16), :]
        b = zs[pl.ds(8 + yi, COLS, stride=16), :]
        xs[0, yi + 2] = w_side * a
        xs[1, yi + 2] = w_mid * a + w_side * b
        xs[2, yi + 2] = w_side * a + w_mid * b
        xs[3, yi + 2] = w_side * b

    def plane(ex, yi):
        f = w_side * (xs[ex, yi] + xs[ex, yi + 2]) + w_mid * xs[ex, yi + 1]
        f = f * ext[ex, yi]
        fcat = jnp.concatenate(split2(f), axis=1)
        t = lax.dot_general(hcat, fcat, (((1,), (1,)), ((), ())), preferred_element_type=F32)
        thi, tlo = split2(t)
        at = pl.ds(pl.multiple_of((ex * EY + yi) * STRATUM, STRATUM), STRATUM)
        for g in range(RZ):
            tt_hi[g, at, :] = thi[g * STRATUM : (g + 1) * STRATUM, :]
            tt_lo[g, at, :] = tlo[g * STRATUM : (g + 1) * STRATUM, :]

    def own_planes(i, _):
        plane(1, i + 1)
        plane(2, i + 1)
        return 0

    lax.fori_loop(0, 8, own_planes, 0)

    code_t = (block_ref[...] * 16 + offset_ref[...]).astype(F32).T.astype(I32)
    for g in range(RZ):
        for p in range(PLANE):
            i = 2 * p + g // 4
            codes[g, p * KD : (p + 1) * KD, :] = jnp.broadcast_to(
                code_t[(g % 4) * KD : (g % 4 + 1) * KD, i : i + 1], (KD, 128)
            )

    lanes = lax.broadcasted_iota(I32, (64, 512), 1)
    rows = lax.broadcasted_iota(I32, (64, 512), 0)
    for s in range(8):
        mover[64 * s : 64 * s + 64, :] = jnp.where(lanes == order_ref[s] * 64 + rows, 1.0, 0.0).astype(BF16)

    okx = {-1: jnp.where(vx > 0, 1, 0), 0: 1, 1: jnp.where(vx < PLANE - 1, 1, 0)}
    oky = {-1: jnp.where(vy > 0, 1, 0), 0: 1, 1: jnp.where(vy < RZ - 1, 1, 0)}
    for copy in signs:
        copy.wait_recv()
    for i, (dx, dy) in enumerate(HALO):
        ok = (okx[-dx] * oky[-dy]).astype(F32)
        xpos = {-1: [(0, 1)], 0: [(1, 0), (2, 1)], 1: [(3, 0)]}[-dx]
        ypos = {-1: [(0, 7)], 0: [(k + 1, k) for k in range(8)], 1: [(9, 0)]}[-dy]
        for ex, bx in xpos:
            for ey, by in ypos:
                ext[ex, ey] = (2 * halo[i, bx, pl.ds(by, 1), :] - 1).astype(F32) * ok

    def x_planes(i, _):
        plane(0, i)
        plane(3, i)
        return 0

    def y_planes(i, _):
        plane(1, i * 9)
        plane(2, i * 9)
        return 0

    lax.fori_loop(0, EY, x_planes, 0)
    lax.fori_loop(0, 2, y_planes, 0)

    lane = lax.broadcasted_iota(I32, (1, 128), 1)
    gx = vx * 2 + lane // EY - 1 + 32
    gy = vy * 8 + lane % EY - 1 + 64
    voxel = (((gx >> 1) & 15) * 8 + ((gy >> 3) & 7)) * 16 + (gx & 1) * 8 + (gy & 7)
    off_lane = lane & 15
    ej = lax.broadcasted_iota(I32, (128, PLANES * STRATUM), 0)
    ek = lax.broadcasted_iota(I32, (128, PLANES * STRATUM), 1)
    spread = jnp.where((ek >> 4) == ej, 1.0, 0.0).astype(BF16)
    place = lax.broadcasted_iota(I32, (PLANE * KD, 128), 0) // KD

    def group(o):
        return lax.rem(vy + o, RZ)

    def contribute(o):
        g = group(o)
        code = codes[g]
        sgn = parity_sign(((code & -16) + place) & voxel, (8, 4, 2, 1)).astype(BF16)
        wide = jnp.dot(sgn, spread, preferred_element_type=F32)
        pick = (code & 15) == off_lane
        s_mat = jnp.concatenate(
            [jnp.where(pick, wide[:, k * 128 : (k + 1) * 128], 0.0).astype(BF16) for k in range(BANDS)], axis=1
        )
        r = jnp.dot(s_mat, tt_hi[g], preferred_element_type=F32)
        r = r + jnp.dot(s_mat, tt_lo[g], preferred_element_type=F32)
        c[g] = (r * (1.0 / 512.0)).reshape(RY, RX, KD, COLS)

    lanes_of = [pl.ds(0, HALF), pl.ds(HALF, HALF)]
    X, ZF = pl.ds(ZR, XR), pl.ds(0, ZR)
    x1, x2, x3 = lax.rem(x + 1, RX), lax.rem(x + 2, RX), lax.rem(x + 3, RX)
    y1, y2, y3 = lax.rem(y + 1, RY), lax.rem(y + 2, RY), lax.rem(y + 3, RY)
    A1, A2, B1, B2, ZC, ZV, ZW = {}, {}, {}, {}, {}, {}, {}

    def sems(o, h, k):
        return a_send.at[o, h, k], a_recv.at[o, h, k]

    def start_a1(o):
        g = group(o)
        for h in range(2):
            L = lanes_of[h]
            for k in range(2):
                cross = pl.ds(2 * k, 2)
                if h == 0:
                    src, dev = c.at[g, cross, x2, X, L], xy(1 - 2 * k, 0)
                else:
                    src, dev = c.at[g, y2, cross, X, L], xy(0, 1 - 2 * k)
                A1[o, h, k] = go(remote(src, ra1.at[o, h, k], *sems(o, h, k), dev))

    def do_a2(o):
        g = group(o)
        for h in range(2):
            L = lanes_of[h]
            for k in range(2):
                A1[o, h, k].wait_recv()
                cross = pl.ds(2 * k, 2)
                if h == 0:
                    nxt = (x1, x3)[k]
                    c[g, cross, nxt, X, L] = c[g, cross, nxt, X, L] + ra1[o, h, k]
                    src, dev = c.at[g, :, nxt, X, L], xy(1 - 2 * k, 0)
                else:
                    nxt = (y1, y3)[k]
                    c[g, nxt, cross, X, L] = c[g, nxt, cross, X, L] + ra1[o, h, k]
                    src, dev = c.at[g, nxt, :, X, L], xy(0, 1 - 2 * k)
                A2[o, h, k] = go(remote(src, ra2.at[o, h, k], *sems(o, h, 2 + k), dev))

    def far_rows(o, k):
        return (pl.ds(ZR, 16), pl.ds(ZR + 16, XR - 16)) if o % 2 == 0 else (pl.ds(ZR + 8, 16), pl.ds(ZR, 8))

    def far_buf(o, h, k):
        return rb1.at[o, h, k, pl.ds(0, 16 - 8 * k)]

    def do_b1(o):
        g = group(o)
        for h in range(2):
            L = lanes_of[h]
            A2[o, h, 0].wait_recv()
            A2[o, h, 1].wait_recv()
            if h == 0:
                c[g, :, x, X, L] = c[g, :, x, X, L] + ra2[o, h, 0] + ra2[o, h, 1]
            else:
                c[g, y, :, X, L] = c[g, y, :, X, L] + ra2[o, h, 0] + ra2[o, h, 1]
            for k in range(2):
                part = far_rows(o, k)[k]
                way = (1 - 2 * k) * (1 if o % 2 == 0 else -1)
                if h == 0:
                    src, dev = c.at[g, y2, x, part, L], xy(0, way)
                else:
                    src, dev = c.at[g, y, x2, part, L], xy(way, 0)
                B1[o, h, k] = go(remote(src, far_buf(o, h, k), *sems(o, h, 4 + k), dev))

    def do_b2(o):
        g = group(o)
        for h in range(2):
            L = lanes_of[h]
            for k in range(2):
                B1[o, h, k].wait_recv()
                part = far_rows(o, k)[k]
                way = (1 - 2 * k) * (1 if o % 2 == 0 else -1)
                at = 0 if way == 1 else 1
                got = rb1[o, h, k, pl.ds(0, 16 - 8 * k)]
                if h == 0:
                    nxt = (y1, y3)[at]
                    c[g, nxt, x, part, L] = c[g, nxt, x, part, L] + got
                    src, dev = c.at[g, nxt, x, X, L], xy(0, way)
                else:
                    nxt = (x1, x3)[at]
                    c[g, y, nxt, part, L] = c[g, y, nxt, part, L] + got
                    src, dev = c.at[g, y, nxt, X, L], xy(way, 0)
                B2[o, h, k] = go(remote(src, rb2.at[o, h, k], *sems(o, h, 6 + k), dev))

    def do_b3(o):
        g = group(o)
        for h in range(2):
            L = lanes_of[h]
            B2[o, h, 0].wait_recv()
            B2[o, h, 1].wait_recv()
            c[g, y, x, X, L] = c[g, y, x, X, L] + rb2[o, h, 0] + rb2[o, h, 1]
        if o:
            ZC[o] = go(remote(c.at[g, y, x, X], rz.at[o - 1], z_send.at[o - 1], z_recv.at[o - 1], z_dev(o)))

    def ring(n):
        for k in range(2):
            if n > 1:
                ZV[n - 1, k].wait_recv()
            to = group((4 - n + 1) if k == 0 else (4 + n - 1))
            up = z_dev(1 if k == 0 else RZ - 1)
            if n == 1:
                half = pl.ds(2 * k, 2)
                src, dst = c.at[to, half, :, ZF], rv.at[0, k, pl.ds(0, 2)]
            else:
                if n == 2:
                    half = pl.ds(2 * k, 2)
                    c[to, half, :, ZF] = c[to, half, :, ZF] + rv[0, k, pl.ds(0, 2)]
                else:
                    c[to, :, :, ZF] = c[to, :, :, ZF] + rv[n - 2, k]
                src, dst = c.at[to, :, :, ZF], rv.at[n - 1, k]
            ZV[n, k] = go(remote(src, dst, v_send.at[0, 2 * n - 2 + k], v_recv.at[0, 2 * n - 2 + k], up))

    def spread_plane():
        ZV[4, 0].wait_recv()
        ZV[4, 1].wait_recv()
        c[vy, :, :, ZF] = c[vy, :, :, ZF] + rv[3, 0] + rv[3, 1]
        for o in range(1, PLANE):
            d = lax.rem(vx + o, PLANE)
            src = c.at[vy, lax.div(d, RX), lax.rem(d, RX), ZF]
            ZW[o] = go(remote(src, rw.at[o - 1], v_send.at[1, o], v_recv.at[1, o], plane_dev(o)))

    stages = ((0, contribute), (0, start_a1), (LAG_A2, do_a2), (LAG_B1, do_b1), (LAG_B2, do_b2), (LAG_B3, do_b3))
    ring_at = {0: 1, 3: 2, 6: 3, 8: 4}
    for step in range(RZ + LAG_B3):
        for lag, stage in stages[:2]:
            if 0 <= step - lag < RZ:
                stage(ORDER[step - lag])
        if step in ring_at:
            ring(ring_at[step])
        if step == 10:
            spread_plane()
        for lag, stage in stages[2:]:
            if 0 <= step - lag < RZ:
                stage(ORDER[step - lag])

    low = c[vy, y, x, ZF]
    for o in range(1, PLANE):
        ZW[o].wait_recv()
        low = low + rw[o - 1]
    high = c[vy, y, x, X]
    for o in ORDER[:-1]:
        ZC[o].wait_recv()
        high = high + rz[o - 1]
    total = jnp.concatenate([low, high], axis=0)
    sk_ref[...] = total

    swap = go(remote(sk_ref, other, z_send.at[7], z_recv.at[7], partner))
    swap.wait_recv()
    theirs = other[...]
    first = jnp.where(sj == 0, 1.0, 0.0)
    left = total * first + theirs * (1.0 - first)
    right = theirs * first + total * (1.0 - first)
    parts = jnp.concatenate(split2(jnp.concatenate([left, right], axis=1)), axis=0)
    moved = jnp.dot(parts, mover[...], preferred_element_type=F32)
    mine = moved[:, :COLS] * first + moved[:, COLS:] * (1.0 - first)
    lhs = jnp.concatenate([mine[:KD], mine[:KD], mine[KD:]], axis=0).astype(BF16)
    rhs = jnp.concatenate([moved[:KD], moved[KD:], moved[:KD]], axis=0).astype(BF16)
    part = lax.dot_general(lhs, rhs, (((0,), (0,)), ((), ())), preferred_element_type=F32)
    for i in range(32):
        for j in range(4):
            gs[4 * i + j] = part[8 * i : 8 * i + 8, 128 * j : 128 * j + 128]

    cp = []
    for o in range(1, PLANE):
        d = lax.rem(vx + o, PLANE)
        cp.append(go(remote(gs.at[pl.ds(d * 8, 8)], r1.at[o - 1], g_send.at[0, o], g_recv.at[0, o], plane_dev(o))))
    acc = gs[pl.ds(vx * 8, 8)]
    for o in range(1, PLANE):
        cp[o - 1].wait_recv()
        acc = acc + r1[o - 1]
    p1[...] = acc
    cp = []
    for o in range(1, RZ):
        d = lax.rem(vy + o, RZ)
        cp.append(go(remote(p1.at[d], r2.at[o - 1], g_send.at[1, o], g_recv.at[1, o], z_dev(o))))
    acc = p1[vy]
    for o in range(1, RZ):
        cp[o - 1].wait_recv()
        acc = acc + r2[o - 1]
    p3[vy] = acc * (1.0 / 4096.0)
    cp = []
    for o in range(1, RZ):
        cp.append(go(remote(p3.at[vy], p3.at[vy], g_send.at[2, o], g_recv.at[2, o], z_dev(o))))
    for o in range(1, RZ):
        cp[o - 1].wait_recv()
    cp = []
    for o in range(1, PLANE):
        cp.append(go(remote(p3, out.at[pl.ds(vx * 8, 8)], g_send.at[3, o], g_recv.at[3, o], plane_dev(o))))
    out[pl.ds(vx * 8, 8)] = p3[...]
    for o in range(1, PLANE):
        cp[o - 1].wait_recv()
    for i in range(32):
        for j in range(4):
            gram_ref[8 * i : 8 * i + 8, 128 * j : 128 * j + 128] = out[4 * i + j]
    for copy in started:
        copy.wait_send()


def sketch_and_gram(order, vol, flip, block, offset):
    V = pltpu.VMEM
    dma = pltpu.SemaphoreType.DMA
    return pl.pallas_call(
        kernel,
        out_shape=(
            jax.ShapeDtypeStruct((KD, COLS), F32),
            jax.ShapeDtypeStruct((COLS, 2 * COLS), F32),
        ),
        in_specs=[
            pl.BlockSpec(memory_space=pltpu.SMEM),
            pl.BlockSpec(memory_space=pl.ANY),
            pl.BlockSpec(memory_space=V),
            pl.BlockSpec(memory_space=V),
            pl.BlockSpec(memory_space=V),
        ],
        out_specs=(pl.BlockSpec(memory_space=V), pl.BlockSpec(memory_space=V)),
        scratch_shapes=[
            V((COLS * 2, 8, 128), BF16),
            V((8, 2, 8, 128), I32),
            V((EX, EY, 1, 128), F32),
            V((RZ, PLANE * KD, 128), I32),
            V((512, 512), BF16),
            V((COLS * 16, 128), F32),
            V((EX, EY + 2, COLS, 128), F32),
            V((RZ, PLANES * STRATUM, COLS), BF16),
            V((RZ, PLANES * STRATUM, COLS), BF16),
            V((RZ, RY, RX, KD, COLS), F32),
            V((RZ, 2, 2, 2, XR, HALF), F32),
            V((RZ, 2, 2, 4, XR, HALF), F32),
            V((RZ, 2, 2, 16, HALF), F32),
            V((RZ, 2, 2, XR, HALF), F32),
            V((RZ - 1, XR, COLS), F32),
            V((4, 2, RY, RX, ZR, COLS), F32),
            V((PLANE - 1, ZR, COLS), F32),
            V((KD, COLS), F32),
            V((128, 8, 128), F32),
            V((PLANE - 1, 8, 8, 128), F32),
            V((8, 8, 128), F32),
            V((RZ - 1, 8, 128), F32),
            V((8, 8, 128), F32),
            V((128, 8, 128), F32),
            dma((CHUNKS,)),
            dma((8,)),
            dma((8,)),
            dma((RZ, 2, 8)),
            dma((RZ, 2, 8)),
            dma((8,)),
            dma((8,)),
            dma((2, 16)),
            dma((2, 16)),
            dma((4, 16)),
            dma((4, 16)),
        ],
        compiler_params=pltpu.CompilerParams(
            collective_id=0, has_side_effects=True, vmem_limit_bytes=60 * 1024 * 1024
        ),
        name="sketch_and_gram",
    )(order, vol, flip, block, offset)


def on_device(volumes, flip_bits, hadamard_block, stratum_offset, subject_order):
    return sketch_and_gram(
        subject_order,
        volumes.reshape(COLS * 2, 8, 128),
        flip_bits,
        hadamard_block.reshape(32, 128),
        stratum_offset.reshape(32, 128),
    )


def solution(mesh):
    placed = (P("subj", None, "vx", "vy", None), P("vx", "vy", None), P(), P(), P())
    return jax.shard_map(
        on_device,
        mesh=mesh,
        in_specs=placed,
        out_specs=(P(("vx", "vy"), "subj"), P("subj", None)),
        check_vma=False,
    )
```

```python
import jax
import jax.numpy as jnp
from jax import lax
from jax.experimental import pallas as pl
from jax.experimental.pallas import tpu as pltpu
from jax.sharding import PartitionSpec as P

MESH = pl.DeviceIdType.MESH
F32, BF16, I32 = jnp.float32, jnp.bfloat16, jnp.int32

w_side = 0.2741
w_mid = 0.4518

RX, RY, RZ = 4, 4, 8
PLANE = RX * RY
KD = 32
COLS = 256
HALF = 128
EX, EY = 4, 10
PLANES = EX * EY
STRATUM = 16


def split2(v):
    hi = v.astype(BF16)
    return hi, (v - hi.astype(F32)).astype(BF16)

HALO = [(dx, dy) for dx in (-1, 0, 1) for dy in (-1, 0, 1) if (dx, dy) != (0, 0)]
ORDER = (4, 3, 5, 2, 6, 1, 7, 0)
CHUNKS = 4
LAG_A2, LAG_B1, LAG_B2, LAG_B3 = 2, 4, 6, 8
PAIRS = RZ // 2
ZR = 8
XR = KD - ZR
BANDS = PLANES * STRATUM // 128


def parity_sign(bits, shifts):
    for s in shifts:
        bits = bits ^ (bits >> s)
    return jnp.where((bits & 1) == 0, 1.0, -1.0)


def kernel(
    order_ref, vol_hbm, flip_ref, block_ref, offset_ref, sk_ref, gram_ref,
    vol, halo, ext, tables, mover, zs, xs, tt_hi, tt_lo,
    c, ra1, ra2, rb1, rb2, rz, rv, rw, other, gs, r1, p1, r2, p3, out,
    ld_sem, h_send, h_recv, a_send, a_recv, z_send, z_recv, v_send, v_recv, g_send, g_recv,
):
    vx, vy, sj = lax.axis_index("vx"), lax.axis_index("vy"), lax.axis_index("subj")
    x, y = lax.rem(vx, RX), lax.div(vx, RX)

    def xy(dx, dy):
        return (lax.rem(y + dy + RY, RY) * RX + lax.rem(x + dx + RX, RX), vy, sj)

    def plane_dev(o):
        return (lax.rem(vx + o, PLANE), vy, sj)

    def z_dev(o):
        return (vx, lax.rem(vy + o, RZ), sj)

    def near(dx, dy):
        return (lax.rem(vx + dx + PLANE, PLANE), lax.rem(vy + dy + RZ, RZ), sj)

    partner = (vx, vy, 1 - sj)

    loads = []
    per = COLS * 2 // CHUNKS
    for i in range(CHUNKS):
        part = pl.ds(i * per, per)
        loads.append(pltpu.make_async_copy(vol_hbm.at[part], vol.at[part], ld_sem.at[i]))
        loads[-1].start()

    barrier = pltpu.get_barrier_semaphore()
    peers = [plane_dev(o) for o in range(1, PLANE)] + [z_dev(o) for o in range(1, RZ)] + [partner]
    peers += [near(dx, dy) for dx, dy in HALO if dx * dy != 0]
    for d in peers:
        pl.semaphore_signal(barrier, inc=1, device_id=d, device_id_type=MESH)

    for bx in range(2):
        for by in range(8):
            ext[bx + 1, by + 1] = (2 * flip_ref[bx, pl.ds(by, 1), :] - 1).astype(F32)

    row = lax.broadcasted_iota(I32, (128, 128), 0)
    col = lax.broadcasted_iota(I32, (128, 128), 1)
    dist = jnp.abs(row - col)
    band = jnp.where(dist == 0, w_mid, jnp.where(dist == 1, w_side, 0.0)).astype(F32)
    wcat = jnp.concatenate(split2(band), axis=1)
    hz = parity_sign(row & col, (4, 2, 1)).astype(BF16)
    hcat = jnp.concatenate([hz, hz], axis=1)

    def smooth_z(i, _):
        v = vol[pl.ds(i * 32, 32)].astype(F32).reshape(256, 128).astype(BF16)
        r = jnp.dot(v, wcat, preferred_element_type=F32)
        zs[pl.ds(i * 256, 256), :] = r[:, :128] + r[:, 128:]
        return 0

    for i in range(CHUNKS):
        loads[i].wait()
        lax.fori_loop(i * per // 32, (i + 1) * per // 32, smooth_z, 0)

    def remote(src, dst, ssem, rsem, dev):
        return pltpu.make_async_remote_copy(
            src_ref=src, dst_ref=dst, send_sem=ssem, recv_sem=rsem, device_id=dev, device_id_type=MESH
        )

    started = []

    def go(copy):
        copy.start()
        started.append(copy)
        return copy

    pl.semaphore_wait(barrier, len(peers))
    signs = [
        go(remote(flip_ref, halo.at[i], h_send.at[i], h_recv.at[i], near(dx, dy)))
        for i, (dx, dy) in enumerate(HALO)
    ]

    zero = jnp.zeros((COLS, 128), F32)
    for ex in range(EX):
        for yi in (0, 1, 10, 11):
            xs[ex, yi] = zero
    for yi in range(8):
        a = zs[pl.ds(yi, COLS, stride=16), :]
        b = zs[pl.ds(8 + yi, COLS, stride=16), :]
        xs[0, yi + 2] = w_side * a
        xs[1, yi + 2] = w_mid * a + w_side * b
        xs[2, yi + 2] = w_side * a + w_mid * b
        xs[3, yi + 2] = w_side * b

    def plane(ex, yi):
        f = w_side * (xs[ex, yi] + xs[ex, yi + 2]) + w_mid * xs[ex, yi + 1]
        f = f * ext[ex, yi]
        fcat = jnp.concatenate(split2(f), axis=1)
        t = lax.dot_general(hcat, fcat, (((1,), (1,)), ((), ())), preferred_element_type=F32)
        thi, tlo = split2(t)
        at = pl.ds(pl.multiple_of((ex * EY + yi) * STRATUM, STRATUM), STRATUM)
        for g in range(RZ):
            tt_hi[g, at, :] = thi[g * STRATUM : (g + 1) * STRATUM, :]
            tt_lo[g, at, :] = tlo[g * STRATUM : (g + 1) * STRATUM, :]

    def own_planes(i, _):
        plane(1, i + 1)
        plane(2, i + 1)
        return 0

    lax.fori_loop(0, 8, own_planes, 0)

    code_t = (block_ref[...] * 16 + offset_ref[...]).astype(F32).T.astype(I32)
    lane = lax.broadcasted_iota(I32, (1, 128), 1)
    gx = vx * 2 + lane // EY - 1 + 32
    gy = vy * 8 + lane % EY - 1 + 64
    voxel = (((gx >> 1) & 15) * 8 + ((gy >> 3) & 7)) * 16 + (gx & 1) * 8 + (gy & 7)
    off_lane = lane & 15
    ej = lax.broadcasted_iota(I32, (128, PLANES * STRATUM), 0)
    ek = lax.broadcasted_iota(I32, (128, PLANES * STRATUM), 1)
    spread = jnp.where((ek >> 4) == ej, 1.0, 0.0).astype(BF16)
    place = lax.broadcasted_iota(I32, (PLANE * KD, 128), 0) // KD
    for g in range(RZ):
        code = jnp.concatenate(
            [
                jnp.broadcast_to(
                    code_t[(g % 4) * KD : (g % 4 + 1) * KD, 2 * p + g // 4 : 2 * p + g // 4 + 1], (KD, 128)
                )
                for p in range(PLANE)
            ],
            axis=0,
        )
        sgn = parity_sign(((code & -16) + place) & voxel, (8, 4, 2, 1)).astype(BF16)
        wide = jnp.dot(sgn, spread, preferred_element_type=F32)
        pick = (code & 15) == off_lane
        for k in range(BANDS):
            at = slice(k * 128, (k + 1) * 128)
            tables[g, :, at] = jnp.where(pick, wide[:, at], 0.0).astype(BF16)

    lanes = lax.broadcasted_iota(I32, (64, 512), 1)
    rows = lax.broadcasted_iota(I32, (64, 512), 0)
    for s in range(8):
        mover[64 * s : 64 * s + 64, :] = jnp.where(lanes == order_ref[s] * 64 + rows, 1.0, 0.0).astype(BF16)

    okx = {-1: jnp.where(vx > 0, 1, 0), 0: 1, 1: jnp.where(vx < PLANE - 1, 1, 0)}
    oky = {-1: jnp.where(vy > 0, 1, 0), 0: 1, 1: jnp.where(vy < RZ - 1, 1, 0)}
    for copy in signs:
        copy.wait_recv()
    for i, (dx, dy) in enumerate(HALO):
        ok = (okx[-dx] * oky[-dy]).astype(F32)
        xpos = {-1: [(0, 1)], 0: [(1, 0), (2, 1)], 1: [(3, 0)]}[-dx]
        ypos = {-1: [(0, 7)], 0: [(k + 1, k) for k in range(8)], 1: [(9, 0)]}[-dy]
        for ex, bx in xpos:
            for ey, by in ypos:
                ext[ex, ey] = (2 * halo[i, bx, pl.ds(by, 1), :] - 1).astype(F32) * ok

    def x_planes(i, _):
        plane(0, i)
        plane(3, i)
        return 0

    def y_planes(i, _):
        plane(1, i * 9)
        plane(2, i * 9)
        return 0

    lax.fori_loop(0, EY, x_planes, 0)
    lax.fori_loop(0, 2, y_planes, 0)

    def contribute(t):
        g = lax.rem(vy + ORDER[t], RZ)
        r = jnp.dot(tables[g], tt_hi[g], preferred_element_type=F32)
        r = (r + jnp.dot(tables[g], tt_lo[g], preferred_element_type=F32)) * (1.0 / 512.0)
        for p in range(PLANE):
            dy, dx = lax.rem(p // RX - y + RY, RY), lax.rem(p % RX - x + RX, RX)
            c[t, dy, dx] = r[p * KD : (p + 1) * KD]

    lanes_of = [pl.ds(0, HALF), pl.ds(HALF, HALF)]
    X, ZF = pl.ds(ZR, XR), pl.ds(0, ZR)
    A1, A2, B1, B2, ZC, ZV, ZW = {}, {}, {}, {}, {}, {}, {}
    WAYS = ((1, 1), (-1, 3))

    def sems(u, h, k):
        return a_send.at[u, h, k], a_recv.at[u, h, k]

    def first(h, way):
        return xy(way, 0) if h == 0 else xy(0, way)

    def second(h, way):
        return xy(0, way) if h == 0 else xy(way, 0)

    def block(h, U, near_axis, other_axis):
        return (U, other_axis, near_axis) if h == 0 else (U, near_axis, other_axis)

    def start_a1(u):
        U = pl.ds(2 * u, 2)
        for h in range(2):
            for k in range(2):
                src = c.at[(*block(h, U, 2, pl.ds(2 * k, 2)), X, lanes_of[h])]
                A1[u, h, k] = go(remote(src, ra1.at[u, h, k], *sems(u, h, k), first(h, WAYS[k][0])))

    def do_a2(u):
        U = pl.ds(2 * u, 2)
        for h in range(2):
            for k in range(2):
                way, near_pos = WAYS[k]
                A1[u, h, k].wait_recv()
                at = (*block(h, U, near_pos, pl.ds(2 * k, 2)), X, lanes_of[h])
                c[at] = c[at] + ra1[u, h, k]
                src = c.at[(*block(h, U, near_pos, pl.ds(0, 4)), X, lanes_of[h])]
                A2[u, h, k] = go(remote(src, ra2.at[u, h, k], *sems(u, h, 2 + k), first(h, way)))

    def far(u, k):
        rows = (16, XR - 16)[(k + u) % 2]
        return pl.ds(ZR if k == 0 else ZR + XR - rows, rows), pl.ds(0, rows)

    def do_b1(u):
        U = pl.ds(2 * u, 2)
        for h in range(2):
            A2[u, h, 0].wait_recv()
            A2[u, h, 1].wait_recv()
            at = (*block(h, U, 0, pl.ds(0, 4)), X, lanes_of[h])
            c[at] = c[at] + ra2[u, h, 0] + ra2[u, h, 1]
            for k in range(2):
                part, room = far(u, k)
                src = c.at[(*block(h, U, 0, 2), part, lanes_of[h])]
                B1[u, h, k] = go(remote(src, rb1.at[u, h, k, :, room], *sems(u, h, 4 + k), second(h, WAYS[k][0])))

    def do_b2(u):
        U = pl.ds(2 * u, 2)
        for h in range(2):
            for k in range(2):
                way, near_pos = WAYS[k]
                B1[u, h, k].wait_recv()
                part, room = far(u, k)
                at = (*block(h, U, 0, near_pos), part, lanes_of[h])
                c[at] = c[at] + rb1[u, h, k, :, room]
                src = c.at[(*block(h, U, 0, near_pos), X, lanes_of[h])]
                B2[u, h, k] = go(remote(src, rb2.at[u, h, k], *sems(u, h, 6 + k), second(h, way)))

    def do_b3(u):
        U = pl.ds(2 * u, 2)
        for h in range(2):
            B2[u, h, 0].wait_recv()
            B2[u, h, 1].wait_recv()
            at = (U, 0, 0, X, lanes_of[h])
            c[at] = c[at] + rb2[u, h, 0] + rb2[u, h, 1]
        for t in (2 * u, 2 * u + 1):
            o = ORDER[t]
            if o:
                ZC[o] = go(remote(c.at[t, 0, 0, X], rz.at[o - 1], z_send.at[o - 1], z_recv.at[o - 1], z_dev(o)))

    def ring(n):
        for b in range(2):
            for k in range(2):
                to = ORDER.index(5 - n if k == 0 else 3 + n)
                if n == 1:
                    own = pl.ds(2 * k + b, 1)
                    src, dst = c.at[to, own, :, ZF], rv.at[0, b, k, pl.ds(0, 1)]
                else:
                    at = b ^ k ^ 1 if n == 2 else b
                    own = pl.ds(2 * at, 2)
                    if n == 2 and b == 1:
                        for i in range(2):
                            ZV[1, i, k].wait_recv()
                            c[to, 2 * k + i, :, ZF] = c[to, 2 * k + i, :, ZF] + rv[0, i, k, 0]
                    elif n > 2:
                        ZV[n - 1, b, k].wait_recv()
                        c[to, own, :, ZF] = c[to, own, :, ZF] + rv[n - 2, b, k]
                    src, dst = c.at[to, own, :, ZF], rv.at[n - 1, at, k]
                piece = at if n == 2 else b
                dev = z_dev(1 if k == 0 else RZ - 1)
                i = 4 * (n - 1) + 2 * piece + k
                ZV[n, piece, k] = go(remote(src, dst, v_send.at[0, i], v_recv.at[0, i], dev))

    def spread_plane():
        t = ORDER.index(0)
        for b in range(2):
            ZV[4, b, 0].wait_recv()
            ZV[4, b, 1].wait_recv()
            own = pl.ds(2 * b, 2)
            c[t, own, :, ZF] = c[t, own, :, ZF] + rv[3, b, 0] + rv[3, b, 1]
        for o in range(1, PLANE):
            dy, dx = o // RX, o % RX
            ZW[o] = go(remote(c.at[t, dy, dx, ZF], rw.at[o - 1], v_send.at[1, o], v_recv.at[1, o], xy(dx, dy)))

    stages = ((LAG_A2, do_a2), (LAG_B1, do_b1), (LAG_B2, do_b2), (LAG_B3, do_b3))
    ring_at = {1: 0, 2: 2, 3: 4, 4: 5}
    for step in range(PAIRS + LAG_B3):
        if step < PAIRS:
            contribute(2 * step)
            if step == 0:
                ring(1)
            contribute(2 * step + 1)
            start_a1(step)
        for n in (2, 3, 4):
            if ring_at[n] == step:
                ring(n)
        for lag, stage in stages:
            if 0 <= step - lag < PAIRS:
                stage(step - lag)
        if step == 6:
            spread_plane()

    low = c[RZ - 1, 0, 0, ZF]
    for o in range(1, PLANE):
        ZW[o].wait_recv()
        low = low + rw[o - 1]
    high = c[RZ - 1, 0, 0, X]
    for o in ORDER[:-1]:
        ZC[o].wait_recv()
        high = high + rz[o - 1]
    total = jnp.concatenate([low, high], axis=0)
    sk_ref[...] = total

    swap = go(remote(sk_ref, other, z_send.at[7], z_recv.at[7], partner))
    swap.wait_recv()
    theirs = other[...]
    first = jnp.where(sj == 0, 1.0, 0.0)
    left = total * first + theirs * (1.0 - first)
    right = theirs * first + total * (1.0 - first)
    parts = jnp.concatenate(split2(jnp.concatenate([left, right], axis=1)), axis=0)
    moved = jnp.dot(parts, mover[...], preferred_element_type=F32)
    mine = moved[:, :COLS] * first + moved[:, COLS:] * (1.0 - first)
    lhs = jnp.concatenate([mine[:KD], mine[:KD], mine[KD:]], axis=0).astype(BF16)
    rhs = jnp.concatenate([moved[:KD], moved[KD:], moved[:KD]], axis=0).astype(BF16)
    part = lax.dot_general(lhs, rhs, (((0,), (0,)), ((), ())), preferred_element_type=F32)
    for i in range(32):
        for j in range(4):
            gs[4 * i + j] = part[8 * i : 8 * i + 8, 128 * j : 128 * j + 128]

    cp = []
    for o in range(1, PLANE):
        d = lax.rem(vx + o, PLANE)
        cp.append(go(remote(gs.at[pl.ds(d * 8, 8)], r1.at[o - 1], g_send.at[0, o], g_recv.at[0, o], plane_dev(o))))
    acc = gs[pl.ds(vx * 8, 8)]
    for o in range(1, PLANE):
        cp[o - 1].wait_recv()
        acc = acc + r1[o - 1]
    p1[...] = acc
    cp = []
    for o in range(1, RZ):
        d = lax.rem(vy + o, RZ)
        cp.append(go(remote(p1.at[d], r2.at[o - 1], g_send.at[1, o], g_recv.at[1, o], z_dev(o))))
    acc = p1[vy]
    for o in range(1, RZ):
        cp[o - 1].wait_recv()
        acc = acc + r2[o - 1]
    p3[vy] = acc * (1.0 / 4096.0)
    cp = []
    for o in range(1, RZ):
        cp.append(go(remote(p3.at[vy], p3.at[vy], g_send.at[2, o], g_recv.at[2, o], z_dev(o))))
    for o in range(1, RZ):
        cp[o - 1].wait_recv()
    cp = []
    for o in range(1, PLANE):
        cp.append(go(remote(p3, out.at[pl.ds(vx * 8, 8)], g_send.at[3, o], g_recv.at[3, o], plane_dev(o))))
    out[pl.ds(vx * 8, 8)] = p3[...]
    for o in range(1, PLANE):
        cp[o - 1].wait_recv()
    for i in range(32):
        for j in range(4):
            gram_ref[8 * i : 8 * i + 8, 128 * j : 128 * j + 128] = out[4 * i + j]
    for copy in started:
        copy.wait_send()


def sketch_and_gram(order, vol, flip, block, offset):
    V = pltpu.VMEM
    dma = pltpu.SemaphoreType.DMA
    return pl.pallas_call(
        kernel,
        out_shape=(
            jax.ShapeDtypeStruct((KD, COLS), F32),
            jax.ShapeDtypeStruct((COLS, 2 * COLS), F32),
        ),
        in_specs=[
            pl.BlockSpec(memory_space=pltpu.SMEM),
            pl.BlockSpec(memory_space=pl.ANY),
            pl.BlockSpec(memory_space=V),
            pl.BlockSpec(memory_space=V),
            pl.BlockSpec(memory_space=V),
        ],
        out_specs=(pl.BlockSpec(memory_space=V), pl.BlockSpec(memory_space=V)),
        scratch_shapes=[
            V((COLS * 2, 8, 128), BF16),
            V((8, 2, 8, 128), I32),
            V((EX, EY, 1, 128), F32),
            V((RZ, PLANE * KD, PLANES * STRATUM), BF16),
            V((512, 512), BF16),
            V((COLS * 16, 128), F32),
            V((EX, EY + 2, COLS, 128), F32),
            V((RZ, PLANES * STRATUM, COLS), BF16),
            V((RZ, PLANES * STRATUM, COLS), BF16),
            V((RZ, RY, RX, KD, COLS), F32),
            V((PAIRS, 2, 2, 2, 2, XR, HALF), F32),
            V((PAIRS, 2, 2, 2, 4, XR, HALF), F32),
            V((PAIRS, 2, 2, 2, 16, HALF), F32),
            V((PAIRS, 2, 2, 2, XR, HALF), F32),
            V((RZ - 1, XR, COLS), F32),
            V((4, 2, 2, 2, RX, ZR, COLS), F32),
            V((PLANE - 1, ZR, COLS), F32),
            V((KD, COLS), F32),
            V((128, 8, 128), F32),
            V((PLANE - 1, 8, 8, 128), F32),
            V((8, 8, 128), F32),
            V((RZ - 1, 8, 128), F32),
            V((8, 8, 128), F32),
            V((128, 8, 128), F32),
            dma((CHUNKS,)),
            dma((8,)),
            dma((8,)),
            dma((PAIRS, 2, 8)),
            dma((PAIRS, 2, 8)),
            dma((8,)),
            dma((8,)),
            dma((2, 16)),
            dma((2, 16)),
            dma((4, 16)),
            dma((4, 16)),
        ],
        compiler_params=pltpu.CompilerParams(
            collective_id=0, has_side_effects=True, vmem_limit_bytes=60 * 1024 * 1024
        ),
        name="sketch_and_gram",
    )(order, vol, flip, block, offset)


def on_device(volumes, flip_bits, hadamard_block, stratum_offset, subject_order):
    return sketch_and_gram(
        subject_order,
        volumes.reshape(COLS * 2, 8, 128),
        flip_bits,
        hadamard_block.reshape(32, 128),
        stratum_offset.reshape(32, 128),
    )


def solution(mesh):
    placed = (P("subj", None, "vx", "vy", None), P("vx", "vy", None), P(), P(), P())
    return jax.shard_map(
        on_device,
        mesh=mesh,
        in_specs=placed,
        out_specs=(P(("vx", "vy"), "subj"), P("subj", None)),
        check_vma=False,
    )
```

```python
import jax
import jax.numpy as jnp
from jax import lax
from jax.experimental import pallas as pl
from jax.experimental.pallas import tpu as pltpu
from jax.sharding import PartitionSpec as P

MESH = pl.DeviceIdType.MESH
F32, BF16, I32 = jnp.float32, jnp.bfloat16, jnp.int32

w_side = 0.2741
w_mid = 0.4518

RX, RY, RZ = 4, 4, 8
PLANE = RX * RY
KD = 32
COLS = 256
HALF = 128
EX, EY = 4, 10
PLANES = EX * EY
STRATUM = 16


def split2(v):
    hi = v.astype(BF16)
    return hi, (v - hi.astype(F32)).astype(BF16)

HALO = [(dx, dy) for dx in (-1, 0, 1) for dy in (-1, 0, 1) if (dx, dy) != (0, 0)]
ORDER = (4, 3, 5, 2, 6, 1, 7, 0)
CHUNKS = 4
LAG_A2, LAG_B1, LAG_B2, LAG_B3 = 2, 4, 6, 8
PAIRS = RZ // 2
PARTS = 4
TILES = 8 // PARTS
ROWS = COLS // PARTS
ZR = 8
XR = KD - ZR
BANDS = PLANES * STRATUM // 128


def parity_sign(bits, shifts):
    for s in shifts:
        bits = bits ^ (bits >> s)
    return jnp.where((bits & 1) == 0, 1.0, -1.0)


def kernel(
    order_ref, vol_hbm, flip_ref, block_ref, offset_ref, sk_ref, gram_ref,
    vol, halo, ext, tables, mover, zs, xs, tt_hi, tt_lo,
    c, ra1, ra2, rb1, rb2, rz, rv, rw, other, gs, r1, r2, p3, out,
    ld_sem, h_send, h_recv, a_send, a_recv, z_send, z_recv, v_send, v_recv, g_send, g_recv,
):
    vx, vy, sj = lax.axis_index("vx"), lax.axis_index("vy"), lax.axis_index("subj")
    x, y = lax.rem(vx, RX), lax.div(vx, RX)

    def xy(dx, dy):
        return (lax.rem(y + dy + RY, RY) * RX + lax.rem(x + dx + RX, RX), vy, sj)

    def plane_dev(o):
        return (lax.rem(vx + o, PLANE), vy, sj)

    def z_dev(o):
        return (vx, lax.rem(vy + o, RZ), sj)

    def near(dx, dy):
        return (lax.rem(vx + dx + PLANE, PLANE), lax.rem(vy + dy + RZ, RZ), sj)

    partner = (vx, vy, 1 - sj)

    loads = []
    per = COLS * 2 // CHUNKS
    for i in range(CHUNKS):
        part = pl.ds(i * per, per)
        loads.append(pltpu.make_async_copy(vol_hbm.at[part], vol.at[part], ld_sem.at[i]))
        loads[-1].start()

    barrier = pltpu.get_barrier_semaphore()
    peers = [plane_dev(o) for o in range(1, PLANE)] + [z_dev(o) for o in range(1, RZ)] + [partner]
    peers += [near(dx, dy) for dx, dy in HALO if dx * dy != 0]
    for d in peers:
        pl.semaphore_signal(barrier, inc=1, device_id=d, device_id_type=MESH)

    for bx in range(2):
        for by in range(8):
            ext[bx + 1, by + 1] = (2 * flip_ref[bx, pl.ds(by, 1), :] - 1).astype(F32)

    row = lax.broadcasted_iota(I32, (128, 128), 0)
    col = lax.broadcasted_iota(I32, (128, 128), 1)
    dist = jnp.abs(row - col)
    band = jnp.where(dist == 0, w_mid, jnp.where(dist == 1, w_side, 0.0)).astype(F32)
    wcat = jnp.concatenate(split2(band), axis=1)
    hz = parity_sign(row & col, (4, 2, 1)).astype(BF16)
    hcat = jnp.concatenate([hz, hz], axis=1)

    def smooth_z(i, _):
        v = vol[pl.ds(i * 32, 32)].astype(F32).reshape(256, 128).astype(BF16)
        r = jnp.dot(v, wcat, preferred_element_type=F32)
        zs[pl.ds(i * 256, 256), :] = r[:, :128] + r[:, 128:]
        return 0

    for i in range(CHUNKS):
        loads[i].wait()
        lax.fori_loop(i * per // 32, (i + 1) * per // 32, smooth_z, 0)

    def remote(src, dst, ssem, rsem, dev):
        return pltpu.make_async_remote_copy(
            src_ref=src, dst_ref=dst, send_sem=ssem, recv_sem=rsem, device_id=dev, device_id_type=MESH
        )

    started = []

    def go(copy):
        copy.start()
        started.append(copy)
        return copy

    pl.semaphore_wait(barrier, len(peers))
    signs = [
        go(remote(flip_ref, halo.at[i], h_send.at[i], h_recv.at[i], near(dx, dy)))
        for i, (dx, dy) in enumerate(HALO)
    ]

    zero = jnp.zeros((COLS, 128), F32)
    for ex in range(EX):
        for yi in (0, 1, 10, 11):
            xs[ex, yi] = zero
    for yi in range(8):
        a = zs[pl.ds(yi, COLS, stride=16), :]
        b = zs[pl.ds(8 + yi, COLS, stride=16), :]
        xs[0, yi + 2] = w_side * a
        xs[1, yi + 2] = w_mid * a + w_side * b
        xs[2, yi + 2] = w_side * a + w_mid * b
        xs[3, yi + 2] = w_side * b

    def plane(ex, yi):
        f = w_side * (xs[ex, yi] + xs[ex, yi + 2]) + w_mid * xs[ex, yi + 1]
        f = f * ext[ex, yi]
        fcat = jnp.concatenate(split2(f), axis=1)
        t = lax.dot_general(hcat, fcat, (((1,), (1,)), ((), ())), preferred_element_type=F32)
        thi, tlo = split2(t)
        at = pl.ds(pl.multiple_of((ex * EY + yi) * STRATUM, STRATUM), STRATUM)
        for g in range(RZ):
            tt_hi[g, at, :] = thi[g * STRATUM : (g + 1) * STRATUM, :]
            tt_lo[g, at, :] = tlo[g * STRATUM : (g + 1) * STRATUM, :]

    def own_planes(i, _):
        plane(1, i + 1)
        plane(2, i + 1)
        return 0

    lax.fori_loop(0, 8, own_planes, 0)

    code_t = (block_ref[...] * 16 + offset_ref[...]).astype(F32).T.astype(I32)
    lane = lax.broadcasted_iota(I32, (1, 128), 1)
    gx = vx * 2 + lane // EY - 1 + 32
    gy = vy * 8 + lane % EY - 1 + 64
    voxel = (((gx >> 1) & 15) * 8 + ((gy >> 3) & 7)) * 16 + (gx & 1) * 8 + (gy & 7)
    off_lane = lane & 15
    ej = lax.broadcasted_iota(I32, (128, PLANES * STRATUM), 0)
    ek = lax.broadcasted_iota(I32, (128, PLANES * STRATUM), 1)
    spread = jnp.where((ek >> 4) == ej, 1.0, 0.0).astype(BF16)
    place = lax.broadcasted_iota(I32, (PLANE * KD, 128), 0) // KD
    for g in range(RZ):
        code = jnp.concatenate(
            [
                jnp.broadcast_to(
                    code_t[(g % 4) * KD : (g % 4 + 1) * KD, 2 * p + g // 4 : 2 * p + g // 4 + 1], (KD, 128)
                )
                for p in range(PLANE)
            ],
            axis=0,
        )
        sgn = parity_sign(((code & -16) + place) & voxel, (8, 4, 2, 1)).astype(BF16)
        wide = jnp.dot(sgn, spread, preferred_element_type=F32)
        pick = (code & 15) == off_lane
        for k in range(BANDS):
            at = slice(k * 128, (k + 1) * 128)
            tables[g, :, at] = jnp.where(pick, wide[:, at], 0.0).astype(BF16)

    lanes = lax.broadcasted_iota(I32, (64, 512), 1)
    rows = lax.broadcasted_iota(I32, (64, 512), 0)
    for s in range(8):
        mover[64 * s : 64 * s + 64, :] = jnp.where(lanes == order_ref[s] * 64 + rows, 1.0, 0.0).astype(BF16)

    okx = {-1: jnp.where(vx > 0, 1, 0), 0: 1, 1: jnp.where(vx < PLANE - 1, 1, 0)}
    oky = {-1: jnp.where(vy > 0, 1, 0), 0: 1, 1: jnp.where(vy < RZ - 1, 1, 0)}
    for copy in signs:
        copy.wait_recv()
    for i, (dx, dy) in enumerate(HALO):
        ok = (okx[-dx] * oky[-dy]).astype(F32)
        xpos = {-1: [(0, 1)], 0: [(1, 0), (2, 1)], 1: [(3, 0)]}[-dx]
        ypos = {-1: [(0, 7)], 0: [(k + 1, k) for k in range(8)], 1: [(9, 0)]}[-dy]
        for ex, bx in xpos:
            for ey, by in ypos:
                ext[ex, ey] = (2 * halo[i, bx, pl.ds(by, 1), :] - 1).astype(F32) * ok

    def x_planes(i, _):
        plane(0, i)
        plane(3, i)
        return 0

    def y_planes(i, _):
        plane(1, i * 9)
        plane(2, i * 9)
        return 0

    lax.fori_loop(0, EY, x_planes, 0)
    lax.fori_loop(0, 2, y_planes, 0)

    def contribute(t):
        g = lax.rem(vy + ORDER[t], RZ)
        r = jnp.dot(tables[g], tt_hi[g], preferred_element_type=F32)
        r = (r + jnp.dot(tables[g], tt_lo[g], preferred_element_type=F32)) * (1.0 / 512.0)
        for p in range(PLANE):
            dy, dx = lax.rem(p // RX - y + RY, RY), lax.rem(p % RX - x + RX, RX)
            c[t, dy, dx] = r[p * KD : (p + 1) * KD]

    lanes_of = [pl.ds(0, HALF), pl.ds(HALF, HALF)]
    X, ZF = pl.ds(ZR, XR), pl.ds(0, ZR)
    A1, A2, B1, B2, ZC, ZV, ZW = {}, {}, {}, {}, {}, {}, {}
    WAYS = ((1, 1), (-1, 3))

    def sems(u, h, k):
        return a_send.at[u, h, k], a_recv.at[u, h, k]

    def first(h, way):
        return xy(way, 0) if h == 0 else xy(0, way)

    def second(h, way):
        return xy(0, way) if h == 0 else xy(way, 0)

    def block(h, U, near_axis, other_axis):
        return (U, other_axis, near_axis) if h == 0 else (U, near_axis, other_axis)

    def start_a1(u):
        U = pl.ds(2 * u, 2)
        for h in range(2):
            for k in range(2):
                src = c.at[(*block(h, U, 2, pl.ds(2 * k, 2)), X, lanes_of[h])]
                A1[u, h, k] = go(remote(src, ra1.at[u, h, k], *sems(u, h, k), first(h, WAYS[k][0])))

    def do_a2(u):
        U = pl.ds(2 * u, 2)
        for h in range(2):
            for k in range(2):
                way, near_pos = WAYS[k]
                A1[u, h, k].wait_recv()
                at = (*block(h, U, near_pos, pl.ds(2 * k, 2)), X, lanes_of[h])
                c[at] = c[at] + ra1[u, h, k]
                src = c.at[(*block(h, U, near_pos, pl.ds(0, 4)), X, lanes_of[h])]
                A2[u, h, k] = go(remote(src, ra2.at[u, h, k], *sems(u, h, 2 + k), first(h, way)))

    def far(u, k):
        rows = (16, XR - 16)[(k + u) % 2]
        return pl.ds(ZR if k == 0 else ZR + XR - rows, rows), pl.ds(0, rows)

    def do_b1(u):
        U = pl.ds(2 * u, 2)
        for h in range(2):
            A2[u, h, 0].wait_recv()
            A2[u, h, 1].wait_recv()
            at = (*block(h, U, 0, pl.ds(0, 4)), X, lanes_of[h])
            c[at] = c[at] + ra2[u, h, 0] + ra2[u, h, 1]
            for k in range(2):
                part, room = far(u, k)
                src = c.at[(*block(h, U, 0, 2), part, lanes_of[h])]
                B1[u, h, k] = go(remote(src, rb1.at[u, h, k, :, room], *sems(u, h, 4 + k), second(h, WAYS[k][0])))

    def do_b2(u):
        U = pl.ds(2 * u, 2)
        for h in range(2):
            for k in range(2):
                way, near_pos = WAYS[k]
                B1[u, h, k].wait_recv()
                part, room = far(u, k)
                at = (*block(h, U, 0, near_pos), part, lanes_of[h])
                c[at] = c[at] + rb1[u, h, k, :, room]
                src = c.at[(*block(h, U, 0, near_pos), X, lanes_of[h])]
                B2[u, h, k] = go(remote(src, rb2.at[u, h, k], *sems(u, h, 6 + k), second(h, way)))

    def do_b3(u):
        U = pl.ds(2 * u, 2)
        for h in range(2):
            B2[u, h, 0].wait_recv()
            B2[u, h, 1].wait_recv()
            at = (U, 0, 0, X, lanes_of[h])
            c[at] = c[at] + rb2[u, h, 0] + rb2[u, h, 1]
        for t in (2 * u, 2 * u + 1):
            o = ORDER[t]
            if o:
                ZC[o] = go(remote(c.at[t, 0, 0, X], rz.at[o - 1], z_send.at[o - 1], z_recv.at[o - 1], z_dev(o)))

    def ring(n):
        for b in range(2):
            for k in range(2):
                to = ORDER.index(5 - n if k == 0 else 3 + n)
                if n == 1:
                    own = pl.ds(2 * k + b, 1)
                    src, dst = c.at[to, own, :, ZF], rv.at[0, b, k, pl.ds(0, 1)]
                else:
                    at = b ^ k ^ 1 if n == 2 else b
                    own = pl.ds(2 * at, 2)
                    if n == 2 and b == 1:
                        for i in range(2):
                            ZV[1, i, k].wait_recv()
                            c[to, 2 * k + i, :, ZF] = c[to, 2 * k + i, :, ZF] + rv[0, i, k, 0]
                    elif n > 2:
                        ZV[n - 1, b, k].wait_recv()
                        c[to, own, :, ZF] = c[to, own, :, ZF] + rv[n - 2, b, k]
                    src, dst = c.at[to, own, :, ZF], rv.at[n - 1, at, k]
                piece = at if n == 2 else b
                dev = z_dev(1 if k == 0 else RZ - 1)
                i = 4 * (n - 1) + 2 * piece + k
                ZV[n, piece, k] = go(remote(src, dst, v_send.at[0, i], v_recv.at[0, i], dev))

    def spread_plane():
        t = ORDER.index(0)
        for b in range(2):
            ZV[4, b, 0].wait_recv()
            ZV[4, b, 1].wait_recv()
            own = pl.ds(2 * b, 2)
            c[t, own, :, ZF] = c[t, own, :, ZF] + rv[3, b, 0] + rv[3, b, 1]
        for o in range(1, PLANE):
            dy, dx = o // RX, o % RX
            ZW[o] = go(remote(c.at[t, dy, dx, ZF], rw.at[o - 1], v_send.at[1, o], v_recv.at[1, o], xy(dx, dy)))

    stages = ((LAG_A2, do_a2), (LAG_B1, do_b1), (LAG_B2, do_b2), (LAG_B3, do_b3))
    ring_at = {1: 0, 2: 2, 3: 4, 4: 5}
    for step in range(PAIRS + LAG_B3):
        if step < PAIRS:
            contribute(2 * step)
            if step == 0:
                ring(1)
            contribute(2 * step + 1)
            start_a1(step)
        for n in (2, 3, 4):
            if ring_at[n] == step:
                ring(n)
        for lag, stage in stages:
            if 0 <= step - lag < PAIRS:
                stage(step - lag)
        if step == 6:
            spread_plane()

    low = c[RZ - 1, 0, 0, ZF]
    for o in range(1, PLANE):
        ZW[o].wait_recv()
        low = low + rw[o - 1]
    high = c[RZ - 1, 0, 0, X]
    for o in ORDER[:-1]:
        ZC[o].wait_recv()
        high = high + rz[o - 1]
    total = jnp.concatenate([low, high], axis=0)
    sk_ref[...] = total

    swap = go(remote(sk_ref, other, z_send.at[7], z_recv.at[7], partner))
    swap.wait_recv()
    theirs = other[...]
    first = jnp.where(sj == 0, 1.0, 0.0)
    left = total * first + theirs * (1.0 - first)
    right = theirs * first + total * (1.0 - first)
    parts = jnp.concatenate(split2(jnp.concatenate([left, right], axis=1)), axis=0)
    moved = jnp.dot(parts, mover[...], preferred_element_type=F32)
    mine = moved[:, :COLS] * first + moved[:, COLS:] * (1.0 - first)
    lhs = jnp.concatenate([mine[:KD], mine[:KD], mine[KD:]], axis=0).astype(BF16)
    rhs = jnp.concatenate([moved[:KD], moved[KD:], moved[:KD]], axis=0).astype(BF16)
    around = [(dy, dx) for dy in range(RY) for dx in range(RX) if dy or dx]
    around.sort(key=lambda d: -min(d[0], RY - d[0]) - min(d[1], RX - d[1]))
    owner = [lax.rem(y + dy, RY) * RX + lax.rem(x + dx, RX) for dy, dx in around]
    far_z = (4, 3, 5, 2, 6, 1, 7)
    G1, G2, G3 = {}, {}, {}

    def gsems(n, q, i):
        return g_send.at[n, q, i], g_recv.at[n, q, i]

    for q in range(PARTS):
        part = lax.dot_general(
            lhs[:, q * ROWS : (q + 1) * ROWS], rhs, (((0,), (0,)), ((), ())), preferred_element_type=F32
        )
        for i in range(ROWS // 8):
            for j in range(4):
                gs[q, 4 * i + j] = part[8 * i : 8 * i + 8, 128 * j : 128 * j + 128]
        for i, (dy, dx) in enumerate(around):
            src = gs.at[q, pl.ds(owner[i] * TILES, TILES)]
            G1[q, i] = go(remote(src, r1.at[q, i], *gsems(0, q, i), xy(dx, dy)))
    for q in range(PARTS):
        acc = gs[q, pl.ds(vx * TILES, TILES)]
        for i in range(PLANE - 1):
            G1[q, i].wait_recv()
            acc = acc + r1[q, i]
        r2[q, vy] = acc
        for i, o in enumerate(far_z):
            G2[q, i] = go(remote(r2.at[q, vy], r2.at[q, vy], *gsems(1, q, i), z_dev(o)))
    for q in range(PARTS):
        for i in range(RZ - 1):
            G2[q, i].wait_recv()
        acc = r2[q, 0]
        for i in range(1, RZ):
            acc = acc + r2[q, i]
        mine_at = pl.ds(vx * TILES, TILES)
        p3[q] = acc * (1.0 / 4096.0)
        for i, (dy, dx) in enumerate(around):
            G3[q, i] = go(remote(p3.at[q], out.at[q, mine_at], *gsems(2, q, i), xy(dx, dy)))
        out[q, mine_at] = p3[q]
    for q in range(PARTS):
        for i in range(PLANE - 1):
            G3[q, i].wait_recv()
        for i in range(ROWS // 8):
            for j in range(4):
                gram_ref[q * ROWS + 8 * i : q * ROWS + 8 * i + 8, 128 * j : 128 * j + 128] = out[q, 4 * i + j]
    for copy in started:
        copy.wait_send()


def sketch_and_gram(order, vol, flip, block, offset):
    V = pltpu.VMEM
    dma = pltpu.SemaphoreType.DMA
    return pl.pallas_call(
        kernel,
        out_shape=(
            jax.ShapeDtypeStruct((KD, COLS), F32),
            jax.ShapeDtypeStruct((COLS, 2 * COLS), F32),
        ),
        in_specs=[
            pl.BlockSpec(memory_space=pltpu.SMEM),
            pl.BlockSpec(memory_space=pl.ANY),
            pl.BlockSpec(memory_space=V),
            pl.BlockSpec(memory_space=V),
            pl.BlockSpec(memory_space=V),
        ],
        out_specs=(pl.BlockSpec(memory_space=V), pl.BlockSpec(memory_space=V)),
        scratch_shapes=[
            V((COLS * 2, 8, 128), BF16),
            V((8, 2, 8, 128), I32),
            V((EX, EY, 1, 128), F32),
            V((RZ, PLANE * KD, PLANES * STRATUM), BF16),
            V((512, 512), BF16),
            V((COLS * 16, 128), F32),
            V((EX, EY + 2, COLS, 128), F32),
            V((RZ, PLANES * STRATUM, COLS), BF16),
            V((RZ, PLANES * STRATUM, COLS), BF16),
            V((RZ, RY, RX, KD, COLS), F32),
            V((PAIRS, 2, 2, 2, 2, XR, HALF), F32),
            V((PAIRS, 2, 2, 2, 4, XR, HALF), F32),
            V((PAIRS, 2, 2, 2, 16, HALF), F32),
            V((PAIRS, 2, 2, 2, XR, HALF), F32),
            V((RZ - 1, XR, COLS), F32),
            V((4, 2, 2, 2, RX, ZR, COLS), F32),
            V((PLANE - 1, ZR, COLS), F32),
            V((KD, COLS), F32),
            V((PARTS, PLANE * TILES, 8, 128), F32),
            V((PARTS, PLANE - 1, TILES, 8, 128), F32),
            V((PARTS, RZ, TILES, 8, 128), F32),
            V((PARTS, TILES, 8, 128), F32),
            V((PARTS, PLANE * TILES, 8, 128), F32),
            dma((CHUNKS,)),
            dma((8,)),
            dma((8,)),
            dma((PAIRS, 2, 8)),
            dma((PAIRS, 2, 8)),
            dma((8,)),
            dma((8,)),
            dma((2, 16)),
            dma((2, 16)),
            dma((3, PARTS, 16)),
            dma((3, PARTS, 16)),
        ],
        compiler_params=pltpu.CompilerParams(
            collective_id=0, has_side_effects=True, vmem_limit_bytes=60 * 1024 * 1024
        ),
        name="sketch_and_gram",
    )(order, vol, flip, block, offset)


def on_device(volumes, flip_bits, hadamard_block, stratum_offset, subject_order):
    return sketch_and_gram(
        subject_order,
        volumes.reshape(COLS * 2, 8, 128),
        flip_bits,
        hadamard_block.reshape(32, 128),
        stratum_offset.reshape(32, 128),
    )


def solution(mesh):
    placed = (P("subj", None, "vx", "vy", None), P("vx", "vy", None), P(), P(), P())
    return jax.shard_map(
        on_device,
        mesh=mesh,
        in_specs=placed,
        out_specs=(P(("vx", "vy"), "subj"), P("subj", None)),
        check_vma=False,
    )
```

```python
import jax
import jax.numpy as jnp
from jax import lax
from jax.experimental import pallas as pl
from jax.experimental.pallas import tpu as pltpu
from jax.sharding import PartitionSpec as P

MESH = pl.DeviceIdType.MESH
F32, BF16, I32 = jnp.float32, jnp.bfloat16, jnp.int32

w_side = 0.2741
w_mid = 0.4518

RX, RY, RZ = 4, 4, 8
PLANE = RX * RY
KD = 32
COLS = 256
HALF = 128
EX, EY = 4, 10
PLANES = EX * EY
STRATUM = 16


def split2(v):
    hi = v.astype(BF16)
    return hi, (v - hi.astype(F32)).astype(BF16)

HALO = [(dx, dy) for dx in (-1, 0, 1) for dy in (-1, 0, 1) if (dx, dy) != (0, 0)]
ORDER = (4, 3, 5, 2, 6, 1, 7, 0)
CHUNKS = 4
LAG_A2, LAG_B1, LAG_B2, LAG_B3 = 2, 4, 6, 8
PAIRS = RZ // 2
PARTS = 4
TILES = 8 // PARTS
ROWS = COLS // PARTS
ZR = 8
XR = KD - ZR
BANDS = PLANES * STRATUM // 128


def parity_sign(bits, shifts):
    for s in shifts:
        bits = bits ^ (bits >> s)
    return jnp.where((bits & 1) == 0, 1.0, -1.0)


def kernel(
    order_hbm, vol_hbm, flip_hbm, block_hbm, offset_hbm, sk_ref, gram_ref,
    order_ref, flip_ref, block_ref, offset_ref, vol, halo, ext, tables, mover, zs, xs, tt_hi, tt_lo,
    c, ra1, ra2, rb1, rb2, rz, rv, rw, other, gs, r1, r2, p3, out,
    ld_sem, sends, a_recv, v_recv, g_recv, recvs,
):
    vx, vy, sj = lax.axis_index("vx"), lax.axis_index("vy"), lax.axis_index("subj")
    x, y = lax.rem(vx, RX), lax.div(vx, RX)

    def xy(dx, dy):
        return (lax.rem(y + dy + RY, RY) * RX + lax.rem(x + dx + RX, RX), vy, sj)

    def plane_dev(o):
        return (lax.rem(vx + o, PLANE), vy, sj)

    def z_dev(o):
        return (vx, lax.rem(vy + o, RZ), sj)

    def near(dx, dy):
        return (lax.rem(vx + dx + PLANE, PLANE), lax.rem(vy + dy + RZ, RZ), sj)

    partner = (vx, vy, 1 - sj)

    small = [
        pltpu.make_async_copy(src, dst, ld_sem.at[CHUNKS + i])
        for i, (src, dst) in enumerate(
            ((flip_hbm, flip_ref), (block_hbm, block_ref), (offset_hbm, offset_ref), (order_hbm, order_ref))
        )
    ]
    small[0].start()
    loads = []
    per = COLS * 2 // CHUNKS
    for i in range(CHUNKS):
        part = pl.ds(i * per, per)
        loads.append(pltpu.make_async_copy(vol_hbm.at[part], vol.at[part], ld_sem.at[i]))
        loads[-1].start()
    for copy in small[1:]:
        copy.start()

    barrier = pltpu.get_barrier_semaphore()
    peers = [plane_dev(o) for o in range(1, PLANE)] + [z_dev(o) for o in range(1, RZ)] + [partner]
    peers += [near(dx, dy) for dx, dy in HALO if dx * dy != 0]
    for d in peers:
        pl.semaphore_signal(barrier, inc=1, device_id=d, device_id_type=MESH)

    small[0].wait()
    for bx in range(2):
        for by in range(8):
            ext[bx + 1, by + 1] = (2 * flip_ref[bx, pl.ds(by, 1), :] - 1).astype(F32)

    row = lax.broadcasted_iota(I32, (128, 128), 0)
    col = lax.broadcasted_iota(I32, (128, 128), 1)
    dist = jnp.abs(row - col)
    band = jnp.where(dist == 0, w_mid, jnp.where(dist == 1, w_side, 0.0)).astype(F32)
    wcat = jnp.concatenate(split2(band), axis=1)
    hz = parity_sign(row & col, (4, 2, 1)).astype(BF16)
    hcat = jnp.concatenate([hz, hz], axis=1)

    def smooth_z(i, _):
        v = vol[pl.ds(i * 32, 32)].astype(F32).reshape(256, 128).astype(BF16)
        r = jnp.dot(v, wcat, preferred_element_type=F32)
        zs[pl.ds(i * 256, 256), :] = r[:, :128] + r[:, 128:]
        return 0

    for i in range(CHUNKS):
        loads[i].wait()
        lax.fori_loop(i * per // 32, (i + 1) * per // 32, smooth_z, 0)

    def remote(src, dst, ssem, rsem, dev):
        return pltpu.make_async_remote_copy(
            src_ref=src, dst_ref=dst, send_sem=ssem, recv_sem=rsem, device_id=dev, device_id_type=MESH
        )

    def go(src, dst, kind, rsem, dev):
        remote(src, dst, sends.at[kind], rsem, dev).start()

    def arrive(whole, rsem):
        remote(whole, whole, sends.at[0], rsem, partner).wait_recv()

    def sent(whole, kind):
        remote(whole, whole, sends.at[kind], recvs.at[0], partner).wait_send()

    pl.semaphore_wait(barrier, len(peers))
    for i, (dx, dy) in enumerate(HALO):
        go(flip_ref, halo.at[i], 0, recvs.at[0], near(dx, dy))

    zero = jnp.zeros((COLS, 128), F32)
    for ex in range(EX):
        for yi in (0, 1, 10, 11):
            xs[ex, yi] = zero
    for yi in range(8):
        a = zs[pl.ds(yi, COLS, stride=16), :]
        b = zs[pl.ds(8 + yi, COLS, stride=16), :]
        xs[0, yi + 2] = w_side * a
        xs[1, yi + 2] = w_mid * a + w_side * b
        xs[2, yi + 2] = w_side * a + w_mid * b
        xs[3, yi + 2] = w_side * b

    def plane(ex, yi):
        f = w_side * (xs[ex, yi] + xs[ex, yi + 2]) + w_mid * xs[ex, yi + 1]
        f = f * ext[ex, yi]
        fcat = jnp.concatenate(split2(f), axis=1)
        t = lax.dot_general(hcat, fcat, (((1,), (1,)), ((), ())), preferred_element_type=F32)
        thi, tlo = split2(t)
        at = pl.ds(pl.multiple_of((ex * EY + yi) * STRATUM, STRATUM), STRATUM)
        for g in range(RZ):
            tt_hi[g, at, :] = thi[g * STRATUM : (g + 1) * STRATUM, :]
            tt_lo[g, at, :] = tlo[g * STRATUM : (g + 1) * STRATUM, :]

    def own_planes(i, _):
        plane(1, i + 1)
        plane(2, i + 1)
        return 0

    lax.fori_loop(0, 8, own_planes, 0)

    for copy in small[1:]:
        copy.wait()
    code_t = (block_ref[...] * 16 + offset_ref[...]).astype(F32).T.astype(I32)
    lane = lax.broadcasted_iota(I32, (1, 128), 1)
    gx = vx * 2 + lane // EY - 1 + 32
    gy = vy * 8 + lane % EY - 1 + 64
    voxel = (((gx >> 1) & 15) * 8 + ((gy >> 3) & 7)) * 16 + (gx & 1) * 8 + (gy & 7)
    off_lane = lane & 15
    ej = lax.broadcasted_iota(I32, (128, PLANES * STRATUM), 0)
    ek = lax.broadcasted_iota(I32, (128, PLANES * STRATUM), 1)
    spread = jnp.where((ek >> 4) == ej, 1.0, 0.0).astype(BF16)
    place = lax.broadcasted_iota(I32, (PLANE * KD, 128), 0) // KD
    for g in range(RZ):
        code = jnp.concatenate(
            [
                jnp.broadcast_to(
                    code_t[(g % 4) * KD : (g % 4 + 1) * KD, 2 * p + g // 4 : 2 * p + g // 4 + 1], (KD, 128)
                )
                for p in range(PLANE)
            ],
            axis=0,
        )
        sgn = parity_sign(((code & -16) + place) & voxel, (8, 4, 2, 1)).astype(BF16)
        wide = jnp.dot(sgn, spread, preferred_element_type=F32)
        pick = (code & 15) == off_lane
        for k in range(BANDS):
            at = slice(k * 128, (k + 1) * 128)
            tables[g, :, at] = jnp.where(pick, wide[:, at], 0.0).astype(BF16)

    lanes = lax.broadcasted_iota(I32, (64, 512), 1)
    rows = lax.broadcasted_iota(I32, (64, 512), 0)
    for s in range(8):
        mover[64 * s : 64 * s + 64, :] = jnp.where(lanes == order_ref[s] * 64 + rows, 1.0, 0.0).astype(BF16)

    okx = {-1: jnp.where(vx > 0, 1, 0), 0: 1, 1: jnp.where(vx < PLANE - 1, 1, 0)}
    oky = {-1: jnp.where(vy > 0, 1, 0), 0: 1, 1: jnp.where(vy < RZ - 1, 1, 0)}
    arrive(halo, recvs.at[0])
    for i, (dx, dy) in enumerate(HALO):
        ok = (okx[-dx] * oky[-dy]).astype(F32)
        xpos = {-1: [(0, 1)], 0: [(1, 0), (2, 1)], 1: [(3, 0)]}[-dx]
        ypos = {-1: [(0, 7)], 0: [(k + 1, k) for k in range(8)], 1: [(9, 0)]}[-dy]
        for ex, bx in xpos:
            for ey, by in ypos:
                ext[ex, ey] = (2 * halo[i, bx, pl.ds(by, 1), :] - 1).astype(F32) * ok

    def x_planes(i, _):
        plane(0, i)
        plane(3, i)
        return 0

    def y_planes(i, _):
        plane(1, i * 9)
        plane(2, i * 9)
        return 0

    lax.fori_loop(0, EY, x_planes, 0)
    lax.fori_loop(0, 2, y_planes, 0)

    def contribute(t):
        g = lax.rem(vy + ORDER[t], RZ)
        r = jnp.dot(tables[g], tt_hi[g], preferred_element_type=F32)
        r = (r + jnp.dot(tables[g], tt_lo[g], preferred_element_type=F32)) * (1.0 / 512.0)
        for p in range(PLANE):
            dy, dx = lax.rem(p // RX - y + RY, RY), lax.rem(p % RX - x + RX, RX)
            c[t, dy, dx] = r[p * KD : (p + 1) * KD]

    lanes_of = [pl.ds(0, HALF), pl.ds(HALF, HALF)]
    X, ZF = pl.ds(ZR, XR), pl.ds(0, ZR)
    WAYS = ((1, 1), (-1, 3))

    def first(h, way):
        return xy(way, 0) if h == 0 else xy(0, way)

    def second(h, way):
        return xy(0, way) if h == 0 else xy(way, 0)

    def block(h, U, near_axis, other_axis):
        return (U, other_axis, near_axis) if h == 0 else (U, near_axis, other_axis)

    def start_a1(u):
        U = pl.ds(2 * u, 2)
        for h in range(2):
            for k in range(2):
                src = c.at[(*block(h, U, 2, pl.ds(2 * k, 2)), X, lanes_of[h])]
                go(src, ra1.at[u, h, k], 1, a_recv.at[0, u], first(h, WAYS[k][0]))

    def do_a2(u):
        U = pl.ds(2 * u, 2)
        arrive(ra1.at[u], a_recv.at[0, u])
        for h in range(2):
            for k in range(2):
                way, near_pos = WAYS[k]
                at = (*block(h, U, near_pos, pl.ds(2 * k, 2)), X, lanes_of[h])
                c[at] = c[at] + ra1[u, h, k]
                src = c.at[(*block(h, U, near_pos, pl.ds(0, 4)), X, lanes_of[h])]
                go(src, ra2.at[u, h, k], 2, a_recv.at[1, u], first(h, way))

    def far(u, k):
        rows = (16, XR - 16)[(k + u) % 2]
        return pl.ds(ZR if k == 0 else ZR + XR - rows, rows), pl.ds(0, rows)

    def do_b1(u):
        U = pl.ds(2 * u, 2)
        arrive(ra2.at[u], a_recv.at[1, u])
        for h in range(2):
            at = (*block(h, U, 0, pl.ds(0, 4)), X, lanes_of[h])
            c[at] = c[at] + ra2[u, h, 0] + ra2[u, h, 1]
            for k in range(2):
                part, room = far(u, k)
                src = c.at[(*block(h, U, 0, 2), part, lanes_of[h])]
                go(src, rb1.at[u, h, k, :, room], 3, a_recv.at[2, u], second(h, WAYS[k][0]))

    def do_b2(u):
        U = pl.ds(2 * u, 2)
        arrive(rb2.at[u, :, 0], a_recv.at[2, u])
        for h in range(2):
            for k in range(2):
                way, near_pos = WAYS[k]
                part, room = far(u, k)
                at = (*block(h, U, 0, near_pos), part, lanes_of[h])
                c[at] = c[at] + rb1[u, h, k, :, room]
                src = c.at[(*block(h, U, 0, near_pos), X, lanes_of[h])]
                go(src, rb2.at[u, h, k], 4, a_recv.at[3, u], second(h, way))

    def do_b3(u):
        U = pl.ds(2 * u, 2)
        arrive(rb2.at[u], a_recv.at[3, u])
        for h in range(2):
            at = (U, 0, 0, X, lanes_of[h])
            c[at] = c[at] + rb2[u, h, 0] + rb2[u, h, 1]
        for t in (2 * u, 2 * u + 1):
            o = ORDER[t]
            if o:
                go(c.at[t, 0, 0, X], rz.at[o - 1], 5, recvs.at[1], z_dev(o))

    def ring(n):
        for b in range(2):
            for k in range(2):
                to = ORDER.index(5 - n if k == 0 else 3 + n)
                if n == 1:
                    own = pl.ds(2 * k + b, 1)
                    src, dst = c.at[to, own, :, ZF], rv.at[0, b, k, pl.ds(0, 1)]
                else:
                    at = b ^ k ^ 1 if n == 2 else b
                    own = pl.ds(2 * at, 2)
                    if n == 2 and b == 1:
                        arrive(rv.at[0, :, k, 0], v_recv.at[0, 0, k])
                        for i in range(2):
                            c[to, 2 * k + i, :, ZF] = c[to, 2 * k + i, :, ZF] + rv[0, i, k, 0]
                    elif n > 2:
                        arrive(rv.at[n - 2, b, k], v_recv.at[n - 2, b, k])
                        c[to, own, :, ZF] = c[to, own, :, ZF] + rv[n - 2, b, k]
                    src, dst = c.at[to, own, :, ZF], rv.at[n - 1, at, k]
                piece = at if n == 2 else b
                dev = z_dev(1 if k == 0 else RZ - 1)
                go(src, dst, 6 if n == 1 else 7, v_recv.at[n - 1, 0 if n == 1 else piece, k], dev)

    def spread_plane():
        t = ORDER.index(0)
        for b in range(2):
            arrive(rv.at[3, b, 0], v_recv.at[3, b, 0])
            arrive(rv.at[3, b, 1], v_recv.at[3, b, 1])
            own = pl.ds(2 * b, 2)
            c[t, own, :, ZF] = c[t, own, :, ZF] + rv[3, b, 0] + rv[3, b, 1]
        for o in range(1, PLANE):
            dy, dx = o // RX, o % RX
            go(c.at[t, dy, dx, ZF], rw.at[o - 1], 8, recvs.at[2], xy(dx, dy))

    stages = ((LAG_A2, do_a2), (LAG_B1, do_b1), (LAG_B2, do_b2), (LAG_B3, do_b3))
    ring_at = {1: 0, 2: 2, 3: 4, 4: 5}
    for step in range(PAIRS + LAG_B3):
        if step < PAIRS:
            contribute(2 * step)
            if step == 0:
                ring(1)
            contribute(2 * step + 1)
            start_a1(step)
        for n in (2, 3, 4):
            if ring_at[n] == step:
                ring(n)
        for lag, stage in stages:
            if 0 <= step - lag < PAIRS:
                stage(step - lag)
        if step == 6:
            spread_plane()

    low = c[RZ - 1, 0, 0, ZF]
    arrive(rw, recvs.at[2])
    for o in range(1, PLANE):
        low = low + rw[o - 1]
    high = c[RZ - 1, 0, 0, X]
    arrive(rz, recvs.at[1])
    for o in ORDER[:-1]:
        high = high + rz[o - 1]
    total = jnp.concatenate([low, high], axis=0)
    sk_ref[...] = total

    go(sk_ref, other, 9, recvs.at[3], partner)
    arrive(other, recvs.at[3])
    theirs = other[...]
    first = jnp.where(sj == 0, 1.0, 0.0)
    left = total * first + theirs * (1.0 - first)
    right = theirs * first + total * (1.0 - first)
    parts = jnp.concatenate(split2(jnp.concatenate([left, right], axis=1)), axis=0)
    moved = jnp.dot(parts, mover[...], preferred_element_type=F32)
    mine = moved[:, :COLS] * first + moved[:, COLS:] * (1.0 - first)
    lhs = jnp.concatenate([mine[:KD], mine[:KD], mine[KD:]], axis=0).astype(BF16)
    rhs = jnp.concatenate([moved[:KD], moved[KD:], moved[:KD]], axis=0).astype(BF16)
    around = [(dy, dx) for dy in range(RY) for dx in range(RX) if dy or dx]
    around.sort(key=lambda d: -min(d[0], RY - d[0]) - min(d[1], RX - d[1]))
    owner = [lax.rem(y + dy, RY) * RX + lax.rem(x + dx, RX) for dy, dx in around]
    far_z = (4, 3, 5, 2, 6, 1, 7)

    for q in range(PARTS):
        part = lax.dot_general(
            lhs[:, q * ROWS : (q + 1) * ROWS], rhs, (((0,), (0,)), ((), ())), preferred_element_type=F32
        )
        for i in range(ROWS // 8):
            for j in range(4):
                gs[q, 4 * i + j] = part[8 * i : 8 * i + 8, 128 * j : 128 * j + 128]
        for i, (dy, dx) in enumerate(around):
            src = gs.at[q, pl.ds(owner[i] * TILES, TILES)]
            go(src, r1.at[q, i], 10, g_recv.at[0, q], xy(dx, dy))
    for q in range(PARTS):
        acc = gs[q, pl.ds(vx * TILES, TILES)]
        arrive(r1.at[q], g_recv.at[0, q])
        for i in range(PLANE - 1):
            acc = acc + r1[q, i]
        r2[q, vy] = acc
        for o in far_z:
            go(r2.at[q, vy], r2.at[q, vy], 11, g_recv.at[1, q], z_dev(o))
    for q in range(PARTS):
        arrive(r2.at[q, pl.ds(0, RZ - 1)], g_recv.at[1, q])
        acc = r2[q, 0]
        for i in range(1, RZ):
            acc = acc + r2[q, i]
        mine_at = pl.ds(vx * TILES, TILES)
        p3[q] = acc * (1.0 / 4096.0)
        for dy, dx in around:
            go(p3.at[q], out.at[q, mine_at], 12, g_recv.at[2, q], xy(dx, dy))
        out[q, mine_at] = p3[q]
    for q in range(PARTS):
        arrive(r1.at[q], g_recv.at[2, q])
        for i in range(ROWS // 8):
            for j in range(4):
                gram_ref[q * ROWS + 8 * i : q * ROWS + 8 * i + 8, 128 * j : 128 * j + 128] = out[q, 4 * i + j]
    whole = (halo, ra1, ra2, rb2.at[:, :, 0], rb2, rz, rv.at[0, :, :, 0], rv.at[pl.ds(1, 3)], rw, other, r1)
    for kind, ref in enumerate((*whole, r2.at[:, pl.ds(0, RZ - 1)], r1)):
        sent(ref, kind)


def sketch_and_gram(order, vol, flip, block, offset):
    V = pltpu.VMEM
    dma = pltpu.SemaphoreType.DMA
    return pl.pallas_call(
        kernel,
        out_shape=(
            jax.ShapeDtypeStruct((KD, COLS), F32),
            jax.ShapeDtypeStruct((COLS, 2 * COLS), F32),
        ),
        in_specs=[pl.BlockSpec(memory_space=pl.ANY)] * 5,
        out_specs=(pl.BlockSpec(memory_space=V), pl.BlockSpec(memory_space=V)),
        scratch_shapes=[
            pltpu.SMEM((8,), I32),
            V((2, 8, 128), I32),
            V((32, 128), I32),
            V((32, 128), I32),
            V((COLS * 2, 8, 128), BF16),
            V((8, 2, 8, 128), I32),
            V((EX, EY, 1, 128), F32),
            V((RZ, PLANE * KD, PLANES * STRATUM), BF16),
            V((512, 512), BF16),
            V((COLS * 16, 128), F32),
            V((EX, EY + 2, COLS, 128), F32),
            V((RZ, PLANES * STRATUM, COLS), BF16),
            V((RZ, PLANES * STRATUM, COLS), BF16),
            V((RZ, RY, RX, KD, COLS), F32),
            V((PAIRS, 2, 2, 2, 2, XR, HALF), F32),
            V((PAIRS, 2, 2, 2, 4, XR, HALF), F32),
            V((PAIRS, 2, 2, 2, 16, HALF), F32),
            V((PAIRS, 2, 2, 2, XR, HALF), F32),
            V((RZ - 1, XR, COLS), F32),
            V((4, 2, 2, 2, RX, ZR, COLS), F32),
            V((PLANE - 1, ZR, COLS), F32),
            V((KD, COLS), F32),
            V((PARTS, PLANE * TILES, 8, 128), F32),
            V((PARTS, PLANE - 1, TILES, 8, 128), F32),
            V((PARTS, RZ, TILES, 8, 128), F32),
            V((PARTS, TILES, 8, 128), F32),
            V((PARTS, PLANE * TILES, 8, 128), F32),
            dma((CHUNKS + 4,)),
            dma((13,)),
            dma((4, PAIRS)),
            dma((4, 2, 2)),
            dma((3, PARTS)),
            dma((4,)),
        ],
        compiler_params=pltpu.CompilerParams(
            collective_id=0, has_side_effects=True, vmem_limit_bytes=60 * 1024 * 1024
        ),
        name="sketch_and_gram",
    )(order, vol, flip, block, offset)


def on_device(volumes, flip_bits, hadamard_block, stratum_offset, subject_order):
    return sketch_and_gram(
        subject_order,
        volumes.reshape(COLS * 2, 8, 128),
        flip_bits,
        hadamard_block.reshape(32, 128),
        stratum_offset.reshape(32, 128),
    )


def solution(mesh):
    placed = (P("subj", None, "vx", "vy", None), P("vx", "vy", None), P(), P(), P())
    return jax.shard_map(
        on_device,
        mesh=mesh,
        in_specs=placed,
        out_specs=(P(("vx", "vy"), "subj"), P("subj", None)),
        check_vma=False,
    )
```

```python
import jax
import jax.numpy as jnp
from jax import lax
from jax.experimental import pallas as pl
from jax.experimental.pallas import tpu as pltpu
from jax.sharding import PartitionSpec as P

MESH = pl.DeviceIdType.MESH
F32, BF16, I32 = jnp.float32, jnp.bfloat16, jnp.int32

w_side = 0.2741
w_mid = 0.4518

RX, RY, RZ = 4, 4, 8
PLANE = RX * RY
KD = 32
COLS = 256
HALF = 128
EX, EY = 4, 10
PLANES = EX * EY
STRATUM = 16


def split2(v):
    hi = v.astype(BF16)
    return hi, (v - hi.astype(F32)).astype(BF16)

HALO = [(dx, dy) for dx in (-1, 0, 1) for dy in (-1, 0, 1) if (dx, dy) != (0, 0)]
ORDER = (4, 3, 5, 2, 6, 1, 7, 0)
CHUNKS = 4
LAG_A2, LAG_B1, LAG_B2, LAG_B3 = 2, 4, 6, 8
PAIRS = RZ // 2
PARTS = 4
TILES = 8 // PARTS
ROWS = COLS // PARTS
ZR = 8
XR = KD - ZR
BANDS = PLANES * STRATUM // 128


def parity_sign(bits, shifts):
    for s in shifts:
        bits = bits ^ (bits >> s)
    return jnp.where((bits & 1) == 0, 1.0, -1.0)


def kernel(
    order_hbm, vol_hbm, flip_hbm, block_hbm, offset_hbm, sk_ref, gram_ref,
    order_ref, flip_ref, block_ref, offset_ref, vol, halo, ext, tables, mover, zs, xs, tt_hi, tt_lo,
    c, ra1, ra2, rb1, rb2, rz, rv, rw, packed, other, gs, r1, r2, p3, out,
    ld_sem, sends, a_recv, v_recv, g_recv, recvs,
):
    vx, vy, sj = lax.axis_index("vx"), lax.axis_index("vy"), lax.axis_index("subj")
    x, y = lax.rem(vx, RX), lax.div(vx, RX)

    def xy(dx, dy):
        return (lax.rem(y + dy + RY, RY) * RX + lax.rem(x + dx + RX, RX), vy, sj)

    def plane_dev(o):
        return (lax.rem(vx + o, PLANE), vy, sj)

    def z_dev(o):
        return (vx, lax.rem(vy + o, RZ), sj)

    def near(dx, dy):
        return (lax.rem(vx + dx + PLANE, PLANE), lax.rem(vy + dy + RZ, RZ), sj)

    partner = (vx, vy, 1 - sj)

    small = [
        pltpu.make_async_copy(src, dst, ld_sem.at[CHUNKS + i])
        for i, (src, dst) in enumerate(
            ((flip_hbm, flip_ref), (block_hbm, block_ref), (offset_hbm, offset_ref), (order_hbm, order_ref))
        )
    ]
    small[0].start()
    loads = []
    per = COLS * 2 // CHUNKS
    for i in range(CHUNKS):
        part = pl.ds(i * per, per)
        loads.append(pltpu.make_async_copy(vol_hbm.at[part], vol.at[part], ld_sem.at[i]))
        loads[-1].start()
    for copy in small[1:]:
        copy.start()

    barrier = pltpu.get_barrier_semaphore()
    peers = [plane_dev(o) for o in range(1, PLANE)] + [z_dev(o) for o in range(1, RZ)] + [partner]
    peers += [near(dx, dy) for dx, dy in HALO if dx * dy != 0]
    for d in peers:
        pl.semaphore_signal(barrier, inc=1, device_id=d, device_id_type=MESH)

    small[0].wait()
    for bx in range(2):
        for by in range(8):
            ext[bx + 1, by + 1] = (2 * flip_ref[bx, pl.ds(by, 1), :] - 1).astype(F32)

    row = lax.broadcasted_iota(I32, (128, 128), 0)
    col = lax.broadcasted_iota(I32, (128, 128), 1)
    dist = jnp.abs(row - col)
    band = jnp.where(dist == 0, w_mid, jnp.where(dist == 1, w_side, 0.0)).astype(F32)
    wcat = jnp.concatenate(split2(band), axis=1)
    hz = parity_sign(row & col, (4, 2, 1)).astype(BF16)
    hcat = jnp.concatenate([hz, hz], axis=1)

    def smooth_z(i, _):
        v = vol[pl.ds(i * 32, 32)].astype(F32).reshape(256, 128).astype(BF16)
        r = jnp.dot(v, wcat, preferred_element_type=F32)
        zs[pl.ds(i * 256, 256), :] = r[:, :128] + r[:, 128:]
        return 0

    for i in range(CHUNKS):
        loads[i].wait()
        lax.fori_loop(i * per // 32, (i + 1) * per // 32, smooth_z, 0)

    def remote(src, dst, ssem, rsem, dev):
        return pltpu.make_async_remote_copy(
            src_ref=src, dst_ref=dst, send_sem=ssem, recv_sem=rsem, device_id=dev, device_id_type=MESH
        )

    def go(src, dst, kind, rsem, dev):
        remote(src, dst, sends.at[kind], rsem, dev).start()

    def arrive(whole, rsem):
        remote(whole, whole, sends.at[0], rsem, partner).wait_recv()

    def sent(whole, kind):
        remote(whole, whole, sends.at[kind], recvs.at[0], partner).wait_send()

    pl.semaphore_wait(barrier, len(peers))
    for i, (dx, dy) in enumerate(HALO):
        go(flip_ref, halo.at[i], 0, recvs.at[0], near(dx, dy))

    zero = jnp.zeros((COLS, 128), F32)
    for ex in range(EX):
        for yi in (0, 1, 10, 11):
            xs[ex, yi] = zero
    for yi in range(8):
        a = zs[pl.ds(yi, COLS, stride=16), :]
        b = zs[pl.ds(8 + yi, COLS, stride=16), :]
        xs[0, yi + 2] = w_side * a
        xs[1, yi + 2] = w_mid * a + w_side * b
        xs[2, yi + 2] = w_side * a + w_mid * b
        xs[3, yi + 2] = w_side * b

    def plane(ex, yi):
        f = w_side * (xs[ex, yi] + xs[ex, yi + 2]) + w_mid * xs[ex, yi + 1]
        f = f * ext[ex, yi]
        fcat = jnp.concatenate(split2(f), axis=1)
        t = lax.dot_general(hcat, fcat, (((1,), (1,)), ((), ())), preferred_element_type=F32)
        thi, tlo = split2(t)
        at = pl.ds(pl.multiple_of((ex * EY + yi) * STRATUM, STRATUM), STRATUM)
        for g in range(RZ):
            tt_hi[g, at, :] = thi[g * STRATUM : (g + 1) * STRATUM, :]
            tt_lo[g, at, :] = tlo[g * STRATUM : (g + 1) * STRATUM, :]

    def own_planes(i, _):
        plane(1, i + 1)
        plane(2, i + 1)
        return 0

    lax.fori_loop(0, 8, own_planes, 0)

    for copy in small[1:]:
        copy.wait()
    code_t = (block_ref[...] * 16 + offset_ref[...]).astype(F32).T.astype(I32)
    lane = lax.broadcasted_iota(I32, (1, 128), 1)
    gx = vx * 2 + lane // EY - 1 + 32
    gy = vy * 8 + lane % EY - 1 + 64
    voxel = (((gx >> 1) & 15) * 8 + ((gy >> 3) & 7)) * 16 + (gx & 1) * 8 + (gy & 7)
    off_lane = lane & 15
    ej = lax.broadcasted_iota(I32, (128, PLANES * STRATUM), 0)
    ek = lax.broadcasted_iota(I32, (128, PLANES * STRATUM), 1)
    spread = jnp.where((ek >> 4) == ej, 1.0, 0.0).astype(BF16)
    place = lax.broadcasted_iota(I32, (PLANE * KD, 128), 0) // KD
    for g in range(RZ):
        code = jnp.concatenate(
            [
                jnp.broadcast_to(
                    code_t[(g % 4) * KD : (g % 4 + 1) * KD, 2 * p + g // 4 : 2 * p + g // 4 + 1], (KD, 128)
                )
                for p in range(PLANE)
            ],
            axis=0,
        )
        sgn = parity_sign(((code & -16) + place) & voxel, (8, 4, 2, 1)).astype(BF16)
        wide = jnp.dot(sgn, spread, preferred_element_type=F32)
        pick = (code & 15) == off_lane
        for k in range(BANDS):
            at = slice(k * 128, (k + 1) * 128)
            tables[g, :, at] = jnp.where(pick, wide[:, at], 0.0).astype(BF16)

    lanes = lax.broadcasted_iota(I32, (64, 512), 1)
    rows = lax.broadcasted_iota(I32, (64, 512), 0)
    for s in range(8):
        mover[64 * s : 64 * s + 64, :] = jnp.where(lanes == order_ref[s] * 64 + rows, 1.0, 0.0).astype(BF16)

    okx = {-1: jnp.where(vx > 0, 1, 0), 0: 1, 1: jnp.where(vx < PLANE - 1, 1, 0)}
    oky = {-1: jnp.where(vy > 0, 1, 0), 0: 1, 1: jnp.where(vy < RZ - 1, 1, 0)}
    arrive(halo, recvs.at[0])
    for i, (dx, dy) in enumerate(HALO):
        ok = (okx[-dx] * oky[-dy]).astype(F32)
        xpos = {-1: [(0, 1)], 0: [(1, 0), (2, 1)], 1: [(3, 0)]}[-dx]
        ypos = {-1: [(0, 7)], 0: [(k + 1, k) for k in range(8)], 1: [(9, 0)]}[-dy]
        for ex, bx in xpos:
            for ey, by in ypos:
                ext[ex, ey] = (2 * halo[i, bx, pl.ds(by, 1), :] - 1).astype(F32) * ok

    def x_planes(i, _):
        plane(0, i)
        plane(3, i)
        return 0

    def y_planes(i, _):
        plane(1, i * 9)
        plane(2, i * 9)
        return 0

    lax.fori_loop(0, EY, x_planes, 0)
    lax.fori_loop(0, 2, y_planes, 0)

    def contribute(t):
        g = lax.rem(vy + ORDER[t], RZ)
        r = jnp.dot(tables[g], tt_hi[g], preferred_element_type=F32)
        r = (r + jnp.dot(tables[g], tt_lo[g], preferred_element_type=F32)) * (1.0 / 512.0)
        for p in range(PLANE):
            dy, dx = lax.rem(p // RX - y + RY, RY), lax.rem(p % RX - x + RX, RX)
            c[t, dy, dx] = r[p * KD : (p + 1) * KD]

    lanes_of = [pl.ds(0, HALF), pl.ds(HALF, HALF)]
    X, ZF = pl.ds(ZR, XR), pl.ds(0, ZR)
    WAYS = ((1, 1), (-1, 3))

    def first(h, way):
        return xy(way, 0) if h == 0 else xy(0, way)

    def second(h, way):
        return xy(0, way) if h == 0 else xy(way, 0)

    def block(h, U, near_axis, other_axis):
        return (U, other_axis, near_axis) if h == 0 else (U, near_axis, other_axis)

    def start_a1(u):
        U = pl.ds(2 * u, 2)
        for h in range(2):
            for k in range(2):
                src = c.at[(*block(h, U, 2, pl.ds(2 * k, 2)), X, lanes_of[h])]
                go(src, ra1.at[u, h, k], 1, a_recv.at[0, u], first(h, WAYS[k][0]))

    def do_a2(u):
        U = pl.ds(2 * u, 2)
        arrive(ra1.at[u], a_recv.at[0, u])
        for h in range(2):
            for k in range(2):
                way, near_pos = WAYS[k]
                at = (*block(h, U, near_pos, pl.ds(2 * k, 2)), X, lanes_of[h])
                c[at] = c[at] + ra1[u, h, k]
                src = c.at[(*block(h, U, near_pos, pl.ds(0, 4)), X, lanes_of[h])]
                go(src, ra2.at[u, h, k], 2, a_recv.at[1, u], first(h, way))

    def far(u, k):
        rows = (16, XR - 16)[(k + u) % 2]
        return pl.ds(ZR if k == 0 else ZR + XR - rows, rows), pl.ds(0, rows)

    def do_b1(u):
        U = pl.ds(2 * u, 2)
        arrive(ra2.at[u], a_recv.at[1, u])
        for h in range(2):
            at = (*block(h, U, 0, pl.ds(0, 4)), X, lanes_of[h])
            c[at] = c[at] + ra2[u, h, 0] + ra2[u, h, 1]
            for k in range(2):
                part, room = far(u, k)
                src = c.at[(*block(h, U, 0, 2), part, lanes_of[h])]
                go(src, rb1.at[u, h, k, :, room], 3, a_recv.at[2, u], second(h, WAYS[k][0]))

    def do_b2(u):
        U = pl.ds(2 * u, 2)
        arrive(rb2.at[u, :, 0], a_recv.at[2, u])
        for h in range(2):
            for k in range(2):
                way, near_pos = WAYS[k]
                part, room = far(u, k)
                at = (*block(h, U, 0, near_pos), part, lanes_of[h])
                c[at] = c[at] + rb1[u, h, k, :, room]
                src = c.at[(*block(h, U, 0, near_pos), X, lanes_of[h])]
                go(src, rb2.at[u, h, k], 4, a_recv.at[3, u], second(h, way))

    def do_b3(u):
        U = pl.ds(2 * u, 2)
        arrive(rb2.at[u], a_recv.at[3, u])
        for h in range(2):
            at = (U, 0, 0, X, lanes_of[h])
            c[at] = c[at] + rb2[u, h, 0] + rb2[u, h, 1]
        for t in (2 * u, 2 * u + 1):
            o = ORDER[t]
            if o:
                go(c.at[t, 0, 0, X], rz.at[o - 1], 5, recvs.at[1], z_dev(o))

    def ring(n):
        for b in range(2):
            for k in range(2):
                to = ORDER.index(5 - n if k == 0 else 3 + n)
                if n == 1:
                    own = pl.ds(2 * k + b, 1)
                    src, dst = c.at[to, own, :, ZF], rv.at[0, b, k, pl.ds(0, 1)]
                else:
                    at = b ^ k ^ 1 if n == 2 else b
                    own = pl.ds(2 * at, 2)
                    if n == 2 and b == 1:
                        arrive(rv.at[0, :, k, 0], v_recv.at[0, 0, k])
                        for i in range(2):
                            c[to, 2 * k + i, :, ZF] = c[to, 2 * k + i, :, ZF] + rv[0, i, k, 0]
                    elif n > 2:
                        arrive(rv.at[n - 2, b, k], v_recv.at[n - 2, b, k])
                        c[to, own, :, ZF] = c[to, own, :, ZF] + rv[n - 2, b, k]
                    src, dst = c.at[to, own, :, ZF], rv.at[n - 1, at, k]
                piece = at if n == 2 else b
                dev = z_dev(1 if k == 0 else RZ - 1)
                go(src, dst, 6 if n == 1 else 7, v_recv.at[n - 1, 0 if n == 1 else piece, k], dev)

    def spread_plane():
        t = ORDER.index(0)
        for b in range(2):
            arrive(rv.at[3, b, 0], v_recv.at[3, b, 0])
            arrive(rv.at[3, b, 1], v_recv.at[3, b, 1])
            own = pl.ds(2 * b, 2)
            c[t, own, :, ZF] = c[t, own, :, ZF] + rv[3, b, 0] + rv[3, b, 1]
        for o in range(1, PLANE):
            dy, dx = o // RX, o % RX
            go(c.at[t, dy, dx, ZF], rw.at[o - 1], 8, recvs.at[2], xy(dx, dy))

    stages = ((LAG_A2, do_a2), (LAG_B1, do_b1), (LAG_B2, do_b2), (LAG_B3, do_b3))
    ring_at = {1: 0, 2: 2, 3: 4, 4: 6}
    for step in range(PAIRS + LAG_B3):
        if step < PAIRS:
            contribute(2 * step)
            if step == 0:
                ring(1)
            contribute(2 * step + 1)
            start_a1(step)
        for n in (2, 3, 4):
            if ring_at[n] == step:
                ring(n)
        for lag, stage in stages:
            if 0 <= step - lag < PAIRS:
                stage(step - lag)
        if step == 8:
            spread_plane()

    low = c[RZ - 1, 0, 0, ZF]
    arrive(rw, recvs.at[2])
    for o in range(1, PLANE):
        low = low + rw[o - 1]
    high = c[RZ - 1, 0, 0, X]
    arrive(rz, recvs.at[1])
    for o in ORDER[:-1]:
        high = high + rz[o - 1]
    total = jnp.concatenate([low, high], axis=0)
    sk_ref[...] = total

    mine_hi, mine_lo = split2(total)
    packed[:KD], packed[KD:] = mine_hi, mine_lo
    go(packed, other, 9, recvs.at[3], partner)
    left = jnp.where(sj == 0, 1.0, 0.0)
    own_half = jnp.concatenate([mine_hi, mine_lo], axis=0)
    moved = jnp.dot(own_half, mover[pl.ds(sj * COLS, COLS)], preferred_element_type=F32)
    arrive(other, recvs.at[3])
    moved = moved + jnp.dot(other[...], mover[pl.ds((1 - sj) * COLS, COLS)], preferred_element_type=F32)
    mine = moved[:, :COLS] * left + moved[:, COLS:] * (1.0 - left)
    lhs = jnp.concatenate([mine[:KD], mine[:KD], mine[KD:]], axis=0).astype(BF16)
    rhs = jnp.concatenate([moved[:KD], moved[KD:], moved[:KD]], axis=0).astype(BF16)
    around = [(dy, dx) for dy in range(RY) for dx in range(RX) if dy or dx]
    around.sort(key=lambda d: -min(d[0], RY - d[0]) - min(d[1], RX - d[1]))
    owner = [lax.rem(y + dy, RY) * RX + lax.rem(x + dx, RX) for dy, dx in around]
    far_z = (4, 3, 5, 2, 6, 1, 7)

    for q in range(PARTS):
        part = lax.dot_general(
            lhs[:, q * ROWS : (q + 1) * ROWS], rhs, (((0,), (0,)), ((), ())), preferred_element_type=F32
        )
        for i in range(ROWS // 8):
            for j in range(4):
                gs[q, 4 * i + j] = part[8 * i : 8 * i + 8, 128 * j : 128 * j + 128]
        for i, (dy, dx) in enumerate(around):
            src = gs.at[q, pl.ds(owner[i] * TILES, TILES)]
            go(src, r1.at[q, i], 10, g_recv.at[0, q], xy(dx, dy))
    for q in range(PARTS):
        acc = gs[q, pl.ds(vx * TILES, TILES)]
        arrive(r1.at[q], g_recv.at[0, q])
        for i in range(PLANE - 1):
            acc = acc + r1[q, i]
        r2[q, vy] = acc
        for o in far_z:
            go(r2.at[q, vy], r2.at[q, vy], 11, g_recv.at[1, q], z_dev(o))
    for q in range(PARTS):
        arrive(r2.at[q, pl.ds(0, RZ - 1)], g_recv.at[1, q])
        acc = r2[q, 0]
        for i in range(1, RZ):
            acc = acc + r2[q, i]
        mine_at = pl.ds(vx * TILES, TILES)
        p3[q] = acc * (1.0 / 4096.0)
        for dy, dx in around:
            go(p3.at[q], out.at[q, mine_at], 12, g_recv.at[2, q], xy(dx, dy))
        out[q, mine_at] = p3[q]
    for q in range(PARTS):
        arrive(r1.at[q], g_recv.at[2, q])
        for i in range(ROWS // 8):
            for j in range(4):
                gram_ref[q * ROWS + 8 * i : q * ROWS + 8 * i + 8, 128 * j : 128 * j + 128] = out[q, 4 * i + j]
    whole = (halo, ra1, ra2, rb2.at[:, :, 0], rb2, rz, rv.at[0, :, :, 0], rv.at[pl.ds(1, 3)], rw, other, r1)
    for kind, ref in enumerate((*whole, r2.at[:, pl.ds(0, RZ - 1)], r1)):
        sent(ref, kind)


def sketch_and_gram(order, vol, flip, block, offset):
    V = pltpu.VMEM
    dma = pltpu.SemaphoreType.DMA
    return pl.pallas_call(
        kernel,
        out_shape=(
            jax.ShapeDtypeStruct((KD, COLS), F32),
            jax.ShapeDtypeStruct((COLS, 2 * COLS), F32),
        ),
        in_specs=[pl.BlockSpec(memory_space=pl.ANY)] * 5,
        out_specs=(pl.BlockSpec(memory_space=V), pl.BlockSpec(memory_space=V)),
        scratch_shapes=[
            pltpu.SMEM((8,), I32),
            V((2, 8, 128), I32),
            V((32, 128), I32),
            V((32, 128), I32),
            V((COLS * 2, 8, 128), BF16),
            V((8, 2, 8, 128), I32),
            V((EX, EY, 1, 128), F32),
            V((RZ, PLANE * KD, PLANES * STRATUM), BF16),
            V((512, 512), BF16),
            V((COLS * 16, 128), F32),
            V((EX, EY + 2, COLS, 128), F32),
            V((RZ, PLANES * STRATUM, COLS), BF16),
            V((RZ, PLANES * STRATUM, COLS), BF16),
            V((RZ, RY, RX, KD, COLS), F32),
            V((PAIRS, 2, 2, 2, 2, XR, HALF), F32),
            V((PAIRS, 2, 2, 2, 4, XR, HALF), F32),
            V((PAIRS, 2, 2, 2, 16, HALF), F32),
            V((PAIRS, 2, 2, 2, XR, HALF), F32),
            V((RZ - 1, XR, COLS), F32),
            V((4, 2, 2, 2, RX, ZR, COLS), F32),
            V((PLANE - 1, ZR, COLS), F32),
            V((2 * KD, COLS), BF16),
            V((2 * KD, COLS), BF16),
            V((PARTS, PLANE * TILES, 8, 128), F32),
            V((PARTS, PLANE - 1, TILES, 8, 128), F32),
            V((PARTS, RZ, TILES, 8, 128), F32),
            V((PARTS, TILES, 8, 128), F32),
            V((PARTS, PLANE * TILES, 8, 128), F32),
            dma((CHUNKS + 4,)),
            dma((13,)),
            dma((4, PAIRS)),
            dma((4, 2, 2)),
            dma((3, PARTS)),
            dma((4,)),
        ],
        compiler_params=pltpu.CompilerParams(
            collective_id=0, has_side_effects=True, vmem_limit_bytes=60 * 1024 * 1024
        ),
        name="sketch_and_gram",
    )(order, vol, flip, block, offset)


def write_kernel(sk, gram, sk_out, gram_out, sem):
    copies = [pltpu.make_async_copy(gram, gram_out, sem.at[0]), pltpu.make_async_copy(sk, sk_out, sem.at[1])]
    for copy in copies:
        copy.start()
    for copy in copies:
        copy.wait()


def write_out(sk, gram):
    return pl.pallas_call(
        write_kernel,
        out_shape=(jax.ShapeDtypeStruct(sk.shape, sk.dtype), jax.ShapeDtypeStruct(gram.shape, gram.dtype)),
        in_specs=[pl.BlockSpec(memory_space=pltpu.VMEM)] * 2,
        out_specs=(pl.BlockSpec(memory_space=pl.ANY), pl.BlockSpec(memory_space=pl.ANY)),
        scratch_shapes=[pltpu.SemaphoreType.DMA((2,))],
        name="write_out",
    )(sk, gram)


def on_device(volumes, flip_bits, hadamard_block, stratum_offset, subject_order):
    sk, gram = sketch_and_gram(
        subject_order,
        volumes.reshape(COLS * 2, 8, 128),
        flip_bits,
        hadamard_block.reshape(32, 128),
        stratum_offset.reshape(32, 128),
    )
    return write_out(sk, gram)


def solution(mesh):
    placed = (P("subj", None, "vx", "vy", None), P("vx", "vy", None), P(), P(), P())
    return jax.shard_map(
        on_device,
        mesh=mesh,
        in_specs=placed,
        out_specs=(P(("vx", "vy"), "subj"), P("subj", None)),
        check_vma=False,
    )
```

```python
import jax
import jax.numpy as jnp
from jax import lax
from jax.experimental import pallas as pl
from jax.experimental.pallas import tpu as pltpu
from jax.sharding import PartitionSpec as P

MESH = pl.DeviceIdType.MESH
F32, BF16, I32 = jnp.float32, jnp.bfloat16, jnp.int32

w_side = 0.2741
w_mid = 0.4518

RX, RY, RZ = 4, 4, 8
PLANE = RX * RY
KD = 32
COLS = 256
HALF = 128
EX, EY = 4, 10
PLANES = EX * EY
STRATUM = 16


def split2(v):
    hi = v.astype(BF16)
    return hi, (v - hi.astype(F32)).astype(BF16)

HALO = [(dx, dy) for dx in (-1, 0, 1) for dy in (-1, 0, 1) if (dx, dy) != (0, 0)]
ORDER = (4, 3, 5, 2, 6, 1, 7, 0)
CHUNKS = 4
LAG_A2, LAG_B1, LAG_B2, LAG_B3 = 2, 4, 6, 8
PAIRS = RZ // 2
PARTS = 4
TILES = 8 // PARTS
ROWS = COLS // PARTS
ZR = 8
XR = KD - ZR
BANDS = PLANES * STRATUM // 128


def parity_sign(bits, shifts):
    for s in shifts:
        bits = bits ^ (bits >> s)
    return jnp.where((bits & 1) == 0, 1.0, -1.0)


def kernel(
    order_hbm, vol_hbm, flip_hbm, block_hbm, offset_hbm, sk_ref, gram_ref,
    order_ref, flip_ref, block_ref, offset_ref, vol, halo, ext, tables, mover, zs, xs, tt_hi, tt_lo,
    c, ra1, ra2, rb1, rb2, rd, rz, rv, rw, packed, other, gs, r1, r2, p3, out,
    ld_sem, sends, a_recv, v_recv, g_recv, recvs,
):
    vx, vy, sj = lax.axis_index("vx"), lax.axis_index("vy"), lax.axis_index("subj")
    x, y = lax.rem(vx, RX), lax.div(vx, RX)

    def xy(dx, dy):
        return (lax.rem(y + dy + RY, RY) * RX + lax.rem(x + dx + RX, RX), vy, sj)

    def plane_dev(o):
        return (lax.rem(vx + o, PLANE), vy, sj)

    def z_dev(o):
        return (vx, lax.rem(vy + o, RZ), sj)

    def near(dx, dy):
        return (lax.rem(vx + dx + PLANE, PLANE), lax.rem(vy + dy + RZ, RZ), sj)

    partner = (vx, vy, 1 - sj)

    small = [
        pltpu.make_async_copy(src, dst, ld_sem.at[CHUNKS + i])
        for i, (src, dst) in enumerate(
            ((flip_hbm, flip_ref), (block_hbm, block_ref), (offset_hbm, offset_ref), (order_hbm, order_ref))
        )
    ]
    small[0].start()
    loads = []
    per = COLS * 2 // CHUNKS
    for i in range(CHUNKS):
        part = pl.ds(i * per, per)
        loads.append(pltpu.make_async_copy(vol_hbm.at[part], vol.at[part], ld_sem.at[i]))
        loads[-1].start()
    for copy in small[1:]:
        copy.start()

    barrier = pltpu.get_barrier_semaphore()
    peers = [plane_dev(o) for o in range(1, PLANE)] + [z_dev(o) for o in range(1, RZ)] + [partner]
    peers += [near(dx, dy) for dx, dy in HALO if dx * dy != 0]
    for d in peers:
        pl.semaphore_signal(barrier, inc=1, device_id=d, device_id_type=MESH)

    small[0].wait()
    for bx in range(2):
        for by in range(8):
            ext[bx + 1, by + 1] = (2 * flip_ref[bx, pl.ds(by, 1), :] - 1).astype(F32)

    row = lax.broadcasted_iota(I32, (128, 128), 0)
    col = lax.broadcasted_iota(I32, (128, 128), 1)
    dist = jnp.abs(row - col)
    band = jnp.where(dist == 0, w_mid, jnp.where(dist == 1, w_side, 0.0)).astype(F32)
    wcat = jnp.concatenate(split2(band), axis=1)
    hz = parity_sign(row & col, (4, 2, 1)).astype(BF16)
    hcat = jnp.concatenate([hz, hz], axis=1)

    def smooth_z(i, _):
        v = vol[pl.ds(i * 32, 32)].astype(F32).reshape(256, 128).astype(BF16)
        r = jnp.dot(v, wcat, preferred_element_type=F32)
        zs[pl.ds(i * 256, 256), :] = r[:, :128] + r[:, 128:]
        return 0

    for i in range(CHUNKS):
        loads[i].wait()
        lax.fori_loop(i * per // 32, (i + 1) * per // 32, smooth_z, 0)

    def remote(src, dst, ssem, rsem, dev):
        return pltpu.make_async_remote_copy(
            src_ref=src, dst_ref=dst, send_sem=ssem, recv_sem=rsem, device_id=dev, device_id_type=MESH
        )

    def go(src, dst, kind, rsem, dev):
        remote(src, dst, sends.at[kind], rsem, dev).start()

    def arrive(whole, rsem):
        remote(whole, whole, sends.at[0], rsem, partner).wait_recv()

    def sent(whole, kind):
        remote(whole, whole, sends.at[kind], recvs.at[0], partner).wait_send()

    pl.semaphore_wait(barrier, len(peers))
    for i, (dx, dy) in enumerate(HALO):
        go(flip_ref, halo.at[i], 0, recvs.at[0], near(dx, dy))

    zero = jnp.zeros((COLS, 128), F32)
    for ex in range(EX):
        for yi in (0, 1, 10, 11):
            xs[ex, yi] = zero
    for yi in range(8):
        a = zs[pl.ds(yi, COLS, stride=16), :]
        b = zs[pl.ds(8 + yi, COLS, stride=16), :]
        xs[0, yi + 2] = w_side * a
        xs[1, yi + 2] = w_mid * a + w_side * b
        xs[2, yi + 2] = w_side * a + w_mid * b
        xs[3, yi + 2] = w_side * b

    def plane(ex, yi):
        f = w_side * (xs[ex, yi] + xs[ex, yi + 2]) + w_mid * xs[ex, yi + 1]
        f = f * ext[ex, yi]
        fcat = jnp.concatenate(split2(f), axis=1)
        t = lax.dot_general(hcat, fcat, (((1,), (1,)), ((), ())), preferred_element_type=F32)
        thi, tlo = split2(t)
        at = pl.ds(pl.multiple_of((ex * EY + yi) * STRATUM, STRATUM), STRATUM)
        for g in range(RZ):
            tt_hi[g, at, :] = thi[g * STRATUM : (g + 1) * STRATUM, :]
            tt_lo[g, at, :] = tlo[g * STRATUM : (g + 1) * STRATUM, :]

    def own_planes(i, _):
        plane(1, i + 1)
        plane(2, i + 1)
        return 0

    lax.fori_loop(0, 8, own_planes, 0)

    for copy in small[1:]:
        copy.wait()
    code_t = (block_ref[...] * 16 + offset_ref[...]).astype(F32).T.astype(I32)
    lane = lax.broadcasted_iota(I32, (1, 128), 1)
    gx = vx * 2 + lane // EY - 1 + 32
    gy = vy * 8 + lane % EY - 1 + 64
    voxel = (((gx >> 1) & 15) * 8 + ((gy >> 3) & 7)) * 16 + (gx & 1) * 8 + (gy & 7)
    off_lane = lane & 15
    ej = lax.broadcasted_iota(I32, (128, PLANES * STRATUM), 0)
    ek = lax.broadcasted_iota(I32, (128, PLANES * STRATUM), 1)
    spread = jnp.where((ek >> 4) == ej, 1.0, 0.0).astype(BF16)
    place = lax.broadcasted_iota(I32, (PLANE * KD, 128), 0) // KD
    for g in range(RZ):
        code = jnp.concatenate(
            [
                jnp.broadcast_to(
                    code_t[(g % 4) * KD : (g % 4 + 1) * KD, 2 * p + g // 4 : 2 * p + g // 4 + 1], (KD, 128)
                )
                for p in range(PLANE)
            ],
            axis=0,
        )
        sgn = parity_sign(((code & -16) + place) & voxel, (8, 4, 2, 1)).astype(BF16)
        wide = jnp.dot(sgn, spread, preferred_element_type=F32)
        pick = (code & 15) == off_lane
        for k in range(BANDS):
            at = slice(k * 128, (k + 1) * 128)
            tables[g, :, at] = jnp.where(pick, wide[:, at], 0.0).astype(BF16)

    lanes = lax.broadcasted_iota(I32, (64, 512), 1)
    rows = lax.broadcasted_iota(I32, (64, 512), 0)
    for s in range(8):
        mover[64 * s : 64 * s + 64, :] = jnp.where(lanes == order_ref[s] * 64 + rows, 1.0, 0.0).astype(BF16)

    okx = {-1: jnp.where(vx > 0, 1, 0), 0: 1, 1: jnp.where(vx < PLANE - 1, 1, 0)}
    oky = {-1: jnp.where(vy > 0, 1, 0), 0: 1, 1: jnp.where(vy < RZ - 1, 1, 0)}
    arrive(halo, recvs.at[0])
    for i, (dx, dy) in enumerate(HALO):
        ok = (okx[-dx] * oky[-dy]).astype(F32)
        xpos = {-1: [(0, 1)], 0: [(1, 0), (2, 1)], 1: [(3, 0)]}[-dx]
        ypos = {-1: [(0, 7)], 0: [(k + 1, k) for k in range(8)], 1: [(9, 0)]}[-dy]
        for ex, bx in xpos:
            for ey, by in ypos:
                ext[ex, ey] = (2 * halo[i, bx, pl.ds(by, 1), :] - 1).astype(F32) * ok

    def x_planes(i, _):
        plane(0, i)
        plane(3, i)
        return 0

    def y_planes(i, _):
        plane(1, i * 9)
        plane(2, i * 9)
        return 0

    lax.fori_loop(0, EY, x_planes, 0)
    lax.fori_loop(0, 2, y_planes, 0)

    def contribute(t):
        g = lax.rem(vy + ORDER[t], RZ)
        r = jnp.dot(tables[g], tt_hi[g], preferred_element_type=F32)
        r = (r + jnp.dot(tables[g], tt_lo[g], preferred_element_type=F32)) * (1.0 / 512.0)
        for p in range(PLANE):
            dy, dx = lax.rem(p // RX - y + RY, RY), lax.rem(p % RX - x + RX, RX)
            c[t, dy, dx] = r[p * KD : (p + 1) * KD]

    lanes_of = [pl.ds(0, HALF), pl.ds(HALF, HALF)]
    X, ZF = pl.ds(ZR, XR), pl.ds(0, ZR)
    WAYS = ((1, 1), (-1, 3))

    def first(h, way):
        return xy(way, 0) if h == 0 else xy(0, way)

    def second(h, way):
        return xy(0, way) if h == 0 else xy(way, 0)

    def block(h, U, near_axis, other_axis):
        return (U, other_axis, near_axis) if h == 0 else (U, near_axis, other_axis)

    def start_a1(u):
        U = pl.ds(2 * u, 2)
        for h in range(2):
            for k in range(2):
                src = c.at[(*block(h, U, 2, pl.ds(2 * k, 2)), X, lanes_of[h])]
                go(src, ra1.at[u, h, k], 1, a_recv.at[0, u], first(h, WAYS[k][0]))

    def do_a2(u):
        U = pl.ds(2 * u, 2)
        arrive(ra1.at[u], a_recv.at[0, u])
        for h in range(2):
            for k in range(2):
                way, near_pos = WAYS[k]
                at = (*block(h, U, near_pos, pl.ds(2 * k, 2)), X, lanes_of[h])
                c[at] = c[at] + ra1[u, h, k]
                src = c.at[(*block(h, U, near_pos, pl.ds(0, 4)), X, lanes_of[h])]
                go(src, ra2.at[u, h, k], 2, a_recv.at[1, u], first(h, way))

    def far(u, k):
        rows = (16, XR - 16)[(k + u) % 2]
        return pl.ds(ZR if k == 0 else ZR + XR - rows, rows), pl.ds(0, rows)

    def do_b1(u):
        U = pl.ds(2 * u, 2)
        arrive(ra2.at[u], a_recv.at[1, u])
        for h in range(2):
            at = (*block(h, U, 0, pl.ds(0, 4)), X, lanes_of[h])
            c[at] = c[at] + ra2[u, h, 0] + ra2[u, h, 1]
            if u == PAIRS - 1:
                for pos in (2, 1, 3):
                    src = c.at[(*block(h, U, 0, pos), X, lanes_of[h])]
                    go(src, rd.at[h, pos - 1], 13, a_recv.at[3, u], second(h, pos))
                continue
            for k in range(2):
                part, room = far(u, k)
                src = c.at[(*block(h, U, 0, 2), part, lanes_of[h])]
                go(src, rb1.at[u, h, k, :, room], 3, a_recv.at[2, u], second(h, WAYS[k][0]))

    def do_b2(u):
        if u == PAIRS - 1:
            return
        U = pl.ds(2 * u, 2)
        arrive(rb2.at[u, :, 0], a_recv.at[2, u])
        for h in range(2):
            for k in range(2):
                way, near_pos = WAYS[k]
                part, room = far(u, k)
                at = (*block(h, U, 0, near_pos), part, lanes_of[h])
                c[at] = c[at] + rb1[u, h, k, :, room]
                src = c.at[(*block(h, U, 0, near_pos), X, lanes_of[h])]
                go(src, rb2.at[u, h, k], 4, a_recv.at[3, u], second(h, way))

    def do_b3(u):
        U = pl.ds(2 * u, 2)
        last = u == PAIRS - 1
        arrive(rd if last else rb2.at[u], a_recv.at[3, u])
        for h in range(2):
            at = (U, 0, 0, X, lanes_of[h])
            if last:
                c[at] = c[at] + rd[h, 0] + rd[h, 1] + rd[h, 2]
            else:
                c[at] = c[at] + rb2[u, h, 0] + rb2[u, h, 1]
        for t in (2 * u, 2 * u + 1):
            o = ORDER[t]
            if o:
                go(c.at[t, 0, 0, X], rz.at[o - 1], 5, recvs.at[1], z_dev(o))

    def ring(n):
        for b in range(2):
            for k in range(2):
                to = ORDER.index(5 - n if k == 0 else 3 + n)
                if n == 1:
                    own = pl.ds(2 * k + b, 1)
                    src, dst = c.at[to, own, :, ZF], rv.at[0, b, k, pl.ds(0, 1)]
                else:
                    at = b ^ k ^ 1 if n == 2 else b
                    own = pl.ds(2 * at, 2)
                    if n == 2 and b == 1:
                        arrive(rv.at[0, :, k, 0], v_recv.at[0, 0, k])
                        for i in range(2):
                            c[to, 2 * k + i, :, ZF] = c[to, 2 * k + i, :, ZF] + rv[0, i, k, 0]
                    elif n > 2:
                        arrive(rv.at[n - 2, b, k], v_recv.at[n - 2, b, k])
                        c[to, own, :, ZF] = c[to, own, :, ZF] + rv[n - 2, b, k]
                    src, dst = c.at[to, own, :, ZF], rv.at[n - 1, at, k]
                piece = at if n == 2 else b
                dev = z_dev(1 if k == 0 else RZ - 1)
                go(src, dst, 6 if n == 1 else 7, v_recv.at[n - 1, 0 if n == 1 else piece, k], dev)

    def spread_plane():
        t = ORDER.index(0)
        for b in range(2):
            arrive(rv.at[3, b, 0], v_recv.at[3, b, 0])
            arrive(rv.at[3, b, 1], v_recv.at[3, b, 1])
            own = pl.ds(2 * b, 2)
            c[t, own, :, ZF] = c[t, own, :, ZF] + rv[3, b, 0] + rv[3, b, 1]
        for o in range(1, PLANE):
            dy, dx = o // RX, o % RX
            go(c.at[t, dy, dx, ZF], rw.at[o - 1], 8, recvs.at[2], xy(dx, dy))

    stages = ((LAG_A2, do_a2), (LAG_B1, do_b1), (LAG_B2, do_b2), (LAG_B3, do_b3))
    ring_at = {1: 0, 2: 2, 3: 4, 4: 6}
    for step in range(PAIRS + LAG_B3):
        if step < PAIRS:
            contribute(2 * step)
            if step == 0:
                ring(1)
            contribute(2 * step + 1)
            start_a1(step)
        for n in (2, 3, 4):
            if ring_at[n] == step:
                ring(n)
        for lag, stage in stages:
            if 0 <= step - lag < PAIRS:
                stage(step - lag)
        if step == 8:
            spread_plane()

    low = c[RZ - 1, 0, 0, ZF]
    arrive(rw, recvs.at[2])
    for o in range(1, PLANE):
        low = low + rw[o - 1]
    high = c[RZ - 1, 0, 0, X]
    arrive(rz, recvs.at[1])
    for o in ORDER[:-1]:
        high = high + rz[o - 1]
    total = jnp.concatenate([low, high], axis=0)
    sk_ref[...] = total

    mine_hi, mine_lo = split2(total)
    packed[:KD], packed[KD:] = mine_hi, mine_lo
    go(packed, other, 9, recvs.at[3], partner)
    left = jnp.where(sj == 0, 1.0, 0.0)
    own_half = jnp.concatenate([mine_hi, mine_lo], axis=0)
    moved = jnp.dot(own_half, mover[pl.ds(sj * COLS, COLS)], preferred_element_type=F32)
    arrive(other, recvs.at[3])
    moved = moved + jnp.dot(other[...], mover[pl.ds((1 - sj) * COLS, COLS)], preferred_element_type=F32)
    mine = moved[:, :COLS] * left + moved[:, COLS:] * (1.0 - left)
    lhs = jnp.concatenate([mine[:KD], mine[:KD], mine[KD:]], axis=0).astype(BF16)
    rhs = jnp.concatenate([moved[:KD], moved[KD:], moved[:KD]], axis=0).astype(BF16)
    around = [(dy, dx) for dy in range(RY) for dx in range(RX) if dy or dx]
    around.sort(key=lambda d: -min(d[0], RY - d[0]) - min(d[1], RX - d[1]))
    owner = [lax.rem(y + dy, RY) * RX + lax.rem(x + dx, RX) for dy, dx in around]
    far_z = (4, 3, 5, 2, 6, 1, 7)

    for q in range(PARTS):
        part = lax.dot_general(
            lhs[:, q * ROWS : (q + 1) * ROWS], rhs, (((0,), (0,)), ((), ())), preferred_element_type=F32
        )
        for i in range(ROWS // 8):
            for j in range(4):
                gs[q, 4 * i + j] = part[8 * i : 8 * i + 8, 128 * j : 128 * j + 128]
        for i, (dy, dx) in enumerate(around):
            src = gs.at[q, pl.ds(owner[i] * TILES, TILES)]
            go(src, r1.at[q, i], 10, g_recv.at[0, q], xy(dx, dy))
    for q in range(PARTS):
        acc = gs[q, pl.ds(vx * TILES, TILES)]
        arrive(r1.at[q], g_recv.at[0, q])
        for i in range(PLANE - 1):
            acc = acc + r1[q, i]
        r2[q, vy] = acc
        for o in far_z:
            go(r2.at[q, vy], r2.at[q, vy], 11, g_recv.at[1, q], z_dev(o))
    for q in range(PARTS):
        arrive(r2.at[q, pl.ds(0, RZ - 1)], g_recv.at[1, q])
        acc = r2[q, 0]
        for i in range(1, RZ):
            acc = acc + r2[q, i]
        mine_at = pl.ds(vx * TILES, TILES)
        p3[q] = acc * (1.0 / 4096.0)
        for dy, dx in around:
            go(p3.at[q], out.at[q, mine_at], 12, g_recv.at[2, q], xy(dx, dy))
        out[q, mine_at] = p3[q]
    for q in range(PARTS):
        arrive(r1.at[q], g_recv.at[2, q])
        for i in range(ROWS // 8):
            for j in range(4):
                gram_ref[q * ROWS + 8 * i : q * ROWS + 8 * i + 8, 128 * j : 128 * j + 128] = out[q, 4 * i + j]
    ring_b = pl.ds(0, PAIRS - 1)
    whole = (halo, ra1, ra2, rb2.at[ring_b, :, 0], rb2.at[ring_b], rz, rv.at[0, :, :, 0], rv.at[pl.ds(1, 3)], rw, other, r1)
    for kind, ref in enumerate((*whole, r2.at[:, pl.ds(0, RZ - 1)], r1, rd)):
        sent(ref, kind)


def sketch_and_gram(order, vol, flip, block, offset):
    V = pltpu.VMEM
    dma = pltpu.SemaphoreType.DMA
    return pl.pallas_call(
        kernel,
        out_shape=(
            jax.ShapeDtypeStruct((KD, COLS), F32),
            jax.ShapeDtypeStruct((COLS, 2 * COLS), F32),
        ),
        in_specs=[pl.BlockSpec(memory_space=pl.ANY)] * 5,
        out_specs=(pl.BlockSpec(memory_space=V), pl.BlockSpec(memory_space=V)),
        scratch_shapes=[
            pltpu.SMEM((8,), I32),
            V((2, 8, 128), I32),
            V((32, 128), I32),
            V((32, 128), I32),
            V((COLS * 2, 8, 128), BF16),
            V((8, 2, 8, 128), I32),
            V((EX, EY, 1, 128), F32),
            V((RZ, PLANE * KD, PLANES * STRATUM), BF16),
            V((512, 512), BF16),
            V((COLS * 16, 128), F32),
            V((EX, EY + 2, COLS, 128), F32),
            V((RZ, PLANES * STRATUM, COLS), BF16),
            V((RZ, PLANES * STRATUM, COLS), BF16),
            V((RZ, RY, RX, KD, COLS), F32),
            V((PAIRS, 2, 2, 2, 2, XR, HALF), F32),
            V((PAIRS, 2, 2, 2, 4, XR, HALF), F32),
            V((PAIRS, 2, 2, 2, 16, HALF), F32),
            V((PAIRS, 2, 2, 2, XR, HALF), F32),
            V((2, 3, 2, XR, HALF), F32),
            V((RZ - 1, XR, COLS), F32),
            V((4, 2, 2, 2, RX, ZR, COLS), F32),
            V((PLANE - 1, ZR, COLS), F32),
            V((2 * KD, COLS), BF16),
            V((2 * KD, COLS), BF16),
            V((PARTS, PLANE * TILES, 8, 128), F32),
            V((PARTS, PLANE - 1, TILES, 8, 128), F32),
            V((PARTS, RZ, TILES, 8, 128), F32),
            V((PARTS, TILES, 8, 128), F32),
            V((PARTS, PLANE * TILES, 8, 128), F32),
            dma((CHUNKS + 4,)),
            dma((14,)),
            dma((4, PAIRS)),
            dma((4, 2, 2)),
            dma((3, PARTS)),
            dma((4,)),
        ],
        compiler_params=pltpu.CompilerParams(
            collective_id=0, has_side_effects=True, vmem_limit_bytes=60 * 1024 * 1024
        ),
        name="sketch_and_gram",
    )(order, vol, flip, block, offset)


def write_kernel(sk, gram, sk_out, gram_out, sem):
    copies = [pltpu.make_async_copy(gram, gram_out, sem.at[0]), pltpu.make_async_copy(sk, sk_out, sem.at[1])]
    for copy in copies:
        copy.start()
    for copy in copies:
        copy.wait()


def write_out(sk, gram):
    return pl.pallas_call(
        write_kernel,
        out_shape=(jax.ShapeDtypeStruct(sk.shape, sk.dtype), jax.ShapeDtypeStruct(gram.shape, gram.dtype)),
        in_specs=[pl.BlockSpec(memory_space=pltpu.VMEM)] * 2,
        out_specs=(pl.BlockSpec(memory_space=pl.ANY), pl.BlockSpec(memory_space=pl.ANY)),
        scratch_shapes=[pltpu.SemaphoreType.DMA((2,))],
        name="write_out",
    )(sk, gram)


def on_device(volumes, flip_bits, hadamard_block, stratum_offset, subject_order):
    sk, gram = sketch_and_gram(
        subject_order,
        volumes.reshape(COLS * 2, 8, 128),
        flip_bits,
        hadamard_block.reshape(32, 128),
        stratum_offset.reshape(32, 128),
    )
    return write_out(sk, gram)


def solution(mesh):
    placed = (P("subj", None, "vx", "vy", None), P("vx", "vy", None), P(), P(), P())
    return jax.shard_map(
        on_device,
        mesh=mesh,
        in_specs=placed,
        out_specs=(P(("vx", "vy"), "subj"), P("subj", None)),
        check_vma=False,
    )
```

```python
import jax
import jax.numpy as jnp
from jax import lax
from jax.experimental import pallas as pl
from jax.experimental.pallas import tpu as pltpu
from jax.sharding import PartitionSpec as P

MESH = pl.DeviceIdType.MESH
F32, BF16, I32 = jnp.float32, jnp.bfloat16, jnp.int32

w_side = 0.2741
w_mid = 0.4518

RX, RY, RZ = 4, 4, 8
PLANE = RX * RY
KD = 32
COLS = 256
HALF = 128
EX, EY = 4, 10
PLANES = EX * EY
STRATUM = 16


def split2(v):
    hi = v.astype(BF16)
    return hi, (v - hi.astype(F32)).astype(BF16)

HALO = [(dx, dy) for dx in (-1, 0, 1) for dy in (-1, 0, 1) if (dx, dy) != (0, 0)]
ORDER = (4, 3, 5, 2, 6, 1, 7, 0)
CHUNKS = 4
LAG_A2, LAG_B1, LAG_B2, LAG_B3 = 2, 4, 6, 8
PAIRS = RZ // 2
PARTS = 4
TILES = 8 // PARTS
ROWS = COLS // PARTS
ZR = 8
XR = KD - ZR
BANDS = PLANES * STRATUM // 128


def parity_sign(bits, shifts):
    for s in shifts:
        bits = bits ^ (bits >> s)
    return jnp.where((bits & 1) == 0, 1.0, -1.0)


def kernel(
    order_hbm, vol_hbm, flip_hbm, block_hbm, offset_hbm, sk_ref, gram_ref,
    order_ref, flip_ref, block_ref, offset_ref, vol, halo, ext, tables, mover, zs, xs, tt_hi, tt_lo,
    c, ra1, ra2, rb1, rb2, rd, rz, rv, rw, packed, other, gs, r1, r2, p3, out,
    ld_sem, sends, a_recv, v_recv, g_recv, recvs,
):
    vx, vy, sj = lax.axis_index("vx"), lax.axis_index("vy"), lax.axis_index("subj")
    x, y = lax.rem(vx, RX), lax.div(vx, RX)

    def xy(dx, dy):
        return (lax.rem(y + dy + RY, RY) * RX + lax.rem(x + dx + RX, RX), vy, sj)

    def plane_dev(o):
        return (lax.rem(vx + o, PLANE), vy, sj)

    def z_dev(o):
        return (vx, lax.rem(vy + o, RZ), sj)

    def near(dx, dy):
        return (lax.rem(vx + dx + PLANE, PLANE), lax.rem(vy + dy + RZ, RZ), sj)

    partner = (vx, vy, 1 - sj)

    small = [
        pltpu.make_async_copy(src, dst, ld_sem.at[CHUNKS + i])
        for i, (src, dst) in enumerate(
            ((flip_hbm, flip_ref), (block_hbm, block_ref), (offset_hbm, offset_ref), (order_hbm, order_ref))
        )
    ]
    small[0].start()
    loads = []
    per = COLS * 2 // CHUNKS
    for i in range(CHUNKS):
        part = pl.ds(i * per, per)
        loads.append(pltpu.make_async_copy(vol_hbm.at[part], vol.at[part], ld_sem.at[i]))
        loads[-1].start()
    for copy in small[1:]:
        copy.start()

    barrier = pltpu.get_barrier_semaphore()
    peers = [plane_dev(o) for o in range(1, PLANE)] + [z_dev(o) for o in range(1, RZ)] + [partner]
    peers += [near(dx, dy) for dx, dy in HALO if dx * dy != 0]
    for d in peers:
        pl.semaphore_signal(barrier, inc=1, device_id=d, device_id_type=MESH)

    small[0].wait()
    for bx in range(2):
        for by in range(8):
            ext[bx + 1, by + 1] = (2 * flip_ref[bx, pl.ds(by, 1), :] - 1).astype(F32)

    row = lax.broadcasted_iota(I32, (128, 128), 0)
    col = lax.broadcasted_iota(I32, (128, 128), 1)
    dist = jnp.abs(row - col)
    band = jnp.where(dist == 0, w_mid, jnp.where(dist == 1, w_side, 0.0)).astype(F32)
    wcat = jnp.concatenate(split2(band), axis=1)
    hz = parity_sign(row & col, (4, 2, 1)).astype(BF16)
    hcat = jnp.concatenate([hz, hz], axis=1)

    def smooth_z(i, _):
        v = vol[pl.ds(i * 32, 32)].astype(F32).reshape(256, 128).astype(BF16)
        r = jnp.dot(v, wcat, preferred_element_type=F32)
        zs[pl.ds(i * 256, 256), :] = r[:, :128] + r[:, 128:]
        return 0

    for i in range(CHUNKS):
        loads[i].wait()
        lax.fori_loop(i * per // 32, (i + 1) * per // 32, smooth_z, 0)

    def remote(src, dst, ssem, rsem, dev):
        return pltpu.make_async_remote_copy(
            src_ref=src, dst_ref=dst, send_sem=ssem, recv_sem=rsem, device_id=dev, device_id_type=MESH
        )

    def go(src, dst, kind, rsem, dev):
        remote(src, dst, sends.at[kind], rsem, dev).start()

    def arrive(whole, rsem):
        remote(whole, whole, sends.at[0], rsem, partner).wait_recv()

    def sent(whole, kind):
        remote(whole, whole, sends.at[kind], recvs.at[0], partner).wait_send()

    pl.semaphore_wait(barrier, len(peers))
    for i, (dx, dy) in enumerate(HALO):
        go(flip_ref, halo.at[i], 0, recvs.at[0], near(dx, dy))

    zero = jnp.zeros((COLS, 128), F32)
    for ex in range(EX):
        for yi in (0, 1, 10, 11):
            xs[ex, yi] = zero
    for yi in range(8):
        a = zs[pl.ds(yi, COLS, stride=16), :]
        b = zs[pl.ds(8 + yi, COLS, stride=16), :]
        xs[0, yi + 2] = w_side * a
        xs[1, yi + 2] = w_mid * a + w_side * b
        xs[2, yi + 2] = w_side * a + w_mid * b
        xs[3, yi + 2] = w_side * b

    def plane(ex, yi):
        f = w_side * (xs[ex, yi] + xs[ex, yi + 2]) + w_mid * xs[ex, yi + 1]
        f = f * ext[ex, yi]
        fcat = jnp.concatenate(split2(f), axis=1)
        t = lax.dot_general(hcat, fcat, (((1,), (1,)), ((), ())), preferred_element_type=F32)
        thi, tlo = split2(t)
        at = pl.ds(pl.multiple_of((ex * EY + yi) * STRATUM, STRATUM), STRATUM)
        for g in range(RZ):
            tt_hi[g, at, :] = thi[g * STRATUM : (g + 1) * STRATUM, :]
            tt_lo[g, at, :] = tlo[g * STRATUM : (g + 1) * STRATUM, :]

    def own_planes(i, _):
        plane(1, i + 1)
        plane(2, i + 1)
        return 0

    lax.fori_loop(0, 8, own_planes, 0)

    for copy in small[1:]:
        copy.wait()
    code_t = (block_ref[...] * 16 + offset_ref[...]).astype(F32).T.astype(I32)
    lane = lax.broadcasted_iota(I32, (1, 128), 1)
    gx = vx * 2 + lane // EY - 1 + 32
    gy = vy * 8 + lane % EY - 1 + 64
    voxel = (((gx >> 1) & 15) * 8 + ((gy >> 3) & 7)) * 16 + (gx & 1) * 8 + (gy & 7)
    off_lane = lane & 15
    ej = lax.broadcasted_iota(I32, (128, PLANES * STRATUM), 0)
    ek = lax.broadcasted_iota(I32, (128, PLANES * STRATUM), 1)
    spread = jnp.where((ek >> 4) == ej, 1.0, 0.0).astype(BF16)
    place = lax.broadcasted_iota(I32, (PLANE * KD, 128), 0) // KD
    for g in range(RZ):
        code = jnp.concatenate(
            [
                jnp.broadcast_to(
                    code_t[(g % 4) * KD : (g % 4 + 1) * KD, 2 * p + g // 4 : 2 * p + g // 4 + 1], (KD, 128)
                )
                for p in range(PLANE)
            ],
            axis=0,
        )
        sgn = parity_sign(((code & -16) + place) & voxel, (8, 4, 2, 1)).astype(BF16)
        wide = jnp.dot(sgn, spread, preferred_element_type=F32)
        pick = (code & 15) == off_lane
        for k in range(BANDS):
            at = slice(k * 128, (k + 1) * 128)
            tables[g, :, at] = jnp.where(pick, wide[:, at], 0.0).astype(BF16)

    okx = {-1: jnp.where(vx > 0, 1, 0), 0: 1, 1: jnp.where(vx < PLANE - 1, 1, 0)}
    oky = {-1: jnp.where(vy > 0, 1, 0), 0: 1, 1: jnp.where(vy < RZ - 1, 1, 0)}
    arrive(halo, recvs.at[0])
    for i, (dx, dy) in enumerate(HALO):
        ok = (okx[-dx] * oky[-dy]).astype(F32)
        xpos = {-1: [(0, 1)], 0: [(1, 0), (2, 1)], 1: [(3, 0)]}[-dx]
        ypos = {-1: [(0, 7)], 0: [(k + 1, k) for k in range(8)], 1: [(9, 0)]}[-dy]
        for ex, bx in xpos:
            for ey, by in ypos:
                ext[ex, ey] = (2 * halo[i, bx, pl.ds(by, 1), :] - 1).astype(F32) * ok

    def x_planes(i, _):
        plane(0, i)
        plane(3, i)
        return 0

    def y_planes(i, _):
        plane(1, i * 9)
        plane(2, i * 9)
        return 0

    lax.fori_loop(0, EY, x_planes, 0)
    lax.fori_loop(0, 2, y_planes, 0)

    def contribute(t):
        g = lax.rem(vy + ORDER[t], RZ)
        r = jnp.dot(tables[g], tt_hi[g], preferred_element_type=F32)
        r = (r + jnp.dot(tables[g], tt_lo[g], preferred_element_type=F32)) * (1.0 / 512.0)
        for p in range(PLANE):
            dy, dx = lax.rem(p // RX - y + RY, RY), lax.rem(p % RX - x + RX, RX)
            c[t, dy, dx] = r[p * KD : (p + 1) * KD]

    lanes_of = [pl.ds(0, HALF), pl.ds(HALF, HALF)]
    X, ZF = pl.ds(ZR, XR), pl.ds(0, ZR)
    WAYS = ((1, 1), (-1, 3))

    def first(h, way):
        return xy(way, 0) if h == 0 else xy(0, way)

    def second(h, way):
        return xy(0, way) if h == 0 else xy(way, 0)

    def block(h, U, near_axis, other_axis):
        return (U, other_axis, near_axis) if h == 0 else (U, near_axis, other_axis)

    def start_a1(u):
        U = pl.ds(2 * u, 2)
        for h in range(2):
            for k in range(2):
                src = c.at[(*block(h, U, 2, pl.ds(2 * k, 2)), X, lanes_of[h])]
                go(src, ra1.at[u, h, k], 1, a_recv.at[0, u], first(h, WAYS[k][0]))

    def do_a2(u):
        U = pl.ds(2 * u, 2)
        arrive(ra1.at[u], a_recv.at[0, u])
        for h in range(2):
            for k in range(2):
                way, near_pos = WAYS[k]
                at = (*block(h, U, near_pos, pl.ds(2 * k, 2)), X, lanes_of[h])
                c[at] = c[at] + ra1[u, h, k]
                src = c.at[(*block(h, U, near_pos, pl.ds(0, 4)), X, lanes_of[h])]
                go(src, ra2.at[u, h, k], 2, a_recv.at[1, u], first(h, way))

    def far(u, k):
        rows = (16, XR - 16)[(k + u) % 2]
        return pl.ds(ZR if k == 0 else ZR + XR - rows, rows), pl.ds(0, rows)

    def do_b1(u):
        U = pl.ds(2 * u, 2)
        arrive(ra2.at[u], a_recv.at[1, u])
        for h in range(2):
            at = (*block(h, U, 0, pl.ds(0, 4)), X, lanes_of[h])
            c[at] = c[at] + ra2[u, h, 0] + ra2[u, h, 1]
            if u == PAIRS - 1:
                for pos in (2, 1, 3):
                    src = c.at[(*block(h, U, 0, pos), X, lanes_of[h])]
                    go(src, rd.at[h, pos - 1], 13, a_recv.at[3, u], second(h, pos))
                continue
            for k in range(2):
                part, room = far(u, k)
                src = c.at[(*block(h, U, 0, 2), part, lanes_of[h])]
                go(src, rb1.at[u, h, k, :, room], 3, a_recv.at[2, u], second(h, WAYS[k][0]))

    def do_b2(u):
        if u == PAIRS - 1:
            return
        U = pl.ds(2 * u, 2)
        arrive(rb2.at[u, :, 0], a_recv.at[2, u])
        for h in range(2):
            for k in range(2):
                way, near_pos = WAYS[k]
                part, room = far(u, k)
                at = (*block(h, U, 0, near_pos), part, lanes_of[h])
                c[at] = c[at] + rb1[u, h, k, :, room]
                src = c.at[(*block(h, U, 0, near_pos), X, lanes_of[h])]
                go(src, rb2.at[u, h, k], 4, a_recv.at[3, u], second(h, way))

    def do_b3(u):
        U = pl.ds(2 * u, 2)
        last = u == PAIRS - 1
        arrive(rd if last else rb2.at[u], a_recv.at[3, u])
        for h in range(2):
            at = (U, 0, 0, X, lanes_of[h])
            if last:
                c[at] = c[at] + rd[h, 0] + rd[h, 1] + rd[h, 2]
            else:
                c[at] = c[at] + rb2[u, h, 0] + rb2[u, h, 1]
        for t in (2 * u, 2 * u + 1):
            o = ORDER[t]
            if o:
                go(c.at[t, 0, 0, X], rz.at[o - 1], 5, recvs.at[1], z_dev(o))

    def ring(n):
        for b in range(2):
            for k in range(2):
                to = ORDER.index(5 - n if k == 0 else 3 + n)
                if n == 1:
                    own = pl.ds(2 * k + b, 1)
                    src, dst = c.at[to, own, :, ZF], rv.at[0, b, k, pl.ds(0, 1)]
                else:
                    at = b ^ k ^ 1 if n == 2 else b
                    own = pl.ds(2 * at, 2)
                    if n == 2 and b == 1:
                        arrive(rv.at[0, :, k, 0], v_recv.at[0, 0, k])
                        for i in range(2):
                            c[to, 2 * k + i, :, ZF] = c[to, 2 * k + i, :, ZF] + rv[0, i, k, 0]
                    elif n > 2:
                        arrive(rv.at[n - 2, b, k], v_recv.at[n - 2, b, k])
                        c[to, own, :, ZF] = c[to, own, :, ZF] + rv[n - 2, b, k]
                    src, dst = c.at[to, own, :, ZF], rv.at[n - 1, at, k]
                piece = at if n == 2 else b
                dev = z_dev(1 if k == 0 else RZ - 1)
                go(src, dst, 6 if n == 1 else 7, v_recv.at[n - 1, 0 if n == 1 else piece, k], dev)

    def spread_plane():
        t = ORDER.index(0)
        for b in range(2):
            arrive(rv.at[3, b, 0], v_recv.at[3, b, 0])
            arrive(rv.at[3, b, 1], v_recv.at[3, b, 1])
            own = pl.ds(2 * b, 2)
            c[t, own, :, ZF] = c[t, own, :, ZF] + rv[3, b, 0] + rv[3, b, 1]
        for o in range(1, PLANE):
            dy, dx = o // RX, o % RX
            go(c.at[t, dy, dx, ZF], rw.at[o - 1], 8, recvs.at[2], xy(dx, dy))

    def column_move():
        lanes = lax.broadcasted_iota(I32, (64, 512), 1)
        rows = lax.broadcasted_iota(I32, (64, 512), 0)
        for s in range(8):
            mover[64 * s : 64 * s + 64, :] = jnp.where(lanes == order_ref[s] * 64 + rows, 1.0, 0.0).astype(BF16)

    stages = ((LAG_A2, do_a2), (LAG_B1, do_b1), (LAG_B2, do_b2), (LAG_B3, do_b3))
    ring_at = {1: 0, 2: 2, 3: 4, 4: 6}
    for step in range(PAIRS + LAG_B3):
        if step < PAIRS:
            contribute(2 * step)
            if step == 0:
                ring(1)
            contribute(2 * step + 1)
            start_a1(step)
        elif step == PAIRS:
            column_move()
        for n in (2, 3, 4):
            if ring_at[n] == step:
                ring(n)
        for lag, stage in stages:
            if 0 <= step - lag < PAIRS:
                stage(step - lag)
        if step == 8:
            spread_plane()

    low = c[RZ - 1, 0, 0, ZF]
    arrive(rw, recvs.at[2])
    for o in range(1, PLANE):
        low = low + rw[o - 1]
    high = c[RZ - 1, 0, 0, X]
    arrive(rz, recvs.at[1])
    for o in ORDER[:-1]:
        high = high + rz[o - 1]
    total = jnp.concatenate([low, high], axis=0)
    sk_ref[...] = total

    mine_hi, mine_lo = split2(total)
    packed[:KD], packed[KD:] = mine_hi, mine_lo
    go(packed, other, 9, recvs.at[3], partner)
    left = jnp.where(sj == 0, 1.0, 0.0)
    own_half = jnp.concatenate([mine_hi, mine_lo], axis=0)
    moved = jnp.dot(own_half, mover[pl.ds(sj * COLS, COLS)], preferred_element_type=F32)
    arrive(other, recvs.at[3])
    moved = moved + jnp.dot(other[...], mover[pl.ds((1 - sj) * COLS, COLS)], preferred_element_type=F32)
    mine = moved[:, :COLS] * left + moved[:, COLS:] * (1.0 - left)
    lhs = jnp.concatenate([mine[:KD], mine[:KD], mine[KD:]], axis=0).astype(BF16)
    rhs = jnp.concatenate([moved[:KD], moved[KD:], moved[:KD]], axis=0).astype(BF16)
    around = [(dy, dx) for dy in range(RY) for dx in range(RX) if dy or dx]
    around.sort(key=lambda d: -min(d[0], RY - d[0]) - min(d[1], RX - d[1]))
    owner = [lax.rem(y + dy, RY) * RX + lax.rem(x + dx, RX) for dy, dx in around]
    far_z = (4, 3, 5, 2, 6, 1, 7)

    for q in range(PARTS):
        part = lax.dot_general(
            lhs[:, q * ROWS : (q + 1) * ROWS], rhs, (((0,), (0,)), ((), ())), preferred_element_type=F32
        )
        for i in range(ROWS // 8):
            for j in range(4):
                gs[q, 4 * i + j] = part[8 * i : 8 * i + 8, 128 * j : 128 * j + 128]
        for i, (dy, dx) in enumerate(around):
            src = gs.at[q, pl.ds(owner[i] * TILES, TILES)]
            go(src, r1.at[q, i], 10, g_recv.at[0, q], xy(dx, dy))
    for q in range(PARTS):
        acc = gs[q, pl.ds(vx * TILES, TILES)]
        arrive(r1.at[q], g_recv.at[0, q])
        for i in range(PLANE - 1):
            acc = acc + r1[q, i]
        r2[q, vy] = acc
        for o in far_z:
            go(r2.at[q, vy], r2.at[q, vy], 11, g_recv.at[1, q], z_dev(o))
    for q in range(PARTS):
        arrive(r2.at[q, pl.ds(0, RZ - 1)], g_recv.at[1, q])
        acc = r2[q, 0]
        for i in range(1, RZ):
            acc = acc + r2[q, i]
        mine_at = pl.ds(vx * TILES, TILES)
        p3[q] = acc * (1.0 / 4096.0)
        for dy, dx in around:
            go(p3.at[q], out.at[q, mine_at], 12, g_recv.at[2, q], xy(dx, dy))
        out[q, mine_at] = p3[q]
    for q in range(PARTS):
        arrive(r1.at[q], g_recv.at[2, q])
        for i in range(ROWS // 8):
            for j in range(4):
                gram_ref[q * ROWS + 8 * i : q * ROWS + 8 * i + 8, 128 * j : 128 * j + 128] = out[q, 4 * i + j]
    ring_b = pl.ds(0, PAIRS - 1)
    whole = (halo, ra1, ra2, rb2.at[ring_b, :, 0], rb2.at[ring_b], rz, rv.at[0, :, :, 0], rv.at[pl.ds(1, 3)], rw, other, r1)
    for kind, ref in enumerate((*whole, r2.at[:, pl.ds(0, RZ - 1)], r1, rd)):
        sent(ref, kind)


def sketch_and_gram(order, vol, flip, block, offset):
    V = pltpu.VMEM
    dma = pltpu.SemaphoreType.DMA
    return pl.pallas_call(
        kernel,
        out_shape=(
            jax.ShapeDtypeStruct((KD, COLS), F32),
            jax.ShapeDtypeStruct((COLS, 2 * COLS), F32),
        ),
        in_specs=[pl.BlockSpec(memory_space=pl.ANY)] * 5,
        out_specs=(pl.BlockSpec(memory_space=V), pl.BlockSpec(memory_space=V)),
        scratch_shapes=[
            pltpu.SMEM((8,), I32),
            V((2, 8, 128), I32),
            V((32, 128), I32),
            V((32, 128), I32),
            V((COLS * 2, 8, 128), BF16),
            V((8, 2, 8, 128), I32),
            V((EX, EY, 1, 128), F32),
            V((RZ, PLANE * KD, PLANES * STRATUM), BF16),
            V((512, 512), BF16),
            V((COLS * 16, 128), F32),
            V((EX, EY + 2, COLS, 128), F32),
            V((RZ, PLANES * STRATUM, COLS), BF16),
            V((RZ, PLANES * STRATUM, COLS), BF16),
            V((RZ, RY, RX, KD, COLS), F32),
            V((PAIRS, 2, 2, 2, 2, XR, HALF), F32),
            V((PAIRS, 2, 2, 2, 4, XR, HALF), F32),
            V((PAIRS, 2, 2, 2, 16, HALF), F32),
            V((PAIRS, 2, 2, 2, XR, HALF), F32),
            V((2, 3, 2, XR, HALF), F32),
            V((RZ - 1, XR, COLS), F32),
            V((4, 2, 2, 2, RX, ZR, COLS), F32),
            V((PLANE - 1, ZR, COLS), F32),
            V((2 * KD, COLS), BF16),
            V((2 * KD, COLS), BF16),
            V((PARTS, PLANE * TILES, 8, 128), F32),
            V((PARTS, PLANE - 1, TILES, 8, 128), F32),
            V((PARTS, RZ, TILES, 8, 128), F32),
            V((PARTS, TILES, 8, 128), F32),
            V((PARTS, PLANE * TILES, 8, 128), F32),
            dma((CHUNKS + 4,)),
            dma((14,)),
            dma((4, PAIRS)),
            dma((4, 2, 2)),
            dma((3, PARTS)),
            dma((4,)),
        ],
        compiler_params=pltpu.CompilerParams(
            collective_id=0, has_side_effects=True, vmem_limit_bytes=60 * 1024 * 1024
        ),
        name="sketch_and_gram",
    )(order, vol, flip, block, offset)


def write_kernel(sk, gram, sk_out, gram_out, sem):
    copies = [pltpu.make_async_copy(gram, gram_out, sem.at[0]), pltpu.make_async_copy(sk, sk_out, sem.at[1])]
    for copy in copies:
        copy.start()
    for copy in copies:
        copy.wait()


def write_out(sk, gram):
    return pl.pallas_call(
        write_kernel,
        out_shape=(jax.ShapeDtypeStruct(sk.shape, sk.dtype), jax.ShapeDtypeStruct(gram.shape, gram.dtype)),
        in_specs=[pl.BlockSpec(memory_space=pltpu.VMEM)] * 2,
        out_specs=(pl.BlockSpec(memory_space=pl.ANY), pl.BlockSpec(memory_space=pl.ANY)),
        scratch_shapes=[pltpu.SemaphoreType.DMA((2,))],
        name="write_out",
    )(sk, gram)


def on_device(volumes, flip_bits, hadamard_block, stratum_offset, subject_order):
    sk, gram = sketch_and_gram(
        subject_order,
        volumes.reshape(COLS * 2, 8, 128),
        flip_bits,
        hadamard_block.reshape(32, 128),
        stratum_offset.reshape(32, 128),
    )
    return write_out(sk, gram)


def solution(mesh):
    placed = (P("subj", None, "vx", "vy", None), P("vx", "vy", None), P(), P(), P())
    return jax.shard_map(
        on_device,
        mesh=mesh,
        in_specs=placed,
        out_specs=(P(("vx", "vy"), "subj"), P("subj", None)),
        check_vma=False,
    )
```
